512 devices in a mesh: dp: 8 (over y, core), place: 64 (over x, z).
Axes of the slice: x: 4, y: 4, z: 16, core: 2. Of those that a mesh axis runs over, the one named last changes fastest.
Arguments:
- tokens: bfloat16 [8, 64, 256, 2048], P('dp', 'place'), may hold values from -6 to 6
- hidden_grad: bfloat16 [8, 64, 256, 256], P('dp', 'place'), may hold values from -6 to 6
- routing: int32 [8, 64, 4, 64], P('dp', 'place'), may hold values from 0 to 63, each once within a row
- row_count: int32 [8, 64], replicated, may hold values from 1 to 256, as said below
- old_slots: int32 [64], replicated, may hold values from 0 to 15, as said below
- new_slots: int32 [64], replicated, may hold values from 0 to 15, as said below
- master: float32 [16, 2048, 512], P(None, ('dp', 'place')), may hold values from -0.125 to 0.125
- first_moment: float32 [16, 2048, 512], P(None, ('dp', 'place')), may hold values from -0.018 to 0.018
- second_moment: float32 [16, 2048, 512], P(None, ('dp', 'place')), may hold values from 1e-06 to 0.0001
Outputs:
- new_weights: bfloat16 [64, 2048, 512], P('place')
- new_master: float32 [16, 2048, 512], P(None, ('dp', 'place'))
- new_first: float32 [16, 2048, 512], P(None, ('dp', 'place'))
- new_second: float32 [16, 2048, 512], P(None, ('dp', 'place'))
The draws below stay inside these ranges and needn't reach their ends.
Inputs may be any that keep to these rules, and one draw needn't show every extreme that they name: `old_slots`: every expert 0 .. 15 holds at least one slot. `new_slots`: every expert 0 .. 15 holds at least one slot. The first row_count[d, p] of a device's 256 row slots are live; some device is full in every draw.
All inputs are finite; a program needn't handle non-finite values.
Results may differ from the reference program's by a relative error of at most 0.001.
The reference program's roundings to bfloat16 on the way (of `old_weights` and `local`) count: a program that leaves them out, or rounds other values in their place, can miss the bound.
Values may be sent and summed in bfloat16 or wider, within the bound.
No kernel may reach another device: no remote copies, remote signals or barrier semaphores. Data moves between devices by JAX's collectives and lax.ppermute only.
A program may use at most 64 MiB of HBM per device.

```python
import math
import jax
import jax.numpy as jnp
from jax import lax

D = 2048
HID = 256
MICRO = 4
ROW_MB = 64
ROWS = 256
EXPERTS = 16
N_DP = 8
N_PLACE = 64


def slot_draw(key, count):
    keys = jax.random.split(key, 4)
    first = jax.random.randint(keys[0], (count - EXPERTS,), 0, EXPERTS)
    second = jax.random.randint(keys[1], (count - EXPERTS,), 0, EXPERTS)
    extra = jnp.minimum(first, second)
    labels = jax.random.permutation(keys[2], EXPERTS)
    slots = labels[jnp.concatenate([jnp.arange(EXPERTS, dtype=jnp.int32), extra.astype(jnp.int32)])]
    return jax.random.permutation(keys[3], slots).astype(jnp.int32)


def draw_old_slots(key, part):
    return slot_draw(jax.random.fold_in(key, 11), N_PLACE)


def draw_new_slots(key, part):
    return slot_draw(jax.random.fold_in(key, 23), N_PLACE)


def draw_row_count(key, part):
    keys = jax.random.split(jax.random.fold_in(key, 37), 2)
    counts = jax.random.randint(keys[0], (N_DP * N_PLACE,), 1, ROWS + 1)
    spot = jax.random.randint(keys[1], (), 0, N_DP * N_PLACE)
    filled = jnp.where(jnp.arange(N_DP * N_PLACE) == spot, ROWS, counts)
    return filled.reshape(N_DP, N_PLACE).astype(jnp.int32)


def shard_levels(key, shape, cuts, least, top_value):
    factor_of, own = 1.0, jax.random.fold_in(key, 6)
    for dim, parts in cuts:
        steps = jnp.exp(jax.random.uniform(jax.random.fold_in(own, dim), (parts,), jnp.float32, least / len(cuts), top_value / len(cuts)))
        factor_of = factor_of * jnp.repeat(steps, shape[dim] // parts).reshape([-1 if axis == dim else 1 for axis in range(len(shape))])
    return factor_of


def noise(rng, extent, scale, limit, cuts=(), kind=jnp.bfloat16):
    entries = scale * jax.random.normal(rng, extent, jnp.float32)
    if cuts:
        entries = entries * shard_levels(rng, extent, cuts, -0.22, 0.18)
    return jnp.clip(entries, -limit, limit).astype(kind)


def setup_inputs(seed: int = 0) -> dict:
    seeds = jax.random.split(jax.random.key(seed), 10)
    return {
        "tokens": noise(seeds[0], (N_DP, N_PLACE, ROWS, D), 1.0, 6.0, ((0, 8), (1, 64))),
        "hidden_grad": noise(seeds[1], (N_DP, N_PLACE, ROWS, HID), 1.0, 6.0, ((0, 8), (1, 64))),
        "routing": jax.vmap(lambda own: jax.random.permutation(own, ROW_MB))(jax.random.split(seeds[2], N_DP * N_PLACE * MICRO)).reshape((N_DP, N_PLACE, MICRO, ROW_MB)).astype(jnp.int32),
        "row_count": draw_row_count(jax.random.fold_in(seeds[9], 71), 0),
        "old_slots": draw_old_slots(jax.random.fold_in(seeds[9], 71), 0),
        "new_slots": draw_new_slots(jax.random.fold_in(seeds[9], 71), 0),
        "master": noise(seeds[6], (EXPERTS, D, 2 * HID), D ** -0.5, 0.125, ((1, 512),), jnp.float32),
        "first_moment": noise(seeds[7], (EXPERTS, D, 2 * HID), 0.003, 0.018, ((1, 512),), jnp.float32),
        "second_moment": jnp.clip(jnp.exp(math.log(0.0001) - 4.6051702 * jax.random.uniform(seeds[8], (EXPERTS, D, 2 * HID), jnp.float32) ** shard_levels(seeds[8], (EXPERTS, D, 2 * HID), ((1, 512),), -0.2, 0.2)), 9.999999974752427e-07, 0.0001),
    }


decay_first = 0.9
decay_second = 0.95
learn_rate = 0.001
weight_decay = 0.1
epsilon = 1e-08
step_number = 20.0

def device_grad(rows_in, grads_in, order, count, weights):
    width = weights.shape[1]
    half = width // 2
    total = jnp.zeros((rows_in.shape[1], width), jnp.float32)
    wide = weights.astype(jnp.float32)
    for batch_index in range(MICRO):
        start = batch_index * ROW_MB
        picked = jnp.take(rows_in, start + order[batch_index].astype(jnp.int32), axis=0)
        picked_wide = picked.astype(jnp.float32)
        both = jnp.dot(picked_wide, wide, precision=lax.Precision.HIGHEST)
        gate = both[:, :half]
        upward = both[:, half:]
        sigma = jax.nn.sigmoid(gate)
        active = gate * sigma
        slope = sigma * (1.0 + gate * (1.0 - sigma))
        live = start + jnp.arange(ROW_MB, dtype=jnp.int32) < count
        incoming = jnp.where(live[:, None], grads_in[start:start + ROW_MB].astype(jnp.float32), 0.0)
        local = jnp.concatenate([incoming * upward * slope, incoming * active], axis=1).astype(jnp.bfloat16)
        total = total + jnp.dot(picked_wide.T, local.astype(jnp.float32), precision=lax.Precision.HIGHEST)
    return total

def reference(tokens, hidden_grad, routing, row_count, old_slots, new_slots, master, first_moment, second_moment):
    devices = N_DP * N_PLACE
    old_weights = master.astype(jnp.bfloat16)
    flat_tokens = tokens.reshape(devices, ROWS, D)
    flat_grads = hidden_grad.reshape(devices, ROWS, HID)
    flat_order = routing.reshape(devices, MICRO, ROW_MB)
    flat_count = row_count.reshape(devices)
    flat_slot = jnp.tile(old_slots, N_DP)

    def visit(summed, item):
        rows_in, grads_in, order, count, slot = item
        weights = old_weights[slot]
        grad = device_grad(rows_in, grads_in, order, count, weights)
        return (summed.at[slot].add(grad), None)
    start_sum = jnp.zeros((EXPERTS, D, 2 * HID), jnp.float32)
    summed, _ = lax.scan(visit, start_sum, (flat_tokens, flat_grads, flat_order, flat_count, flat_slot))
    select = (old_slots[:, None] == jnp.arange(EXPERTS, dtype=jnp.int32)[None, :]).astype(jnp.float32)
    per_slot = lax.optimization_barrier(jnp.sum(row_count.astype(jnp.float32), axis=0))
    total = jnp.dot(per_slot, select, precision=lax.Precision.HIGHEST)
    grad = summed / total[:, None, None]
    new_first = decay_first * first_moment + (1.0 - decay_first) * grad
    new_second = decay_second * second_moment + (1.0 - decay_second) * grad * grad
    first_hat = new_first / (1.0 - decay_first ** step_number)
    second_hat = new_second / (1.0 - decay_second ** step_number)
    new_master = master - learn_rate * (first_hat / (jnp.sqrt(second_hat) + epsilon) + weight_decay * master)
    new_weights = new_master.astype(jnp.bfloat16)[new_slots]
    return (new_weights, new_master, new_first, new_second)
```

```python
import jax
import jax.numpy as jnp
from jax import lax
from jax.experimental import pallas as pl
from jax.experimental.pallas import tpu as pltpu
from jax.sharding import Mesh
from jax.sharding import PartitionSpec as P


decay_first = 0.9
decay_second = 0.95
learn_rate = 0.001
weight_decay = 0.1
epsilon = 1e-08
step_number = 20.0

Y, C, X, Z = 4, 2, 4, 16
UP = [(i, (i + 1) % Y) for i in range(Y)]
DOWN = [(i, (i - 1) % Y) for i in range(Y)]
ACROSS = [(i, (i + 2) % Y) for i in range(Y)]
SWAP = [(0, 1), (1, 0)]


def group_grad(core_ref, w_ref, h0_ref, h1_ref, *refs):
    chunks, (out_ref, local_ref) = refs[:-2], refs[-2:]
    half = w_ref.shape[1] // 2
    row = 0
    starts = []
    for k, chunk in enumerate(chunks):
        rows = chunk.shape[0]
        h_ref = h0_ref if k < len(chunks) // 2 else h1_ref
        first = row % h_ref.shape[0]
        both = jnp.dot(chunk[...], w_ref[...], preferred_element_type=jnp.float32)
        other = pltpu.roll(both, half, 1)
        lane = lax.broadcasted_iota(jnp.int32, both.shape, 1)
        gate = jnp.where(lane < half, both, other)
        sigma = jax.nn.sigmoid(gate)
        active = gate * sigma
        slope = sigma * (1.0 + gate * (1.0 - sigma))
        incoming = h_ref[first : first + rows, :].astype(jnp.float32)
        local = jnp.where(lane < half, incoming * other * slope, incoming * active)
        local_ref[:, row : row + rows] = local.T.astype(jnp.bfloat16)
        starts.append(row)
        row += rows
    core = core_ref[0]
    wide = out_ref.shape[0] // Y
    for y in range(Y):
        at = pl.multiple_of((2 * y + core) * wide, wide)
        total = jnp.zeros((2 * half, wide), jnp.float32)
        for start, chunk in zip(starts, chunks):
            total = total + jnp.dot(
                local_ref[:, start : start + chunk.shape[0]],
                chunk[:, pl.ds(at, wide)],
                preferred_element_type=jnp.float32,
            )
        out_ref[y * wide : (y + 1) * wide, :] = total.T


def call_group_grad(core, w, h0, h1, chunks):
    vmem = pl.BlockSpec(memory_space=pltpu.VMEM)
    rows = sum(c.shape[0] for c in chunks)
    deep, cols = w.shape
    return pl.pallas_call(
        group_grad,
        out_shape=jax.ShapeDtypeStruct((deep // C, cols), jnp.float32),
        in_specs=[pl.BlockSpec(memory_space=pltpu.SMEM)] + [vmem] * (3 + len(chunks)),
        out_specs=vmem,
        scratch_shapes=[pltpu.VMEM((cols, rows), jnp.bfloat16)],
        name="group_grad",
    )(core, w, h0, h1, *chunks)


def one_hot(slots, experts, dtype):
    return (slots[:, None] == jnp.arange(experts, dtype=jnp.int32)[None, :]).astype(dtype)


def shards(
    tokens, hidden_grad, routing, row_count, old_slots, new_slots, master, first_moment, second_moment
):
    y, core = lax.axis_index("y"), lax.axis_index("core")
    group_here = y * C + core
    place_here = lax.axis_index("x") * Z + lax.axis_index("z")
    experts, rows_shard, width = master.shape
    hid = width // 2
    part = hid // Y

    own = tokens[0, 0]
    rows = own.shape[0]
    low = lax.ppermute(own, "y", UP)
    high = lax.ppermute(own, "y", DOWN)
    own_c = lax.ppermute(own, "core", SWAP)

    picked = jnp.dot(
        one_hot(old_slots, experts, jnp.bfloat16),
        master.astype(jnp.bfloat16).reshape(experts, rows_shard * width),
        preferred_element_type=jnp.float32,
    ).astype(jnp.bfloat16)
    landed = lax.all_to_all(
        picked.reshape(X * Z, rows_shard, width), ("x", "z"), 0, 0, tiled=True
    ).reshape(X * Z * rows_shard, width)

    order = routing[0, 0]
    batches, batch_rows = order.shape
    count = row_count[group_here, place_here]
    live = jnp.arange(rows, dtype=jnp.int32) < count
    masked = jnp.where(live[:, None], hidden_grad[0, 0], jnp.zeros((), jnp.bfloat16))
    slot_of = (
        order[:, None, :] == jnp.arange(batch_rows, dtype=jnp.int32)[None, :, None]
    ).astype(jnp.bfloat16)
    moved = lax.dot_general(
        slot_of,
        masked.reshape(batches, batch_rows, hid),
        (((2,), (1,)), ((0,), (0,))),
        preferred_element_type=jnp.float32,
    ).astype(jnp.bfloat16).reshape(rows, hid)
    slices = [moved[:, k * part : (k + 1) * part] for k in range(Y)]
    by_chip = jnp.stack([jnp.concatenate([s, s], axis=1) for s in slices])

    def for_chip(step):
        return lax.dynamic_index_in_dim(by_chip, (y + step) % Y, keepdims=False)

    h_low = lax.ppermute(for_chip(1), "y", UP)
    h_high = lax.ppermute(for_chip(3), "y", DOWN)
    h_far = lax.ppermute(for_chip(2), "y", ACROSS)
    h_own = jnp.concatenate([for_chip(0), h_low, h_high, h_far], axis=0)
    h_own_c = lax.ppermute(h_own, "core", SWAP)

    half_rows = rows // 2
    far_a = lax.ppermute(low[:half_rows], "y", UP)
    far_b = lax.ppermute(high[half_rows:], "y", DOWN)
    low_c = lax.ppermute(low, "core", SWAP)
    high_c = lax.ppermute(high, "core", SWAP)
    far_a_c = lax.ppermute(far_a, "core", SWAP)
    far_b_c = lax.ppermute(far_b, "core", SWAP)

    columns = jnp.stack(
        [
            jnp.concatenate(
                [landed[:, k * part : (k + 1) * part], landed[:, hid + k * part : hid + (k + 1) * part]],
                axis=1,
            )
            for k in range(Y)
        ]
    )
    columns = jnp.broadcast_to(columns[:, None], (Y, C, *columns.shape[1:]))
    weights = lax.all_to_all(
        columns.reshape(Y * C, *columns.shape[2:]), ("y", "core"), 0, 0, tiled=True
    )
    weights = weights.reshape(-1, 2 * part)

    summed = call_group_grad(
        core.astype(jnp.int32).reshape(1),
        weights,
        h_own,
        h_own_c,
        [own, low, high, far_a, far_b, own_c, low_c, high_c, far_a_c, far_b_c],
    )

    got = lax.all_to_all(
        summed.reshape(Y * X, Z * rows_shard, 2 * part), ("y", "x"), 0, 0, tiled=True
    )
    got = got.reshape(Y, X, Z, rows_shard, 2 * part).transpose(2, 1, 0, 3, 4)
    got = lax.all_to_all(
        got.reshape(Z, X * Y * rows_shard, 2 * part), "z", 0, 0, tiled=True
    )
    old_zx = old_slots.reshape(X, Z).T.reshape(-1)
    select = one_hot(old_zx, experts, jnp.float32)
    grad_sum = jnp.dot(
        select.T, got.reshape(Z * X, Y * rows_shard * 2 * part), precision=lax.Precision.HIGHEST
    )
    grad_sum = (
        grad_sum.reshape(experts, Y, rows_shard, 2, part)
        .transpose(0, 2, 3, 1, 4)
        .reshape(experts, rows_shard, width)
    )
    per_slot = jnp.sum(row_count.astype(jnp.float32), axis=0)
    total = jnp.dot(
        per_slot, one_hot(old_slots, experts, jnp.float32), precision=lax.Precision.HIGHEST
    )
    grad = grad_sum / total[:, None, None]
    new_first = decay_first * first_moment + (1.0 - decay_first) * grad
    new_second = decay_second * second_moment + (1.0 - decay_second) * grad * grad
    first_hat = new_first / (1.0 - decay_first**step_number)
    second_hat = new_second / (1.0 - decay_second**step_number)
    new_master = master - learn_rate * (
        first_hat / (jnp.sqrt(second_hat) + epsilon) + weight_decay * master
    )

    new_zx = new_slots.reshape(X, Z).T.reshape(-1)
    picked = jnp.dot(
        one_hot(new_zx, experts, jnp.bfloat16),
        new_master.astype(jnp.bfloat16).reshape(experts, rows_shard * width),
        preferred_element_type=jnp.float32,
    ).astype(jnp.bfloat16)
    landed = lax.all_to_all(
        picked.reshape(Z, X * rows_shard, width), "z", 0, 0, tiled=True
    )
    landed = (
        landed.reshape(Z, X, rows_shard, width).transpose(1, 0, 2, 3).reshape(X, Z * rows_shard, width)
    )
    landed = jnp.broadcast_to(landed[None], (Y, *landed.shape))
    mine = lax.all_to_all(
        landed.reshape(Y * X, Z * rows_shard, width), ("y", "x"), 0, 0, tiled=True
    ).reshape(Y, X * Z * rows_shard, width)
    theirs = lax.ppermute(mine, "core", SWAP)
    even = jnp.where(core == 0, mine, theirs)
    odd = jnp.where(core == 0, theirs, mine)
    new_weights = jnp.stack([even, odd], axis=1).reshape(1, -1, width)
    return (new_weights, new_master, new_first, new_second)


def solution(mesh):
    fine = Mesh(mesh.devices.reshape(Y, C, X, Z), ("y", "core", "x", "z"))
    dp, place = ("y", "core"), ("x", "z")
    placed = (
        P(dp, place, None, None),
        P(dp, place, None, None),
        P(dp, place, None, None),
        P(),
        P(),
        P(),
        P(None, dp + place, None),
        P(None, dp + place, None),
        P(None, dp + place, None),
    )

    return jax.shard_map(
        shards,
        mesh=fine,
        in_specs=placed,
        out_specs=(
            P(place, None, None),
            P(None, dp + place, None),
            P(None, dp + place, None),
            P(None, dp + place, None),
        ),
        check_vma=False,
    )
```

```python
import jax
import jax.numpy as jnp
from jax import lax
from jax.experimental import pallas as pl
from jax.experimental.pallas import tpu as pltpu
from jax.sharding import Mesh
from jax.sharding import PartitionSpec as P


decay_first = 0.9
decay_second = 0.95
learn_rate = 0.001
weight_decay = 0.1
epsilon = 1e-08
step_number = 20.0

Y, C, X, Z = 4, 2, 4, 16
PLACES = X * Z
UP = [(i, (i + 1) % Y) for i in range(Y)]
DOWN = [(i, (i - 1) % Y) for i in range(Y)]
ACROSS = [(i, (i + 2) % Y) for i in range(Y)]
SWAP = [(0, 1), (1, 0)]
VMEM = pl.BlockSpec(memory_space=pltpu.VMEM)
SMEM = pl.BlockSpec(memory_space=pltpu.SMEM)
ANY = pl.BlockSpec(memory_space=pl.ANY)


def grant(mib):
    return pltpu.CompilerParams(vmem_limit_bytes=mib << 20)


def lower_half(x):
    return lax.broadcasted_iota(jnp.int32, x.shape, x.ndim - 1) < x.shape[-1] // 2


def swapped(x):
    return pltpu.roll(x, x.shape[-1] // 2, x.ndim - 1)


def split_cols(*refs):
    ins, out = refs[:-1], refs[-1]
    lanes = out.shape[-1]
    half = ins[0].shape[-1] // 2
    for n, x in enumerate(ins):
        for pair in range(Y // 2):
            gate = x[:, :, pair * lanes : (pair + 1) * lanes]
            up = x[:, :, half + pair * lanes : half + (pair + 1) * lanes]
            low = lower_half(gate)
            out[2 * pair, n] = jnp.where(low, gate, swapped(up))
            out[2 * pair + 1, n] = jnp.where(low, swapped(gate), up)


def join_cols(y_ref, own, low, high, far, *refs):
    outs, parts = refs[:-1], refs[-1]
    y = y_ref[0]
    parts[y] = own[...]
    parts[(y + 3) % Y] = low[...]
    parts[(y + 1) % Y] = high[...]
    parts[(y + 2) % Y] = far[...]
    lanes = own.shape[-1]
    half = outs[0].shape[-1] // 2
    for n, out in enumerate(outs):
        for pair in range(Y // 2):
            a, b = parts[2 * pair, n], parts[2 * pair + 1, n]
            first = lower_half(a)
            out[:, :, pair * lanes : (pair + 1) * lanes] = jnp.where(first, a, swapped(b))
            out[:, :, half + pair * lanes : half + (pair + 1) * lanes] = jnp.where(
                first, swapped(a), b
            )


def pick_old(slots, state, out, table):
    for e in range(table.shape[0]):
        table[e] = jnp.concatenate([state[y, 0, e] for y in range(Y)], axis=0).astype(jnp.bfloat16)
    for p in range(PLACES):
        out[p] = table[slots[p]]


def adam(old, new, total, got, state, out, after, acc, table):
    experts = acc.shape[0]
    rows = state.shape[3]
    acc[...] = jnp.zeros_like(acc)
    for p in range(PLACES):
        acc[old[p]] += got[p]
    for e in range(experts):
        master, first, second = (
            jnp.concatenate([state[y, n, e] for y in range(Y)], axis=0) for n in range(3)
        )
        grad = acc[e] / total[e]
        new_first = decay_first * first + (1.0 - decay_first) * grad
        new_second = decay_second * second + (1.0 - decay_second) * grad * grad
        first_hat = new_first / (1.0 - decay_first**step_number)
        second_hat = new_second / (1.0 - decay_second**step_number)
        new_master = master - learn_rate * (
            first_hat / (jnp.sqrt(second_hat) + epsilon) + weight_decay * master
        )
        table[e] = new_master.astype(jnp.bfloat16)
        for n, value in enumerate((new_master, new_first, new_second)):
            for y in range(Y):
                after[y, n, e] = value[y * rows : (y + 1) * rows]
    for p in range(PLACES):
        out[p] = table[new[p]]


def group_grad(core_ref, mine, theirs, h0_ref, h1_ref, *refs):
    chunks, (out_ref, tok, w_ref, local_ref, sems) = refs[:-5], refs[-5:]
    starts, row = [], 0
    copies = []
    for k, chunk in enumerate(chunks):
        rows = chunk.shape[0]
        copy = pltpu.make_async_copy(chunk, tok.at[pl.ds(row, rows)], sems.at[k])
        copy.start()
        copies.append(copy)
        starts.append((row, rows))
        row += rows
    core = core_ref[0]
    wide = mine.shape[1]
    for y in range(Y):
        w_ref[pl.ds(pl.multiple_of((2 * y + core) * wide, wide), wide), :] = mine[y]
        w_ref[pl.ds(pl.multiple_of((2 * y + 1 - core) * wide, wide), wide), :] = theirs[y]
    for k, (row, rows) in enumerate(starts):
        copies[k].wait()
        h_ref = h0_ref if k < len(chunks) // 2 else h1_ref
        at = row % h_ref.shape[0]
        both = jnp.dot(
            tok[row : row + rows, :], w_ref[...], preferred_element_type=jnp.float32
        )
        other = swapped(both)
        first = lower_half(both)
        gate = jnp.where(first, both, other)
        sigma = jax.nn.sigmoid(gate)
        active = gate * sigma
        slope = sigma * (1.0 + gate * (1.0 - sigma))
        incoming = h_ref[at : at + rows, :].astype(jnp.float32)
        local = jnp.where(first, incoming * other * slope, incoming * active)
        local_ref[:, row : row + rows] = local.T.astype(jnp.bfloat16)
    for y in range(Y):
        at = pl.multiple_of((2 * y + core) * wide, wide)
        total = jnp.dot(
            local_ref[...], tok[:, pl.ds(at, wide)], preferred_element_type=jnp.float32
        )
        out_ref[:, 4 * y : 4 * y + 4, :] = total.T.reshape(wide // 4, 4, -1)


def join_weights(core_ref, mine, theirs, out):
    core = core_ref[0]
    lanes = mine.shape[-1]
    half = out.shape[-1] // 2
    for which, source in ((core, mine), (1 - core, theirs)):
        for pair in range(Y // 2):
            a = source[2 * pair, 0].astype(jnp.float32)
            b = source[2 * pair + 1, 0].astype(jnp.float32)
            first = lower_half(a)
            out[0, which, :, pair * lanes : (pair + 1) * lanes] = jnp.where(
                first, a, swapped(b)
            ).astype(jnp.bfloat16)
            out[0, which, :, half + pair * lanes : half + (pair + 1) * lanes] = jnp.where(
                first, swapped(a), b
            ).astype(jnp.bfloat16)


def shards(
    tokens, hidden_grad, routing, row_count, old_slots, new_slots, master, first_moment, second_moment
):
    y, core = lax.axis_index("y"), lax.axis_index("core")
    group_here = y * C + core
    place_here = lax.axis_index("x") * Z + lax.axis_index("z")
    experts, rows_shard, width = master.shape
    hid = width // 2
    part = hid // Y
    lanes = 2 * part
    f32, bf16 = jnp.float32, jnp.bfloat16
    core_id = core.astype(jnp.int32).reshape(1)
    y_id = y.astype(jnp.int32).reshape(1)

    own = tokens[0, 0]
    rows = own.shape[0]
    low = lax.ppermute(own, "y", UP)
    high = lax.ppermute(own, "y", DOWN)
    own_c = lax.ppermute(own, "core", SWAP)

    columns = pl.pallas_call(
        split_cols,
        out_shape=jax.ShapeDtypeStruct((Y, 3, experts, rows_shard, lanes), f32),
        in_specs=[VMEM] * 3,
        out_specs=VMEM,
        compiler_params=grant(4),
        name="split_cols",
    )(master, first_moment, second_moment)
    state = lax.all_to_all(
        columns.reshape(Y, 3 * experts, rows_shard, lanes), "y", 0, 0, tiled=True
    ).reshape(Y, 3, experts, rows_shard, lanes)
    picked = pl.pallas_call(
        pick_old,
        out_shape=jax.ShapeDtypeStruct((PLACES, Y * rows_shard, lanes), bf16),
        in_specs=[SMEM, VMEM],
        out_specs=VMEM,
        scratch_shapes=[pltpu.VMEM((experts, Y * rows_shard, lanes), bf16)],
        compiler_params=grant(4),
        name="pick_old",
    )(old_slots, state)
    landed = lax.all_to_all(picked, ("x", "z"), 0, 0, tiled=True)

    def by_rows(x):
        return (
            x.reshape(PLACES, Y, rows_shard, lanes)
            .transpose(1, 0, 2, 3)
            .reshape(Y, PLACES * rows_shard, lanes)
        )

    w_mine = by_rows(landed)
    w_theirs = lax.ppermute(w_mine, "core", SWAP)

    order = routing[0, 0]
    batches, batch_rows = order.shape
    count = row_count[group_here, place_here]
    live = jnp.arange(rows, dtype=jnp.int32) < count
    masked = jnp.where(live[:, None], hidden_grad[0, 0], jnp.zeros((), bf16))
    slot_of = (
        order[:, None, :] == jnp.arange(batch_rows, dtype=jnp.int32)[None, :, None]
    ).astype(bf16)
    moved = lax.dot_general(
        slot_of,
        masked.reshape(batches, batch_rows, hid),
        (((2,), (1,)), ((0,), (0,))),
        preferred_element_type=f32,
    ).astype(bf16).reshape(rows, hid)
    slices = [moved[:, k * part : (k + 1) * part] for k in range(Y)]
    by_chip = jnp.stack([jnp.concatenate([s, s], axis=1) for s in slices])

    def for_chip(step, x=by_chip):
        return lax.dynamic_index_in_dim(x, (y + step) % Y, keepdims=False)

    h_low = lax.ppermute(for_chip(1), "y", UP)
    h_high = lax.ppermute(for_chip(3), "y", DOWN)
    h_far = lax.ppermute(for_chip(2), "y", ACROSS)
    h_own = jnp.concatenate([for_chip(0), h_low, h_high, h_far], axis=0)
    h_own_c = lax.ppermute(h_own, "core", SWAP)

    half_rows = rows // 2
    far_a = lax.ppermute(low[:half_rows], "y", UP)
    far_b = lax.ppermute(high[half_rows:], "y", DOWN)
    low_c = lax.ppermute(low, "core", SWAP)
    high_c = lax.ppermute(high, "core", SWAP)
    far_a_c = lax.ppermute(far_a, "core", SWAP)
    far_b_c = lax.ppermute(far_b, "core", SWAP)

    chunks = [own, low, high, far_a, far_b, own_c, low_c, high_c, far_a_c, far_b_c]
    group_rows = sum(c.shape[0] for c in chunks)
    deep = own.shape[1]
    summed = pl.pallas_call(
        group_grad,
        out_shape=jax.ShapeDtypeStruct((PLACES, Y * rows_shard, lanes), f32),
        in_specs=[SMEM] + [VMEM] * 4 + [ANY] * len(chunks),
        out_specs=VMEM,
        scratch_shapes=[
            pltpu.VMEM((group_rows, deep), bf16),
            pltpu.VMEM((deep, lanes), bf16),
            pltpu.VMEM((lanes, group_rows), bf16),
            pltpu.SemaphoreType.DMA((len(chunks),)),
        ],
        compiler_params=grant(24),
        name="group_grad",
    )(core_id, w_mine, w_theirs, h_own, h_own_c, *chunks)

    got = lax.all_to_all(summed, ("x", "z"), 0, 0, tiled=True)
    select = (old_slots[:, None] == jnp.arange(experts, dtype=jnp.int32)[None, :]).astype(f32)
    per_slot = jnp.sum(row_count.astype(f32), axis=0)
    total = jnp.dot(per_slot, select, precision=lax.Precision.HIGHEST)
    picked, after = pl.pallas_call(
        adam,
        out_shape=(
            jax.ShapeDtypeStruct((PLACES, Y * rows_shard, lanes), bf16),
            jax.ShapeDtypeStruct((Y, 3, experts, rows_shard, lanes), f32),
        ),
        in_specs=[SMEM] * 3 + [VMEM] * 2,
        out_specs=(VMEM, VMEM),
        scratch_shapes=[
            pltpu.VMEM((experts, Y * rows_shard, lanes), f32),
            pltpu.VMEM((experts, Y * rows_shard, lanes), bf16),
        ],
        compiler_params=grant(6),
        name="adam",
    )(old_slots, new_slots, total, got, state)
    landed = lax.all_to_all(picked, ("x", "z"), 0, 0, tiled=True)

    s_low = lax.ppermute(for_chip(1, after), "y", UP)
    s_high = lax.ppermute(for_chip(3, after), "y", DOWN)
    s_far = lax.ppermute(for_chip(2, after), "y", ACROSS)
    whole = jax.ShapeDtypeStruct((experts, rows_shard, width), f32)
    new_master, new_first, new_second = pl.pallas_call(
        join_cols,
        out_shape=(whole,) * 3,
        in_specs=[SMEM] + [VMEM] * 4,
        out_specs=(VMEM,) * 3,
        scratch_shapes=[pltpu.VMEM((Y, 3, experts, rows_shard, lanes), f32)],
        compiler_params=grant(6),
        name="join_cols",
    )(y_id, for_chip(0, after), s_low, s_high, s_far)

    landed = by_rows(landed)
    copies = jnp.broadcast_to(landed[None], (Y, *landed.shape))
    mine = lax.all_to_all(copies, "y", 0, 0, tiled=True)
    theirs = lax.ppermute(mine, "core", SWAP)
    block = pl.BlockSpec((Y, 1, PLACES * rows_shard, lanes), lambda i: (0, i, 0, 0))
    new_weights = pl.pallas_call(
        join_weights,
        grid=(Y,),
        out_shape=jax.ShapeDtypeStruct((Y, C, PLACES * rows_shard, width), bf16),
        in_specs=[SMEM, block, block],
        out_specs=pl.BlockSpec((1, C, PLACES * rows_shard, width), lambda i: (i, 0, 0, 0)),
        compiler_params=grant(8),
        name="join_weights",
    )(core_id, mine, theirs)
    return (new_weights.reshape(1, -1, width), new_master, new_first, new_second)


def solution(mesh):
    fine = Mesh(mesh.devices.reshape(Y, C, X, Z), ("y", "core", "x", "z"))
    dp, place = ("y", "core"), ("x", "z")
    placed = (
        P(dp, place, None, None),
        P(dp, place, None, None),
        P(dp, place, None, None),
        P(),
        P(),
        P(),
        P(None, dp + place, None),
        P(None, dp + place, None),
        P(None, dp + place, None),
    )

    return jax.shard_map(
        shards,
        mesh=fine,
        in_specs=placed,
        out_specs=(
            P(place, None, None),
            P(None, dp + place, None),
            P(None, dp + place, None),
            P(None, dp + place, None),
        ),
        check_vma=False,
    )
```

```python
import jax
import jax.numpy as jnp
from jax import lax
from jax.experimental import pallas as pl
from jax.experimental.pallas import tpu as pltpu
from jax.sharding import Mesh
from jax.sharding import PartitionSpec as P


decay_first = 0.9
decay_second = 0.95
learn_rate = 0.001
weight_decay = 0.1
epsilon = 1e-08
step_number = 20.0

Y, C, X, Z = 4, 2, 4, 16
PLACES = X * Z
UP = [(i, (i + 1) % Y) for i in range(Y)]
DOWN = [(i, (i - 1) % Y) for i in range(Y)]
ACROSS = [(i, (i + 2) % Y) for i in range(Y)]
SWAP = [(0, 1), (1, 0)]
VMEM = pl.BlockSpec(memory_space=pltpu.VMEM)
SMEM = pl.BlockSpec(memory_space=pltpu.SMEM)
ANY = pl.BlockSpec(memory_space=pl.ANY)


def grant(mib):
    return pltpu.CompilerParams(vmem_limit_bytes=mib << 20)


def lower_half(x):
    return lax.broadcasted_iota(jnp.int32, x.shape, x.ndim - 1) < x.shape[-1] // 2


def swapped(x):
    return pltpu.roll(x, x.shape[-1] // 2, x.ndim - 1)


def split_cols(*refs):
    ins, out = refs[:-1], refs[-1]
    lanes = out.shape[-1]
    half = ins[0].shape[-1] // 2
    for n, x in enumerate(ins):
        for pair in range(Y // 2):
            gate = x[:, :, pair * lanes : (pair + 1) * lanes]
            up = x[:, :, half + pair * lanes : half + (pair + 1) * lanes]
            low = lower_half(gate)
            out[2 * pair, n] = jnp.where(low, gate, swapped(up))
            out[2 * pair + 1, n] = jnp.where(low, swapped(gate), up)


def join_cols(y_ref, own, low, high, far, *refs):
    outs, parts = refs[:-1], refs[-1]
    y = y_ref[0]
    parts[y] = own[...]
    parts[(y + 3) % Y] = low[...]
    parts[(y + 1) % Y] = high[...]
    parts[(y + 2) % Y] = far[...]
    lanes = own.shape[-1]
    half = outs[0].shape[-1] // 2
    for n, out in enumerate(outs):
        for pair in range(Y // 2):
            a, b = parts[2 * pair, n], parts[2 * pair + 1, n]
            first = lower_half(a)
            out[:, :, pair * lanes : (pair + 1) * lanes] = jnp.where(first, a, swapped(b))
            out[:, :, half + pair * lanes : half + (pair + 1) * lanes] = jnp.where(
                first, swapped(a), b
            )


def prepare(where, counts, order, hidden, master, out):
    batches, batch_rows = order.shape
    experts, rows_shard, width = master.shape
    lanes = out.shape[-1]
    half = width // 2
    count = counts[where[0], where[1]]
    blocks = []
    for m in range(batches):
        at = m * batch_rows
        slot = lax.broadcasted_iota(jnp.int32, (batch_rows, hidden.shape[1]), 0) + at
        live = jnp.where(slot < count, hidden[at : at + batch_rows, :].astype(jnp.float32), 0.0)
        row = lax.broadcasted_iota(jnp.int32, (batch_rows, batch_rows), 0)
        moves = (jnp.broadcast_to(order[m : m + 1, :], row.shape) == row).astype(jnp.bfloat16)
        blocks.append(
            jnp.dot(moves, live.astype(jnp.bfloat16), preferred_element_type=jnp.float32)
        )
    upper = jnp.concatenate(blocks[: batches // 2], axis=0)
    lower = jnp.concatenate(blocks[batches // 2 :], axis=0)
    weights = experts * rows_shard
    for pair in range(Y // 2):
        cut = slice(pair * lanes, (pair + 1) * lanes)
        first = lower_half(upper[:, cut])
        out[2 * pair, weights:, :] = jnp.where(
            first, upper[:, cut], swapped(lower[:, cut])
        ).astype(jnp.bfloat16)
        out[2 * pair + 1, weights:, :] = jnp.where(
            first, swapped(upper[:, cut]), lower[:, cut]
        ).astype(jnp.bfloat16)
        gate = jnp.concatenate([master[e, :, cut] for e in range(experts)], axis=0)
        up_cut = slice(half + pair * lanes, half + (pair + 1) * lanes)
        up = jnp.concatenate([master[e, :, up_cut] for e in range(experts)], axis=0)
        first = lower_half(gate)
        out[2 * pair, :weights, :] = jnp.where(first, gate, swapped(up)).astype(jnp.bfloat16)
        out[2 * pair + 1, :weights, :] = jnp.where(first, swapped(gate), up).astype(jnp.bfloat16)


def pick_old(slots, payload, out, table):
    experts, rows, _ = table.shape
    rows_shard = rows // Y
    parts = [payload[y, : experts * rows_shard, :].astype(jnp.float32) for y in range(Y)]
    for e in range(experts):
        table[e] = jnp.concatenate(
            [part[e * rows_shard : (e + 1) * rows_shard] for part in parts], axis=0
        ).astype(jnp.bfloat16)
    for p in range(PLACES):
        out[p] = table[slots[p]]


def adam(old, new, total, y_ref, got, own, low, high, far, out, after, state, acc, table):
    experts = acc.shape[0]
    rows = state.shape[3]
    y_here = y_ref[0]
    state[y_here] = own[...]
    state[(y_here + 3) % Y] = low[...]
    state[(y_here + 1) % Y] = high[...]
    state[(y_here + 2) % Y] = far[...]
    acc[...] = jnp.zeros_like(acc)
    for p in range(PLACES):
        acc[old[p]] += got[p]
    for e in range(experts):
        master, first, second = (
            jnp.concatenate([state[y, n, e] for y in range(Y)], axis=0) for n in range(3)
        )
        grad = acc[e] / total[e]
        new_first = decay_first * first + (1.0 - decay_first) * grad
        new_second = decay_second * second + (1.0 - decay_second) * grad * grad
        first_hat = new_first / (1.0 - decay_first**step_number)
        second_hat = new_second / (1.0 - decay_second**step_number)
        new_master = master - learn_rate * (
            first_hat / (jnp.sqrt(second_hat) + epsilon) + weight_decay * master
        )
        table[e] = new_master.astype(jnp.bfloat16)
        for n, value in enumerate((new_master, new_first, new_second)):
            for y in range(Y):
                after[y, n, e] = value[y * rows : (y + 1) * rows]
    for p in range(PLACES):
        out[p] = table[new[p]]


def half_grad(out_ref, local_ref, chunks, half, wide):
    for y in range(Y):
        at = pl.multiple_of((2 * y + half) * wide, wide)
        total, row = None, 0
        for chunk in chunks:
            rows = chunk.shape[0]
            term = jnp.dot(
                local_ref[:, row : row + rows],
                chunk[:, pl.ds(at, wide)],
                preferred_element_type=jnp.float32,
            )
            total = term if total is None else total + term
            row += rows
        out_ref[:, 4 * y : 4 * y + 4, :] = total.T.reshape(wide // 4, 4, -1)


def grad_theirs(where, mine, theirs, payload, *refs):
    chunks, (out_ref, local_ref, w_ref) = refs[:-3], refs[-3:]
    y_here, core = where[0], where[1]
    wide = mine.shape[1]
    for y in range(Y):
        w_ref[pl.ds(pl.multiple_of((2 * y + core) * wide, wide), wide), :] = mine[y]
        w_ref[pl.ds(pl.multiple_of((2 * y + 1 - core) * wide, wide), wide), :] = theirs[y]
    sources = [y_here, (y_here + 3) % Y, (y_here + 1) % Y, (y_here + 2) % Y, (y_here + 2) % Y]
    packed = chunks[-1].shape[0]
    weights = payload.shape[1] - packed
    row = 0
    for k, chunk in enumerate(chunks):
        rows = chunk.shape[0]
        both = jnp.dot(chunk[...], w_ref[...], preferred_element_type=jnp.float32)
        other = swapped(both)
        first = lower_half(both)
        gate = jnp.where(first, both, other)
        sigma = jax.nn.sigmoid(gate)
        active = gate * sigma
        slope = sigma * (1.0 + gate * (1.0 - sigma))
        hidden = payload[sources[k], weights:, :].astype(jnp.float32)
        around = swapped(hidden)
        begin = lower_half(hidden)
        halves = [jnp.where(begin, hidden, around), jnp.where(begin, around, hidden)]
        if rows > packed:
            incoming = jnp.concatenate(halves, axis=0)
        else:
            incoming = halves[k - 3]
        local = jnp.where(first, incoming * other * slope, incoming * active)
        local_ref[:, row : row + rows] = local.T.astype(jnp.bfloat16)
        row += rows
    half_grad(out_ref, local_ref, chunks, 1 - core, wide)


def grad_mine(where, local_ref, *refs):
    chunks, out_ref = refs[:-1], refs[-1]
    half_grad(out_ref, local_ref, chunks, where[1], out_ref.shape[0] * 4)


def joined(out, source):
    lanes = source.shape[-1]
    half = out.shape[-1] // 2
    for pair in range(Y // 2):
        a = source[2 * pair, 0].astype(jnp.float32)
        b = source[2 * pair + 1, 0].astype(jnp.float32)
        first = lower_half(a)
        out[0, 0, :, pair * lanes : (pair + 1) * lanes] = jnp.where(
            first, a, swapped(b)
        ).astype(jnp.bfloat16)
        out[0, 0, :, half + pair * lanes : half + (pair + 1) * lanes] = jnp.where(
            first, swapped(a), b
        ).astype(jnp.bfloat16)


def join_mine(where, source, out):
    joined(out, source)


def join_theirs(where, source, begun, out):
    joined(out, source)


def shards(
    tokens, hidden_grad, routing, row_count, old_slots, new_slots, master, first_moment, second_moment
):
    y, core = lax.axis_index("y"), lax.axis_index("core")
    group_here = y * C + core
    place_here = lax.axis_index("x") * Z + lax.axis_index("z")
    experts, rows_shard, width = master.shape
    hid = width // 2
    part = hid // Y
    lanes = 2 * part
    f32, bf16 = jnp.float32, jnp.bfloat16
    where = jnp.stack([y, core]).astype(jnp.int32)
    y_id = y.astype(jnp.int32).reshape(1)
    spot = jnp.stack([group_here, place_here]).astype(jnp.int32)

    own = tokens[0, 0]
    rows = own.shape[0]
    half_rows = rows // 2
    low = lax.ppermute(own, "y", UP)
    high = lax.ppermute(own, "y", DOWN)

    payload = pl.pallas_call(
        prepare,
        out_shape=jax.ShapeDtypeStruct((Y, experts * rows_shard + half_rows, lanes), bf16),
        in_specs=[SMEM, SMEM, VMEM, VMEM, VMEM],
        out_specs=VMEM,
        name="prepare",
    )(spot, row_count, routing[0, 0], hidden_grad[0, 0], master)
    payload = lax.all_to_all(payload, "y", 0, 0, tiled=True)
    picked = pl.pallas_call(
        pick_old,
        out_shape=jax.ShapeDtypeStruct((PLACES, Y * rows_shard, lanes), bf16),
        in_specs=[SMEM, VMEM],
        out_specs=VMEM,
        scratch_shapes=[pltpu.VMEM((experts, Y * rows_shard, lanes), bf16)],
        compiler_params=grant(4),
        name="pick_old",
    )(old_slots, payload)
    landed = lax.all_to_all(picked, ("x", "z"), 0, 0, tiled=True)
    far_a = lax.ppermute(low[:half_rows], "y", UP)
    far_b = lax.ppermute(high[half_rows:], "y", DOWN)

    def by_rows(x):
        return (
            x.reshape(PLACES, Y, rows_shard, lanes)
            .transpose(1, 0, 2, 3)
            .reshape(Y, PLACES * rows_shard, lanes)
        )

    w_mine = by_rows(landed)
    w_theirs = lax.ppermute(w_mine, "core", SWAP)

    chunks = [own, low, high, far_a, far_b]
    line_rows = sum(c.shape[0] for c in chunks)
    deep = own.shape[1]
    grad_shape = jax.ShapeDtypeStruct((PLACES, Y * rows_shard, lanes), f32)
    sent, local = pl.pallas_call(
        grad_theirs,
        out_shape=(grad_shape, jax.ShapeDtypeStruct((lanes, line_rows), bf16)),
        in_specs=[SMEM] + [VMEM] * (3 + len(chunks)),
        out_specs=(VMEM, VMEM),
        scratch_shapes=[pltpu.VMEM((deep, lanes), bf16)],
        compiler_params=grant(24),
        name="grad_theirs",
    )(where, w_mine, w_theirs, payload, *chunks)
    received = lax.ppermute(sent, "core", SWAP)
    summed = pl.pallas_call(
        grad_mine,
        out_shape=grad_shape,
        in_specs=[SMEM] + [VMEM] * (1 + len(chunks)),
        out_specs=VMEM,
        compiler_params=grant(24),
        name="grad_mine",
    )(where, local, *chunks)
    summed = summed + received

    columns = pl.pallas_call(
        split_cols,
        out_shape=jax.ShapeDtypeStruct((Y, 3, experts, rows_shard, lanes), f32),
        in_specs=[VMEM] * 3,
        out_specs=VMEM,
        compiler_params=grant(4),
        name="split_cols",
    )(master, first_moment, second_moment)

    def for_chip(step, x):
        return lax.dynamic_index_in_dim(x, (y + step) % Y, keepdims=False)

    m_low = lax.ppermute(for_chip(1, columns), "y", UP)
    m_high = lax.ppermute(for_chip(3, columns), "y", DOWN)
    m_far = lax.ppermute(for_chip(2, columns), "y", ACROSS)
    m_own = for_chip(0, columns)

    got = lax.all_to_all(summed, ("x", "z"), 0, 0, tiled=True)
    select = (old_slots[:, None] == jnp.arange(experts, dtype=jnp.int32)[None, :]).astype(f32)
    per_slot = jnp.sum(row_count.astype(f32), axis=0)
    total = jnp.dot(per_slot, select, precision=lax.Precision.HIGHEST)
    picked, after = pl.pallas_call(
        adam,
        out_shape=(
            jax.ShapeDtypeStruct((PLACES, Y * rows_shard, lanes), bf16),
            jax.ShapeDtypeStruct((Y, 3, experts, rows_shard, lanes), f32),
        ),
        in_specs=[SMEM] * 4 + [VMEM] * 5,
        out_specs=(VMEM, VMEM),
        scratch_shapes=[
            pltpu.VMEM((Y, 3, experts, rows_shard, lanes), f32),
            pltpu.VMEM((experts, Y * rows_shard, lanes), f32),
            pltpu.VMEM((experts, Y * rows_shard, lanes), bf16),
        ],
        compiler_params=grant(6),
        name="adam",
    )(old_slots, new_slots, total, y_id, got, m_own, m_low, m_high, m_far)
    landed = lax.all_to_all(picked, ("x", "z"), 0, 0, tiled=True)

    s_low = lax.ppermute(for_chip(1, after), "y", UP)
    s_high = lax.ppermute(for_chip(3, after), "y", DOWN)
    s_far = lax.ppermute(for_chip(2, after), "y", ACROSS)
    whole = jax.ShapeDtypeStruct((experts, rows_shard, width), f32)
    new_master, new_first, new_second = pl.pallas_call(
        join_cols,
        out_shape=(whole,) * 3,
        in_specs=[SMEM] + [VMEM] * 4,
        out_specs=(VMEM,) * 3,
        scratch_shapes=[pltpu.VMEM((Y, 3, experts, rows_shard, lanes), f32)],
        compiler_params=grant(6),
        name="join_cols",
    )(y_id, for_chip(0, after), s_low, s_high, s_far)

    landed = by_rows(landed)
    copies = jnp.broadcast_to(landed[None], (Y, *landed.shape))
    mine = lax.all_to_all(copies, "y", 0, 0, tiled=True)
    theirs = lax.ppermute(mine, "core", SWAP)
    block_rows = PLACES * rows_shard
    whole = jax.ShapeDtypeStruct((Y, C, block_rows, width), bf16)
    block = pl.BlockSpec((Y, 1, block_rows, lanes), lambda i, at: (0, i, 0, 0))
    begun = pl.pallas_call(
        join_mine,
        out_shape=whole,
        grid_spec=pltpu.PrefetchScalarGridSpec(
            num_scalar_prefetch=1,
            grid=(Y,),
            in_specs=[block],
            out_specs=pl.BlockSpec((1, 1, block_rows, width), lambda i, at: (i, at[1], 0, 0)),
        ),
        compiler_params=grant(8),
        name="join_mine",
    )(where, mine)
    new_weights = pl.pallas_call(
        join_theirs,
        out_shape=whole,
        grid_spec=pltpu.PrefetchScalarGridSpec(
            num_scalar_prefetch=1,
            grid=(Y,),
            in_specs=[block, ANY],
            out_specs=pl.BlockSpec((1, 1, block_rows, width), lambda i, at: (i, 1 - at[1], 0, 0)),
        ),
        input_output_aliases={2: 0},
        compiler_params=grant(8),
        name="join_theirs",
    )(where, theirs, begun)
    return (new_weights.reshape(1, -1, width), new_master, new_first, new_second)


def solution(mesh):
    fine = Mesh(mesh.devices.reshape(Y, C, X, Z), ("y", "core", "x", "z"))
    dp, place = ("y", "core"), ("x", "z")
    placed = (
        P(dp, place, None, None),
        P(dp, place, None, None),
        P(dp, place, None, None),
        P(),
        P(),
        P(),
        P(None, dp + place, None),
        P(None, dp + place, None),
        P(None, dp + place, None),
    )

    return jax.shard_map(
        shards,
        mesh=fine,
        in_specs=placed,
        out_specs=(
            P(place, None, None),
            P(None, dp + place, None),
            P(None, dp + place, None),
            P(None, dp + place, None),
        ),
        check_vma=False,
    )
```

```python
import jax
import jax.numpy as jnp
from jax import lax
from jax.experimental import pallas as pl
from jax.experimental.pallas import tpu as pltpu
from jax.sharding import Mesh
from jax.sharding import PartitionSpec as P


decay_first = 0.9
decay_second = 0.95
learn_rate = 0.001
weight_decay = 0.1
epsilon = 1e-08
step_number = 20.0

Y, C, X, Z = 4, 2, 4, 16
PLACES = X * Z
UP = [(i, (i + 1) % Y) for i in range(Y)]
DOWN = [(i, (i - 1) % Y) for i in range(Y)]
ACROSS = [(i, (i + 2) % Y) for i in range(Y)]
SWAP = [(0, 1), (1, 0)]
LINE = ((0, None), (3, 0), (3, 1), (1, 0), (1, 1), (2, 0), (2, 1))
VMEM = pl.BlockSpec(memory_space=pltpu.VMEM)
SMEM = pl.BlockSpec(memory_space=pltpu.SMEM)
ANY = pl.BlockSpec(memory_space=pl.ANY)


def grant(mib):
    return pltpu.CompilerParams(vmem_limit_bytes=mib << 20)


def lower_half(x):
    return lax.broadcasted_iota(jnp.int32, x.shape, x.ndim - 1) < x.shape[-1] // 2


def swapped(x):
    return pltpu.roll(x, x.shape[-1] // 2, x.ndim - 1)


def split_cols(*refs):
    ins, out = refs[:-1], refs[-1]
    lanes = out.shape[-1]
    half = ins[0].shape[-1] // 2
    for n, x in enumerate(ins):
        for pair in range(Y // 2):
            gate = x[:, :, pair * lanes : (pair + 1) * lanes]
            up = x[:, :, half + pair * lanes : half + (pair + 1) * lanes]
            low = lower_half(gate)
            out[2 * pair, n] = jnp.where(low, gate, swapped(up))
            out[2 * pair + 1, n] = jnp.where(low, swapped(gate), up)


def join_cols(own, low, high, far, *refs):
    outs, parts = refs[:-1], refs[-1]
    y = lax.axis_index("y")
    parts[y] = own[...]
    parts[(y + 3) % Y] = low[...]
    parts[(y + 1) % Y] = high[...]
    parts[(y + 2) % Y] = far[...]
    lanes = own.shape[-1]
    half = outs[0].shape[-1] // 2
    for n, out in enumerate(outs):
        for pair in range(Y // 2):
            a, b = parts[2 * pair, n], parts[2 * pair + 1, n]
            first = lower_half(a)
            out[:, :, pair * lanes : (pair + 1) * lanes] = jnp.where(first, a, swapped(b))
            out[:, :, half + pair * lanes : half + (pair + 1) * lanes] = jnp.where(
                first, swapped(a), b
            )


def prepare(counts, order, hidden, master, out):
    batches, batch_rows = order.shape
    experts, rows_shard, width = master.shape
    lanes = out.shape[-1]
    half = width // 2
    group_here = lax.axis_index("y") * C + lax.axis_index("core")
    count = counts[group_here, lax.axis_index("x") * Z + lax.axis_index("z")]
    blocks = []
    for m in range(batches):
        at = m * batch_rows
        slot = lax.broadcasted_iota(jnp.int32, (batch_rows, hidden.shape[1]), 0) + at
        live = jnp.where(slot < count, hidden[at : at + batch_rows, :].astype(jnp.float32), 0.0)
        row = lax.broadcasted_iota(jnp.int32, (batch_rows, batch_rows), 0)
        moves = (jnp.broadcast_to(order[m : m + 1, :], row.shape) == row).astype(jnp.bfloat16)
        blocks.append(
            jnp.dot(moves, live.astype(jnp.bfloat16), preferred_element_type=jnp.float32)
        )
    upper = jnp.concatenate(blocks[: batches // 2], axis=0)
    lower = jnp.concatenate(blocks[batches // 2 :], axis=0)
    weights = experts * rows_shard
    for pair in range(Y // 2):
        cut = slice(pair * lanes, (pair + 1) * lanes)
        first = lower_half(upper[:, cut])
        out[2 * pair, weights:, :] = jnp.where(
            first, upper[:, cut], swapped(lower[:, cut])
        ).astype(jnp.bfloat16)
        out[2 * pair + 1, weights:, :] = jnp.where(
            first, swapped(upper[:, cut]), lower[:, cut]
        ).astype(jnp.bfloat16)
        gate = jnp.concatenate([master[e, :, cut] for e in range(experts)], axis=0)
        up_cut = slice(half + pair * lanes, half + (pair + 1) * lanes)
        up = jnp.concatenate([master[e, :, up_cut] for e in range(experts)], axis=0)
        first = lower_half(gate)
        out[2 * pair, :weights, :] = jnp.where(first, gate, swapped(up)).astype(jnp.bfloat16)
        out[2 * pair + 1, :weights, :] = jnp.where(first, swapped(gate), up).astype(jnp.bfloat16)


def pick_old(slots, payload, out, table, picked, sem):
    experts, rows, _ = table.shape
    rows_shard = rows // Y
    parts = [payload[y, : experts * rows_shard, :].astype(jnp.float32) for y in range(Y)]
    for e in range(experts):
        table[e] = jnp.concatenate(
            [part[e * rows_shard : (e + 1) * rows_shard] for part in parts], axis=0
        ).astype(jnp.bfloat16)
    for p in range(PLACES):
        picked[p] = table[slots[p]]
    copy = pltpu.make_async_copy(picked, out, sem)
    copy.start()
    copy.wait()


def adam(old, new, total, got, own, low, high, far, out, after, state, acc, table):
    experts = acc.shape[0]
    rows = state.shape[3]
    y_here = lax.axis_index("y")
    state[y_here] = own[...]
    state[(y_here + 3) % Y] = low[...]
    state[(y_here + 1) % Y] = high[...]
    state[(y_here + 2) % Y] = far[...]
    acc[...] = jnp.zeros_like(acc)
    for p in range(PLACES):
        acc[old[p]] += got[p]
    for e in range(experts):
        master, first, second = (
            jnp.concatenate([state[y, n, e] for y in range(Y)], axis=0) for n in range(3)
        )
        grad = acc[e] / total[e]
        new_first = decay_first * first + (1.0 - decay_first) * grad
        new_second = decay_second * second + (1.0 - decay_second) * grad * grad
        first_hat = new_first / (1.0 - decay_first**step_number)
        second_hat = new_second / (1.0 - decay_second**step_number)
        new_master = master - learn_rate * (
            first_hat / (jnp.sqrt(second_hat) + epsilon) + weight_decay * master
        )
        table[e] = new_master.astype(jnp.bfloat16)
        for n, value in enumerate((new_master, new_first, new_second)):
            for y in range(Y):
                after[y, n, e] = value[y * rows : (y + 1) * rows]
    for p in range(PLACES):
        out[p] = table[new[p]]


def half_grad(out_ref, local_ref, chunks, half):
    rows_shard = out_ref.shape[1] // Y
    wide = PLACES * rows_shard
    for y in range(Y):
        at = pl.multiple_of((2 * y + half) * wide, wide)
        total, row = None, 0
        for chunk in chunks:
            rows = chunk.shape[0]
            term = jnp.dot(
                local_ref[:, row : row + rows],
                chunk[:, pl.ds(at, wide)],
                preferred_element_type=jnp.float32,
            )
            total = term if total is None else total + term
            row += rows
        out_ref[:, y * rows_shard : (y + 1) * rows_shard, :] = total.T.reshape(
            PLACES, rows_shard, -1
        )


def grad_theirs(mine, theirs, payload, *refs):
    chunks, (out_ref, local_ref, w_ref) = refs[:-3], refs[-3:]
    y_here, core = lax.axis_index("y"), lax.axis_index("core")
    rows_shard = mine.shape[1] // Y
    wide = PLACES * rows_shard
    for source, which in ((mine, core), (theirs, 1 - core)):
        block = source[...].astype(jnp.float32)
        for y in range(Y):
            w_ref[pl.ds(pl.multiple_of((2 * y + which) * wide, wide), wide), :] = (
                block[:, y * rows_shard : (y + 1) * rows_shard, :]
                .reshape(wide, -1)
                .astype(jnp.bfloat16)
            )
    packed = chunks[-1].shape[0]
    weights = payload.shape[1] - packed
    row = 0
    for (step, part), chunk in zip(LINE, chunks):
        rows = chunk.shape[0]
        both = jnp.dot(chunk[...], w_ref[...], preferred_element_type=jnp.float32)
        other = swapped(both)
        first = lower_half(both)
        gate = jnp.where(first, both, other)
        sigma = jax.nn.sigmoid(gate)
        active = gate * sigma
        slope = sigma * (1.0 + gate * (1.0 - sigma))
        hidden = payload[(y_here + step) % Y, weights:, :].astype(jnp.float32)
        around = swapped(hidden)
        begin = lower_half(hidden)
        halves = [jnp.where(begin, hidden, around), jnp.where(begin, around, hidden)]
        incoming = jnp.concatenate(halves, axis=0) if part is None else halves[part]
        local = jnp.where(first, incoming * other * slope, incoming * active)
        local_ref[:, row : row + rows] = local.T.astype(jnp.bfloat16)
        row += rows
    half_grad(out_ref, local_ref, chunks, 1 - core)


def grad_mine(local_ref, *refs):
    chunks, out_ref = refs[:-1], refs[-1]
    half_grad(out_ref, local_ref, chunks, lax.axis_index("core"))


def join(source, out, which, blocks, sems):
    lanes = source.shape[-1]
    half = out.shape[-1] // 2
    copies = []
    for y in range(Y):
        for pair in range(Y // 2):
            a = source[2 * pair, y].astype(jnp.float32)
            b = source[2 * pair + 1, y].astype(jnp.float32)
            first = lower_half(a)
            blocks[y, :, pair * lanes : (pair + 1) * lanes] = jnp.where(
                first, a, swapped(b)
            ).astype(jnp.bfloat16)
            blocks[y, :, half + pair * lanes : half + (pair + 1) * lanes] = jnp.where(
                first, swapped(a), b
            ).astype(jnp.bfloat16)
        copy = pltpu.make_async_copy(blocks.at[y], out.at[y, which], sems.at[y])
        copy.start()
        copies.append(copy)
    for copy in copies:
        copy.wait()


def join_mine(source, out, blocks, sems):
    join(source, out, lax.axis_index("core"), blocks, sems)


def join_theirs(source, begun, out, blocks, sems):
    join(source, out, 1 - lax.axis_index("core"), blocks, sems)


def shards(
    tokens, hidden_grad, routing, row_count, old_slots, new_slots, master, first_moment, second_moment
):
    y = lax.axis_index("y")
    experts, rows_shard, width = master.shape
    hid = width // 2
    part = hid // Y
    lanes = 2 * part
    f32, bf16 = jnp.float32, jnp.bfloat16
    own = tokens[0, 0]
    rows = own.shape[0]
    half_rows = rows // 2
    own_a, own_b = own[:half_rows], own[half_rows:]

    payload = pl.pallas_call(
        prepare,
        out_shape=jax.ShapeDtypeStruct((Y, experts * rows_shard + half_rows, lanes), bf16),
        in_specs=[SMEM, VMEM, VMEM, VMEM],
        out_specs=VMEM,
        name="prepare",
    )(row_count, routing[0, 0], hidden_grad[0, 0], master)
    payload = lax.all_to_all(payload, "y", 0, 0, tiled=True)
    low_a = lax.ppermute(own_a, "y", UP)
    high_b = lax.ppermute(own_b, "y", DOWN)
    low_b = lax.ppermute(own_b, "y", UP)
    high_a = lax.ppermute(own_a, "y", DOWN)
    picked = pl.pallas_call(
        pick_old,
        out_shape=jax.ShapeDtypeStruct((PLACES, Y * rows_shard, lanes), bf16),
        in_specs=[SMEM, VMEM],
        out_specs=pl.BlockSpec(memory_space=pltpu.MemorySpace.HBM),
        scratch_shapes=[
            pltpu.VMEM((experts, Y * rows_shard, lanes), bf16),
            pltpu.VMEM((PLACES, Y * rows_shard, lanes), bf16),
            pltpu.SemaphoreType.DMA(()),
        ],
        compiler_params=grant(4),
        name="pick_old",
    )(old_slots, payload)
    landed = lax.all_to_all(picked, ("x", "z"), 0, 0, tiled=True)
    far_a = lax.ppermute(low_a, "y", UP)
    far_b = lax.ppermute(high_b, "y", DOWN)

    def by_rows(x):
        return (
            x.reshape(PLACES, Y, rows_shard, lanes)
            .transpose(1, 0, 2, 3)
            .reshape(Y, PLACES * rows_shard, lanes)
        )

    w_mine = landed
    w_theirs = lax.ppermute(w_mine, "core", SWAP)

    chunks = [own, low_a, low_b, high_a, high_b, far_a, far_b]
    line_rows = sum(c.shape[0] for c in chunks)
    deep = own.shape[1]
    grad_shape = jax.ShapeDtypeStruct((PLACES, Y * rows_shard, lanes), f32)
    sent, local = pl.pallas_call(
        grad_theirs,
        out_shape=(grad_shape, jax.ShapeDtypeStruct((lanes, line_rows), bf16)),
        in_specs=[VMEM] * (3 + len(chunks)),
        out_specs=(VMEM, VMEM),
        scratch_shapes=[pltpu.VMEM((deep, lanes), bf16)],
        compiler_params=grant(24),
        name="grad_theirs",
    )(w_mine, w_theirs, payload, *chunks)
    received = lax.ppermute(sent, "core", SWAP)
    summed = pl.pallas_call(
        grad_mine,
        out_shape=grad_shape,
        in_specs=[VMEM] * (1 + len(chunks)),
        out_specs=VMEM,
        compiler_params=grant(24),
        name="grad_mine",
    )(local, *chunks)
    summed = summed + received

    columns = pl.pallas_call(
        split_cols,
        out_shape=jax.ShapeDtypeStruct((Y, 3, experts, rows_shard, lanes), f32),
        in_specs=[VMEM] * 3,
        out_specs=VMEM,
        compiler_params=grant(4),
        name="split_cols",
    )(master, first_moment, second_moment)

    def for_chip(step, x):
        return lax.dynamic_index_in_dim(x, (y + step) % Y, keepdims=False)

    m_low = lax.ppermute(for_chip(1, columns), "y", UP)
    m_high = lax.ppermute(for_chip(3, columns), "y", DOWN)
    m_far = lax.ppermute(for_chip(2, columns), "y", ACROSS)
    m_own = for_chip(0, columns)

    got = lax.all_to_all(summed, ("x", "z"), 0, 0, tiled=True)
    select = (old_slots[:, None] == jnp.arange(experts, dtype=jnp.int32)[None, :]).astype(f32)
    per_slot = jnp.sum(row_count.astype(f32), axis=0)
    total = jnp.dot(per_slot, select, precision=lax.Precision.HIGHEST)
    picked, after = pl.pallas_call(
        adam,
        out_shape=(
            jax.ShapeDtypeStruct((PLACES, Y * rows_shard, lanes), bf16),
            jax.ShapeDtypeStruct((Y, 3, experts, rows_shard, lanes), f32),
        ),
        in_specs=[SMEM] * 3 + [VMEM] * 5,
        out_specs=(VMEM, VMEM),
        scratch_shapes=[
            pltpu.VMEM((Y, 3, experts, rows_shard, lanes), f32),
            pltpu.VMEM((experts, Y * rows_shard, lanes), f32),
            pltpu.VMEM((experts, Y * rows_shard, lanes), bf16),
        ],
        compiler_params=grant(6),
        name="adam",
    )(old_slots, new_slots, total, got, m_own, m_low, m_high, m_far)
    landed = lax.all_to_all(picked, ("x", "z"), 0, 0, tiled=True)

    s_low = lax.ppermute(for_chip(1, after), "y", UP)
    s_high = lax.ppermute(for_chip(3, after), "y", DOWN)
    s_far = lax.ppermute(for_chip(2, after), "y", ACROSS)
    whole = jax.ShapeDtypeStruct((experts, rows_shard, width), f32)
    new_master, new_first, new_second = pl.pallas_call(
        join_cols,
        out_shape=(whole,) * 3,
        in_specs=[VMEM] * 4,
        out_specs=(VMEM,) * 3,
        scratch_shapes=[pltpu.VMEM((Y, 3, experts, rows_shard, lanes), f32)],
        compiler_params=grant(6),
        name="join_cols",
    )(for_chip(0, after), s_low, s_high, s_far)

    landed = by_rows(landed)
    copies = jnp.broadcast_to(landed[None], (Y, *landed.shape))
    mine = lax.all_to_all(copies, "y", 0, 0, tiled=True)
    theirs = lax.ppermute(mine, "core", SWAP)
    block_rows = PLACES * rows_shard
    hbm = pl.BlockSpec(memory_space=pltpu.MemorySpace.HBM)
    scratch = [pltpu.VMEM((Y, block_rows, width), bf16), pltpu.SemaphoreType.DMA((Y,))]
    whole = jax.ShapeDtypeStruct((Y, C, block_rows, width), bf16)
    begun = pl.pallas_call(
        join_mine,
        out_shape=whole,
        in_specs=[VMEM],
        out_specs=hbm,
        scratch_shapes=scratch,
        compiler_params=grant(8),
        name="join_mine",
    )(mine)
    new_weights = pl.pallas_call(
        join_theirs,
        out_shape=whole,
        in_specs=[VMEM, hbm],
        out_specs=hbm,
        scratch_shapes=scratch,
        input_output_aliases={1: 0},
        compiler_params=grant(8),
        name="join_theirs",
    )(theirs, begun)
    return (new_weights.reshape(1, -1, width), new_master, new_first, new_second)


def solution(mesh):
    fine = Mesh(mesh.devices.reshape(Y, C, X, Z), ("y", "core", "x", "z"))
    dp, place = ("y", "core"), ("x", "z")
    placed = (
        P(dp, place, None, None),
        P(dp, place, None, None),
        P(dp, place, None, None),
        P(),
        P(),
        P(),
        P(None, dp + place, None),
        P(None, dp + place, None),
        P(None, dp + place, None),
    )

    return jax.shard_map(
        shards,
        mesh=fine,
        in_specs=placed,
        out_specs=(
            P(place, None, None),
            P(None, dp + place, None),
            P(None, dp + place, None),
            P(None, dp + place, None),
        ),
        check_vma=False,
    )
```

```python
import jax
import jax.numpy as jnp
from jax import lax
from jax.experimental import pallas as pl
from jax.experimental.pallas import tpu as pltpu
from jax.sharding import Mesh
from jax.sharding import PartitionSpec as P


decay_first = 0.9
decay_second = 0.95
learn_rate = 0.001
weight_decay = 0.1
epsilon = 1e-08
step_number = 20.0

Y, C, X, Z = 4, 2, 4, 16
PLACES = X * Z
UP = [(i, (i + 1) % Y) for i in range(Y)]
DOWN = [(i, (i - 1) % Y) for i in range(Y)]
ACROSS = [(i, (i + 2) % Y) for i in range(Y)]
SWAP = [(0, 1), (1, 0)]
LINE = ((0, None), (3, 0), (3, 1), (1, 0), (1, 1), (2, 0), (2, 1))
VMEM = pl.BlockSpec(memory_space=pltpu.VMEM)
SMEM = pl.BlockSpec(memory_space=pltpu.SMEM)
ANY = pl.BlockSpec(memory_space=pl.ANY)


def grant(mib):
    return pltpu.CompilerParams(vmem_limit_bytes=mib << 20)


def lower_half(x):
    return lax.broadcasted_iota(jnp.int32, x.shape, x.ndim - 1) < x.shape[-1] // 2


def swapped(x):
    return pltpu.roll(x, x.shape[-1] // 2, x.ndim - 1)


def split_cols(*refs):
    ins, out = refs[:-1], refs[-1]
    lanes = out.shape[-1]
    half = ins[0].shape[-1] // 2
    for n, x in enumerate(ins):
        for pair in range(Y // 2):
            gate = x[:, :, pair * lanes : (pair + 1) * lanes]
            up = x[:, :, half + pair * lanes : half + (pair + 1) * lanes]
            low = lower_half(gate)
            out[2 * pair, n] = jnp.where(low, gate, swapped(up))
            out[2 * pair + 1, n] = jnp.where(low, swapped(gate), up)


def join_cols(own, low, high, far, *refs):
    outs, parts = refs[:-1], refs[-1]
    y = lax.axis_index("y")
    parts[y] = own[...]
    parts[(y + 3) % Y] = low[...]
    parts[(y + 1) % Y] = high[...]
    parts[(y + 2) % Y] = far[...]
    lanes = own.shape[-1]
    half = outs[0].shape[-1] // 2
    for n, out in enumerate(outs):
        for pair in range(Y // 2):
            a, b = parts[2 * pair, n], parts[2 * pair + 1, n]
            first = lower_half(a)
            out[:, :, pair * lanes : (pair + 1) * lanes] = jnp.where(first, a, swapped(b))
            out[:, :, half + pair * lanes : half + (pair + 1) * lanes] = jnp.where(
                first, swapped(a), b
            )


def prepare(counts, order, hidden, master, out):
    batches, batch_rows = order.shape
    experts, rows_shard, width = master.shape
    lanes = out.shape[-1]
    half = width // 2
    group_here = lax.axis_index("y") * C + lax.axis_index("core")
    count = counts[group_here, lax.axis_index("x") * Z + lax.axis_index("z")]
    blocks = []
    for m in range(batches):
        at = m * batch_rows
        slot = lax.broadcasted_iota(jnp.int32, (batch_rows, hidden.shape[1]), 0) + at
        live = jnp.where(slot < count, hidden[at : at + batch_rows, :].astype(jnp.float32), 0.0)
        row = lax.broadcasted_iota(jnp.int32, (batch_rows, batch_rows), 0)
        moves = (jnp.broadcast_to(order[m : m + 1, :], row.shape) == row).astype(jnp.bfloat16)
        blocks.append(
            jnp.dot(moves, live.astype(jnp.bfloat16), preferred_element_type=jnp.float32)
        )
    upper = jnp.concatenate(blocks[: batches // 2], axis=0)
    lower = jnp.concatenate(blocks[batches // 2 :], axis=0)
    weights = experts * rows_shard
    for pair in range(Y // 2):
        cut = slice(pair * lanes, (pair + 1) * lanes)
        first = lower_half(upper[:, cut])
        out[2 * pair, weights:, :] = jnp.where(
            first, upper[:, cut], swapped(lower[:, cut])
        ).astype(jnp.bfloat16)
        out[2 * pair + 1, weights:, :] = jnp.where(
            first, swapped(upper[:, cut]), lower[:, cut]
        ).astype(jnp.bfloat16)
        gate = jnp.concatenate([master[e, :, cut] for e in range(experts)], axis=0)
        up_cut = slice(half + pair * lanes, half + (pair + 1) * lanes)
        up = jnp.concatenate([master[e, :, up_cut] for e in range(experts)], axis=0)
        first = lower_half(gate)
        out[2 * pair, :weights, :] = jnp.where(first, gate, swapped(up)).astype(jnp.bfloat16)
        out[2 * pair + 1, :weights, :] = jnp.where(first, swapped(gate), up).astype(jnp.bfloat16)


def pick_old(slots, payload, out, table, picked, sem):
    experts, rows, _ = table.shape
    rows_shard = rows // Y
    parts = [payload[y, : experts * rows_shard, :].astype(jnp.float32) for y in range(Y)]
    for e in range(experts):
        table[e] = jnp.concatenate(
            [part[e * rows_shard : (e + 1) * rows_shard] for part in parts], axis=0
        ).astype(jnp.bfloat16)
    for p in range(PLACES):
        picked[p] = table[slots[p]]
    copy = pltpu.make_async_copy(picked, out, sem)
    copy.start()
    copy.wait()


def adam(old, new, total, got, own, low, high, far, out, after, state, acc, table):
    experts, pairs = acc.shape[:2]
    rows = state.shape[3]
    y_here = lax.axis_index("y")
    state[y_here] = own[...]
    state[(y_here + 3) % Y] = low[...]
    state[(y_here + 1) % Y] = high[...]
    state[(y_here + 2) % Y] = far[...]
    acc[...] = jnp.zeros_like(acc)
    for p in range(PLACES):
        acc[old[p]] += got[p, :pairs] * jnp.exp2(got[p, pairs:] - 14.0)
    for e in range(experts):
        master, first, second = (
            jnp.concatenate([state[y, n, e] for y in range(Y)], axis=0) for n in range(3)
        )
        grad = jnp.concatenate([acc[e, t] for t in range(pairs)], axis=0) / total[e]
        new_first = decay_first * first + (1.0 - decay_first) * grad
        new_second = decay_second * second + (1.0 - decay_second) * grad * grad
        first_hat = new_first / (1.0 - decay_first**step_number)
        second_hat = new_second / (1.0 - decay_second**step_number)
        new_master = master - learn_rate * (
            first_hat / (jnp.sqrt(second_hat) + epsilon) + weight_decay * master
        )
        table[e] = new_master.astype(jnp.bfloat16)
        for n, value in enumerate((new_master, new_first, new_second)):
            for y in range(Y):
                after[y, n, e] = value[y * rows : (y + 1) * rows]
    for p in range(PLACES):
        out[p] = table[new[p]]


def half_grad(out_ref, local_ref, chunks, half):
    rows_shard = out_ref.shape[1] // Y
    wide = PLACES * rows_shard
    peak = None
    for y in range(Y):
        at = pl.multiple_of((2 * y + half) * wide, wide)
        total, row = None, 0
        for chunk in chunks:
            rows = chunk.shape[0]
            term = jnp.dot(
                local_ref[:, row : row + rows],
                chunk[:, pl.ds(at, wide)],
                preferred_element_type=jnp.float32,
            )
            total = term if total is None else total + term
            row += rows
        size = jnp.abs(total)
        peak = size if peak is None else jnp.maximum(peak, size)
        out_ref[:PLACES, y * rows_shard : (y + 1) * rows_shard, :] = total.T.reshape(
            PLACES, rows_shard, -1
        )
    out_ref[PLACES] = jnp.broadcast_to(jnp.max(peak, keepdims=True), out_ref.shape[1:])


def forward_part(chunk, weights, which):
    rows_shard = weights.shape[1] // Y
    wide = PLACES * rows_shard
    total = None
    for y in range(Y):
        at = pl.multiple_of((2 * y + which) * wide, wide)
        block = weights[:, y * rows_shard : (y + 1) * rows_shard, :].astype(jnp.float32)
        term = jnp.dot(
            chunk[:, pl.ds(at, wide)],
            block.reshape(wide, -1).astype(jnp.bfloat16),
            preferred_element_type=jnp.float32,
        )
        total = term if total is None else total + term
    return total


def forward_mine(mine, *refs):
    chunks, out_ref = refs[:-1], refs[-1]
    weights = mine[...]
    row = 0
    for chunk in chunks:
        rows = chunk.shape[0]
        out_ref[row : row + rows, :] = forward_part(chunk, weights, lax.axis_index("core"))
        row += rows


def grad_theirs(part_ref, theirs, payload, *refs):
    chunks, (out_ref, local_ref) = refs[:-2], refs[-2:]
    y_here, core = lax.axis_index("y"), lax.axis_index("core")
    weights = theirs[...]
    packed = chunks[-1].shape[0]
    head = payload.shape[1] - packed
    row = 0
    for (step, part), chunk in zip(LINE, chunks):
        rows = chunk.shape[0]
        both = part_ref[row : row + rows, :] + forward_part(chunk, weights, 1 - core)
        other = swapped(both)
        first = lower_half(both)
        gate = jnp.where(first, both, other)
        sigma = jax.nn.sigmoid(gate)
        active = gate * sigma
        slope = sigma * (1.0 + gate * (1.0 - sigma))
        hidden = payload[(y_here + step) % Y, head:, :].astype(jnp.float32)
        around = swapped(hidden)
        begin = lower_half(hidden)
        halves = [jnp.where(begin, hidden, around), jnp.where(begin, around, hidden)]
        incoming = jnp.concatenate(halves, axis=0) if part is None else halves[part]
        local = jnp.where(first, incoming * other * slope, incoming * active)
        local_ref[:, row : row + rows] = local.T.astype(jnp.bfloat16)
        row += rows
    half_grad(out_ref, local_ref, chunks, 1 - core)


def grad_mine(local_ref, *refs):
    chunks, out_ref = refs[:-1], refs[-1]
    half_grad(out_ref, local_ref, chunks, lax.axis_index("core"))


def combine(mine, theirs, out):
    pairs = out.shape[1] - 1
    bits = jnp.ceil(jnp.log2(jnp.maximum(mine[PLACES] + theirs[PLACES], 1e-30)))
    scale = jnp.exp2(14.0 - bits)
    for t in range(pairs):
        cut = slice(2 * t, 2 * t + 2)
        out[:, t] = (mine[:PLACES, cut, :] + theirs[:PLACES, cut, :]) * scale[cut]
    out[:, pairs] = jnp.broadcast_to(bits[:2], (PLACES, 2, bits.shape[1]))


def join(source, out, which, blocks, sems):
    lanes = source.shape[-1]
    half = out.shape[-1] // 2
    copies = []
    for y in range(Y):
        for pair in range(Y // 2):
            a = source[2 * pair, y].astype(jnp.float32)
            b = source[2 * pair + 1, y].astype(jnp.float32)
            first = lower_half(a)
            blocks[y, :, pair * lanes : (pair + 1) * lanes] = jnp.where(
                first, a, swapped(b)
            ).astype(jnp.bfloat16)
            blocks[y, :, half + pair * lanes : half + (pair + 1) * lanes] = jnp.where(
                first, swapped(a), b
            ).astype(jnp.bfloat16)
        copy = pltpu.make_async_copy(blocks.at[y], out.at[y, which], sems.at[y])
        copy.start()
        copies.append(copy)
    for copy in copies:
        copy.wait()


def join_mine(source, out, blocks, sems):
    join(source, out, lax.axis_index("core"), blocks, sems)


def join_theirs(source, begun, out, blocks, sems):
    join(source, out, 1 - lax.axis_index("core"), blocks, sems)


def shards(
    tokens, hidden_grad, routing, row_count, old_slots, new_slots, master, first_moment, second_moment
):
    y = lax.axis_index("y")
    experts, rows_shard, width = master.shape
    hid = width // 2
    part = hid // Y
    lanes = 2 * part
    f32, bf16 = jnp.float32, jnp.bfloat16
    own = tokens[0, 0]
    rows = own.shape[0]
    half_rows = rows // 2
    own_a, own_b = own[:half_rows], own[half_rows:]

    payload = pl.pallas_call(
        prepare,
        out_shape=jax.ShapeDtypeStruct((Y, experts * rows_shard + half_rows, lanes), bf16),
        in_specs=[SMEM, VMEM, VMEM, VMEM],
        out_specs=VMEM,
        name="prepare",
    )(row_count, routing[0, 0], hidden_grad[0, 0], master)
    payload = lax.all_to_all(payload, "y", 0, 0, tiled=True)
    low_a = lax.ppermute(own_a, "y", UP)
    high_b = lax.ppermute(own_b, "y", DOWN)
    low_b = lax.ppermute(own_b, "y", UP)
    high_a = lax.ppermute(own_a, "y", DOWN)
    picked = pl.pallas_call(
        pick_old,
        out_shape=jax.ShapeDtypeStruct((PLACES, Y * rows_shard, lanes), bf16),
        in_specs=[SMEM, VMEM],
        out_specs=pl.BlockSpec(memory_space=pltpu.MemorySpace.HBM),
        scratch_shapes=[
            pltpu.VMEM((experts, Y * rows_shard, lanes), bf16),
            pltpu.VMEM((PLACES, Y * rows_shard, lanes), bf16),
            pltpu.SemaphoreType.DMA(()),
        ],
        compiler_params=grant(4),
        name="pick_old",
    )(old_slots, payload)
    landed = lax.all_to_all(picked, ("x", "z"), 0, 0, tiled=True)
    far_a = lax.ppermute(low_a, "y", UP)
    far_b = lax.ppermute(high_b, "y", DOWN)

    def by_rows(x):
        return (
            x.reshape(PLACES, Y, rows_shard, lanes)
            .transpose(1, 0, 2, 3)
            .reshape(Y, PLACES * rows_shard, lanes)
        )

    w_mine = landed
    w_theirs = lax.ppermute(w_mine, "core", SWAP)

    chunks = [own, low_a, low_b, high_a, high_b, far_a, far_b]
    line_rows = sum(c.shape[0] for c in chunks)
    forward = pl.pallas_call(
        forward_mine,
        out_shape=jax.ShapeDtypeStruct((line_rows, lanes), f32),
        in_specs=[VMEM] * (1 + len(chunks)),
        out_specs=VMEM,
        compiler_params=grant(24),
        name="forward_mine",
    )(w_mine, *chunks)
    grad_shape = jax.ShapeDtypeStruct((PLACES + 1, Y * rows_shard, lanes), f32)
    sent, local = pl.pallas_call(
        grad_theirs,
        out_shape=(grad_shape, jax.ShapeDtypeStruct((lanes, line_rows), bf16)),
        in_specs=[VMEM] * (3 + len(chunks)),
        out_specs=(VMEM, VMEM),
        compiler_params=grant(24),
        name="grad_theirs",
    )(forward, w_theirs, payload, *chunks)
    received = lax.ppermute(sent, "core", SWAP)
    summed = pl.pallas_call(
        grad_mine,
        out_shape=grad_shape,
        in_specs=[VMEM] * (1 + len(chunks)),
        out_specs=VMEM,
        compiler_params=grant(24),
        name="grad_mine",
    )(local, *chunks)
    pairs = Y * rows_shard // 2
    scaled = pl.pallas_call(
        combine,
        out_shape=jax.ShapeDtypeStruct((PLACES, pairs + 1, 2, lanes), f32),
        in_specs=[VMEM] * 2,
        out_specs=VMEM,
        compiler_params=grant(6),
        name="combine",
    )(summed, received)

    columns = pl.pallas_call(
        split_cols,
        out_shape=jax.ShapeDtypeStruct((Y, 3, experts, rows_shard, lanes), f32),
        in_specs=[VMEM] * 3,
        out_specs=VMEM,
        compiler_params=grant(4),
        name="split_cols",
    )(master, first_moment, second_moment)

    def for_chip(step, x):
        return lax.dynamic_index_in_dim(x, (y + step) % Y, keepdims=False)

    m_low = lax.ppermute(for_chip(1, columns), "y", UP)
    m_high = lax.ppermute(for_chip(3, columns), "y", DOWN)
    m_far = lax.ppermute(for_chip(2, columns), "y", ACROSS)
    m_own = for_chip(0, columns)

    got = lax.all_to_all(scaled.astype(jnp.float16), ("x", "z"), 0, 0, tiled=True)
    got = got.astype(f32)
    select = (old_slots[:, None] == jnp.arange(experts, dtype=jnp.int32)[None, :]).astype(f32)
    per_slot = jnp.sum(row_count.astype(f32), axis=0)
    total = jnp.dot(per_slot, select, precision=lax.Precision.HIGHEST)
    picked, after = pl.pallas_call(
        adam,
        out_shape=(
            jax.ShapeDtypeStruct((PLACES, Y * rows_shard, lanes), bf16),
            jax.ShapeDtypeStruct((Y, 3, experts, rows_shard, lanes), f32),
        ),
        in_specs=[SMEM] * 3 + [VMEM] * 5,
        out_specs=(VMEM, VMEM),
        scratch_shapes=[
            pltpu.VMEM((Y, 3, experts, rows_shard, lanes), f32),
            pltpu.VMEM((experts, pairs, 2, lanes), f32),
            pltpu.VMEM((experts, Y * rows_shard, lanes), bf16),
        ],
        compiler_params=grant(6),
        name="adam",
    )(old_slots, new_slots, total, got, m_own, m_low, m_high, m_far)
    landed = lax.all_to_all(picked, ("x", "z"), 0, 0, tiled=True)

    s_low = lax.ppermute(for_chip(1, after), "y", UP)
    s_high = lax.ppermute(for_chip(3, after), "y", DOWN)
    s_far = lax.ppermute(for_chip(2, after), "y", ACROSS)
    whole = jax.ShapeDtypeStruct((experts, rows_shard, width), f32)
    new_master, new_first, new_second = pl.pallas_call(
        join_cols,
        out_shape=(whole,) * 3,
        in_specs=[VMEM] * 4,
        out_specs=(VMEM,) * 3,
        scratch_shapes=[pltpu.VMEM((Y, 3, experts, rows_shard, lanes), f32)],
        compiler_params=grant(6),
        name="join_cols",
    )(for_chip(0, after), s_low, s_high, s_far)

    landed = by_rows(landed)
    copies = jnp.broadcast_to(landed[None], (Y, *landed.shape))
    mine = lax.all_to_all(copies, "y", 0, 0, tiled=True)
    theirs = lax.ppermute(mine, "core", SWAP)
    block_rows = PLACES * rows_shard
    hbm = pl.BlockSpec(memory_space=pltpu.MemorySpace.HBM)
    scratch = [pltpu.VMEM((Y, block_rows, width), bf16), pltpu.SemaphoreType.DMA((Y,))]
    whole = jax.ShapeDtypeStruct((Y, C, block_rows, width), bf16)
    begun = pl.pallas_call(
        join_mine,
        out_shape=whole,
        in_specs=[VMEM],
        out_specs=hbm,
        scratch_shapes=scratch,
        compiler_params=grant(8),
        name="join_mine",
    )(mine)
    new_weights = pl.pallas_call(
        join_theirs,
        out_shape=whole,
        in_specs=[VMEM, hbm],
        out_specs=hbm,
        scratch_shapes=scratch,
        input_output_aliases={1: 0},
        compiler_params=grant(8),
        name="join_theirs",
    )(theirs, begun)
    return (new_weights.reshape(1, -1, width), new_master, new_first, new_second)


def solution(mesh):
    fine = Mesh(mesh.devices.reshape(Y, C, X, Z), ("y", "core", "x", "z"))
    dp, place = ("y", "core"), ("x", "z")
    placed = (
        P(dp, place, None, None),
        P(dp, place, None, None),
        P(dp, place, None, None),
        P(),
        P(),
        P(),
        P(None, dp + place, None),
        P(None, dp + place, None),
        P(None, dp + place, None),
    )

    return jax.shard_map(
        shards,
        mesh=fine,
        in_specs=placed,
        out_specs=(
            P(place, None, None),
            P(None, dp + place, None),
            P(None, dp + place, None),
            P(None, dp + place, None),
        ),
        check_vma=False,
    )
```

```python
import jax
import jax.numpy as jnp
from jax import lax
from jax.experimental import pallas as pl
from jax.experimental.pallas import tpu as pltpu
from jax.sharding import Mesh
from jax.sharding import PartitionSpec as P


decay_first = 0.9
decay_second = 0.95
learn_rate = 0.001
weight_decay = 0.1
epsilon = 1e-08
step_number = 20.0

Y, C, X, Z = 4, 2, 4, 16
PLACES = X * Z
UP = [(i, (i + 1) % Y) for i in range(Y)]
DOWN = [(i, (i - 1) % Y) for i in range(Y)]
ACROSS = [(i, (i + 2) % Y) for i in range(Y)]
SWAP = [(0, 1), (1, 0)]
LINE = ((0, None), (3, 0), (3, 1), (1, 0), (1, 1), (2, 0), (2, 1))
VMEM = pl.BlockSpec(memory_space=pltpu.VMEM)
SMEM = pl.BlockSpec(memory_space=pltpu.SMEM)
ANY = pl.BlockSpec(memory_space=pl.ANY)


def grant(mib):
    return pltpu.CompilerParams(vmem_limit_bytes=mib << 20)


def lower_half(x):
    return lax.broadcasted_iota(jnp.int32, x.shape, x.ndim - 1) < x.shape[-1] // 2


def swapped(x):
    return pltpu.roll(x, x.shape[-1] // 2, x.ndim - 1)


def split_cols(*refs):
    ins, out = refs[:-1], refs[-1]
    lanes = out.shape[-1]
    half = ins[0].shape[-1] // 2
    for n, x in enumerate(ins):
        for pair in range(Y // 2):
            gate = x[:, :, pair * lanes : (pair + 1) * lanes]
            up = x[:, :, half + pair * lanes : half + (pair + 1) * lanes]
            low = lower_half(gate)
            out[2 * pair, n] = jnp.where(low, gate, swapped(up))
            out[2 * pair + 1, n] = jnp.where(low, swapped(gate), up)


def join_cols(own, low, high, far, *refs):
    outs, parts = refs[:-1], refs[-1]
    y = lax.axis_index("y")
    parts[y] = own[...]
    parts[(y + 3) % Y] = low[...]
    parts[(y + 1) % Y] = high[...]
    parts[(y + 2) % Y] = far[...]
    lanes = own.shape[-1]
    half = outs[0].shape[-1] // 2
    for n, out in enumerate(outs):
        for pair in range(Y // 2):
            a, b = parts[2 * pair, n], parts[2 * pair + 1, n]
            first = lower_half(a)
            out[:, :, pair * lanes : (pair + 1) * lanes] = jnp.where(first, a, swapped(b))
            out[:, :, half + pair * lanes : half + (pair + 1) * lanes] = jnp.where(
                first, swapped(a), b
            )


def prepare(counts, order, hidden, master, tokens, out, upper_out, lower_out, held, sems):
    whole = pltpu.make_async_copy(tokens, held, sems.at[0])
    whole.start()
    batches, batch_rows = order.shape
    experts, rows_shard, width = master.shape
    lanes = out.shape[-1]
    half = width // 2
    group_here = lax.axis_index("y") * C + lax.axis_index("core")
    count = counts[group_here, lax.axis_index("x") * Z + lax.axis_index("z")]
    blocks = []
    for m in range(batches):
        at = m * batch_rows
        slot = lax.broadcasted_iota(jnp.int32, (batch_rows, hidden.shape[1]), 0) + at
        live = jnp.where(slot < count, hidden[at : at + batch_rows, :].astype(jnp.float32), 0.0)
        row = lax.broadcasted_iota(jnp.int32, (batch_rows, batch_rows), 0)
        moves = (jnp.broadcast_to(order[m : m + 1, :], row.shape) == row).astype(jnp.bfloat16)
        blocks.append(
            jnp.dot(moves, live.astype(jnp.bfloat16), preferred_element_type=jnp.float32)
        )
    upper = jnp.concatenate(blocks[: batches // 2], axis=0)
    lower = jnp.concatenate(blocks[batches // 2 :], axis=0)
    weights = experts * rows_shard
    for pair in range(Y // 2):
        cut = slice(pair * lanes, (pair + 1) * lanes)
        first = lower_half(upper[:, cut])
        out[2 * pair, weights:, :] = jnp.where(
            first, upper[:, cut], swapped(lower[:, cut])
        ).astype(jnp.bfloat16)
        out[2 * pair + 1, weights:, :] = jnp.where(
            first, swapped(upper[:, cut]), lower[:, cut]
        ).astype(jnp.bfloat16)
        gate = jnp.concatenate([master[e, :, cut] for e in range(experts)], axis=0)
        up_cut = slice(half + pair * lanes, half + (pair + 1) * lanes)
        up = jnp.concatenate([master[e, :, up_cut] for e in range(experts)], axis=0)
        first = lower_half(gate)
        out[2 * pair, :weights, :] = jnp.where(first, gate, swapped(up)).astype(jnp.bfloat16)
        out[2 * pair + 1, :weights, :] = jnp.where(first, swapped(gate), up).astype(jnp.bfloat16)
    whole.wait()
    cut = held.shape[0] // 2
    upper_copy = pltpu.make_async_copy(held.at[pl.ds(0, cut)], upper_out, sems.at[0])
    lower_copy = pltpu.make_async_copy(held.at[pl.ds(cut, cut)], lower_out, sems.at[1])
    upper_copy.start()
    lower_copy.start()
    upper_copy.wait()
    lower_copy.wait()


def pick_old(slots, payload, out, table, picked, sem):
    experts, rows, _ = table.shape
    rows_shard = rows // Y
    parts = [payload[y, : experts * rows_shard, :].astype(jnp.float32) for y in range(Y)]
    for e in range(experts):
        table[e] = jnp.concatenate(
            [part[e * rows_shard : (e + 1) * rows_shard] for part in parts], axis=0
        ).astype(jnp.bfloat16)
    for p in range(PLACES):
        picked[p] = table[slots[p]]
    copy = pltpu.make_async_copy(picked, out, sem)
    copy.start()
    copy.wait()


def adam(old, new, total, got, own, low, high, far, out, after, state, acc, table):
    experts, _, data = acc.shape
    rows, lanes = state.shape[3:]
    y_here = lax.axis_index("y")
    state[y_here] = own[...]
    state[(y_here + 3) % Y] = low[...]
    state[(y_here + 1) % Y] = high[...]
    state[(y_here + 2) % Y] = far[...]
    acc[...] = jnp.zeros_like(acc)
    for p in range(PLACES):
        undo = jnp.exp2(got[p, :, data:] - 14.0)
        acc[old[p]] += got[p, :, :data] * jnp.concatenate([undo] * (data // lanes), axis=1)
    for e in range(experts):
        master, first, second = (
            jnp.concatenate([state[y, n, e] for y in range(Y)], axis=0) for n in range(3)
        )
        grad = jnp.concatenate(
            [acc[e, :, at : at + lanes] for at in range(0, data, lanes)], axis=0
        )
        grad = grad / total[e]
        new_first = decay_first * first + (1.0 - decay_first) * grad
        new_second = decay_second * second + (1.0 - decay_second) * grad * grad
        first_hat = new_first / (1.0 - decay_first**step_number)
        second_hat = new_second / (1.0 - decay_second**step_number)
        new_master = master - learn_rate * (
            first_hat / (jnp.sqrt(second_hat) + epsilon) + weight_decay * master
        )
        table[e] = new_master.astype(jnp.bfloat16)
        for n, value in enumerate((new_master, new_first, new_second)):
            for y in range(Y):
                after[y, n, e] = value[y * rows : (y + 1) * rows]
    for p in range(PLACES):
        out[p] = table[new[p]]


def half_grad(out_ref, local_ref, chunks, half):
    rows_shard = out_ref.shape[1] // Y
    wide = PLACES * rows_shard
    peak = None
    for y in range(Y):
        at = pl.multiple_of((2 * y + half) * wide, wide)
        total, row = None, 0
        for chunk in chunks:
            rows = chunk.shape[0]
            term = jnp.dot(
                local_ref[:, row : row + rows],
                chunk[:, pl.ds(at, wide)],
                preferred_element_type=jnp.float32,
            )
            total = term if total is None else total + term
            row += rows
        size = jnp.abs(total)
        peak = size if peak is None else jnp.maximum(peak, size)
        out_ref[:PLACES, y * rows_shard : (y + 1) * rows_shard, :] = total.T.reshape(
            PLACES, rows_shard, -1
        )
    out_ref[PLACES] = jnp.broadcast_to(jnp.max(peak, keepdims=True), out_ref.shape[1:])


def forward_part(chunk, weights, which):
    rows_shard = weights.shape[1] // Y
    wide = PLACES * rows_shard
    total = None
    for y in range(Y):
        at = pl.multiple_of((2 * y + which) * wide, wide)
        block = weights[:, y * rows_shard : (y + 1) * rows_shard, :].astype(jnp.float32)
        term = jnp.dot(
            chunk[:, pl.ds(at, wide)],
            block.reshape(wide, -1).astype(jnp.bfloat16),
            preferred_element_type=jnp.float32,
        )
        total = term if total is None else total + term
    return total


def forward_mine(mine, *refs):
    chunks, out_ref = refs[:-1], refs[-1]
    weights = mine[...]
    row = 0
    for chunk in chunks:
        rows = chunk.shape[0]
        out_ref[row : row + rows, :] = forward_part(chunk, weights, lax.axis_index("core"))
        row += rows


def grad_theirs(part_ref, mine, theirs, payload, *refs):
    chunks, (out_ref, local_ref) = refs[:-2], refs[-2:]
    y_here, core = lax.axis_index("y"), lax.axis_index("core")
    weights = theirs[...]
    packed = chunks[-1].shape[0]
    head = payload.shape[1] - packed
    row = 0
    for (step, part), chunk in zip(LINE, chunks):
        rows = chunk.shape[0]
        if row < part_ref.shape[0]:
            both = part_ref[row : row + rows, :]
        else:
            both = forward_part(chunk, mine[...], core)
        both = both + forward_part(chunk, weights, 1 - core)
        other = swapped(both)
        first = lower_half(both)
        gate = jnp.where(first, both, other)
        sigma = jax.nn.sigmoid(gate)
        active = gate * sigma
        slope = sigma * (1.0 + gate * (1.0 - sigma))
        hidden = payload[(y_here + step) % Y, head:, :].astype(jnp.float32)
        around = swapped(hidden)
        begin = lower_half(hidden)
        halves = [jnp.where(begin, hidden, around), jnp.where(begin, around, hidden)]
        incoming = jnp.concatenate(halves, axis=0) if part is None else halves[part]
        local = jnp.where(first, incoming * other * slope, incoming * active)
        local_ref[:, row : row + rows] = local.T.astype(jnp.bfloat16)
        row += rows
    half_grad(out_ref, local_ref, chunks, 1 - core)


def grad_mine(local_ref, *refs):
    chunks, out_ref = refs[:-1], refs[-1]
    half_grad(out_ref, local_ref, chunks, lax.axis_index("core"))


def combine(mine, theirs, out):
    lanes = mine.shape[-1]
    pairs = out.shape[2] // lanes - 1
    bits = jnp.ceil(jnp.log2(jnp.maximum(mine[PLACES] + theirs[PLACES], 1e-30)))
    scale = jnp.exp2(14.0 - bits)
    for t in range(pairs):
        cut = slice(2 * t, 2 * t + 2)
        out[:, :, t * lanes : (t + 1) * lanes] = (
            mine[:PLACES, cut, :] + theirs[:PLACES, cut, :]
        ) * scale[cut]
    out[:, :, pairs * lanes :] = jnp.broadcast_to(bits[:2], (PLACES, 2, bits.shape[1]))


def join(source, out, which, blocks, sems):
    lanes = source.shape[-1]
    half = out.shape[-1] // 2
    copies = []
    for y in range(Y):
        for pair in range(Y // 2):
            a = source[2 * pair, y].astype(jnp.float32)
            b = source[2 * pair + 1, y].astype(jnp.float32)
            first = lower_half(a)
            blocks[y, :, pair * lanes : (pair + 1) * lanes] = jnp.where(
                first, a, swapped(b)
            ).astype(jnp.bfloat16)
            blocks[y, :, half + pair * lanes : half + (pair + 1) * lanes] = jnp.where(
                first, swapped(a), b
            ).astype(jnp.bfloat16)
        copy = pltpu.make_async_copy(blocks.at[y], out.at[y, which], sems.at[y])
        copy.start()
        copies.append(copy)
    for copy in copies:
        copy.wait()


def join_mine(source, out, blocks, sems):
    join(source, out, lax.axis_index("core"), blocks, sems)


def join_theirs(source, begun, out, blocks, sems):
    join(source, out, 1 - lax.axis_index("core"), blocks, sems)


def shards(
    tokens, hidden_grad, routing, row_count, old_slots, new_slots, master, first_moment, second_moment
):
    y = lax.axis_index("y")
    experts, rows_shard, width = master.shape
    hid = width // 2
    part = hid // Y
    lanes = 2 * part
    f32, bf16 = jnp.float32, jnp.bfloat16
    own = tokens[0, 0]
    rows = own.shape[0]
    half_rows = rows // 2
    half_shape = jax.ShapeDtypeStruct((half_rows, own.shape[1]), bf16)
    hbm = pl.BlockSpec(memory_space=pltpu.MemorySpace.HBM)
    payload, own_a, own_b = pl.pallas_call(
        prepare,
        out_shape=(
            jax.ShapeDtypeStruct((Y, experts * rows_shard + half_rows, lanes), bf16),
            half_shape,
            half_shape,
        ),
        in_specs=[SMEM, VMEM, VMEM, VMEM, hbm],
        out_specs=(VMEM, hbm, hbm),
        scratch_shapes=[pltpu.VMEM(own.shape, bf16), pltpu.SemaphoreType.DMA((2,))],
        name="prepare",
    )(row_count, routing[0, 0], hidden_grad[0, 0], master, own)
    payload = lax.all_to_all(payload, "y", 0, 0, tiled=True)
    low_a = lax.ppermute(own_a, "y", UP)
    high_b = lax.ppermute(own_b, "y", DOWN)
    low_b = lax.ppermute(own_b, "y", UP)
    high_a = lax.ppermute(own_a, "y", DOWN)
    picked = pl.pallas_call(
        pick_old,
        out_shape=jax.ShapeDtypeStruct((PLACES, Y * rows_shard, lanes), bf16),
        in_specs=[SMEM, VMEM],
        out_specs=pl.BlockSpec(memory_space=pltpu.MemorySpace.HBM),
        scratch_shapes=[
            pltpu.VMEM((experts, Y * rows_shard, lanes), bf16),
            pltpu.VMEM((PLACES, Y * rows_shard, lanes), bf16),
            pltpu.SemaphoreType.DMA(()),
        ],
        compiler_params=grant(4),
        name="pick_old",
    )(old_slots, payload)
    landed = lax.all_to_all(picked, ("x", "z"), 0, 0, tiled=True)
    far_a = lax.ppermute(low_a, "y", UP)
    far_b = lax.ppermute(high_b, "y", DOWN)

    def by_rows(x):
        return (
            x.reshape(PLACES, Y, rows_shard, lanes)
            .transpose(1, 0, 2, 3)
            .reshape(Y, PLACES * rows_shard, lanes)
        )

    w_mine = landed
    w_theirs = lax.ppermute(w_mine, "core", SWAP)

    chunks = [own, low_a, low_b, high_a, high_b, far_a, far_b]
    line_rows = sum(c.shape[0] for c in chunks)
    forward = pl.pallas_call(
        forward_mine,
        out_shape=jax.ShapeDtypeStruct((line_rows - rows, lanes), f32),
        in_specs=[VMEM] * (len(chunks) - 1),
        out_specs=VMEM,
        compiler_params=grant(24),
        name="forward_mine",
    )(w_mine, *chunks[:-2])
    grad_shape = jax.ShapeDtypeStruct((PLACES + 1, Y * rows_shard, lanes), f32)
    sent, local = pl.pallas_call(
        grad_theirs,
        out_shape=(grad_shape, jax.ShapeDtypeStruct((lanes, line_rows), bf16)),
        in_specs=[VMEM] * (4 + len(chunks)),
        out_specs=(VMEM, VMEM),
        compiler_params=grant(24),
        name="grad_theirs",
    )(forward, w_mine, w_theirs, payload, *chunks)
    received = lax.ppermute(sent, "core", SWAP)
    summed = pl.pallas_call(
        grad_mine,
        out_shape=grad_shape,
        in_specs=[VMEM] * (1 + len(chunks)),
        out_specs=VMEM,
        compiler_params=grant(24),
        name="grad_mine",
    )(local, *chunks)
    pairs = Y * rows_shard // 2
    scaled = pl.pallas_call(
        combine,
        out_shape=jax.ShapeDtypeStruct((PLACES, 2, (pairs + 1) * lanes), f32),
        in_specs=[VMEM] * 2,
        out_specs=VMEM,
        compiler_params=grant(6),
        name="combine",
    )(summed, received)

    columns = pl.pallas_call(
        split_cols,
        out_shape=jax.ShapeDtypeStruct((Y, 3, experts, rows_shard, lanes), f32),
        in_specs=[VMEM] * 3,
        out_specs=VMEM,
        compiler_params=grant(4),
        name="split_cols",
    )(master, first_moment, second_moment)

    def for_chip(step, x):
        return lax.dynamic_index_in_dim(x, (y + step) % Y, keepdims=False)

    m_low = lax.ppermute(for_chip(1, columns), "y", UP)
    m_high = lax.ppermute(for_chip(3, columns), "y", DOWN)
    m_far = lax.ppermute(for_chip(2, columns), "y", ACROSS)
    m_own = for_chip(0, columns)

    got = lax.all_to_all(scaled.astype(jnp.float16), ("x", "z"), 0, 0, tiled=True)
    got = got.astype(f32)
    select = (old_slots[:, None] == jnp.arange(experts, dtype=jnp.int32)[None, :]).astype(f32)
    per_slot = jnp.sum(row_count.astype(f32), axis=0)
    total = jnp.dot(per_slot, select, precision=lax.Precision.HIGHEST)
    picked, after = pl.pallas_call(
        adam,
        out_shape=(
            jax.ShapeDtypeStruct((PLACES, Y * rows_shard, lanes), bf16),
            jax.ShapeDtypeStruct((Y, 3, experts, rows_shard, lanes), f32),
        ),
        in_specs=[SMEM] * 3 + [VMEM] * 5,
        out_specs=(VMEM, VMEM),
        scratch_shapes=[
            pltpu.VMEM((Y, 3, experts, rows_shard, lanes), f32),
            pltpu.VMEM((experts, 2, pairs * lanes), f32),
            pltpu.VMEM((experts, Y * rows_shard, lanes), bf16),
        ],
        compiler_params=grant(6),
        name="adam",
    )(old_slots, new_slots, total, got, m_own, m_low, m_high, m_far)
    landed = lax.all_to_all(picked, ("x", "z"), 0, 0, tiled=True)

    s_low = lax.ppermute(for_chip(1, after), "y", UP)
    s_high = lax.ppermute(for_chip(3, after), "y", DOWN)
    s_far = lax.ppermute(for_chip(2, after), "y", ACROSS)
    whole = jax.ShapeDtypeStruct((experts, rows_shard, width), f32)
    new_master, new_first, new_second = pl.pallas_call(
        join_cols,
        out_shape=(whole,) * 3,
        in_specs=[VMEM] * 4,
        out_specs=(VMEM,) * 3,
        scratch_shapes=[pltpu.VMEM((Y, 3, experts, rows_shard, lanes), f32)],
        compiler_params=grant(6),
        name="join_cols",
    )(for_chip(0, after), s_low, s_high, s_far)

    landed = by_rows(landed)
    copies = jnp.broadcast_to(landed[None], (Y, *landed.shape))
    mine = lax.all_to_all(copies, "y", 0, 0, tiled=True)
    theirs = lax.ppermute(mine, "core", SWAP)
    block_rows = PLACES * rows_shard
    scratch = [pltpu.VMEM((Y, block_rows, width), bf16), pltpu.SemaphoreType.DMA((Y,))]
    whole = jax.ShapeDtypeStruct((Y, C, block_rows, width), bf16)
    begun = pl.pallas_call(
        join_mine,
        out_shape=whole,
        in_specs=[VMEM],
        out_specs=hbm,
        scratch_shapes=scratch,
        compiler_params=grant(8),
        name="join_mine",
    )(mine)
    new_weights = pl.pallas_call(
        join_theirs,
        out_shape=whole,
        in_specs=[VMEM, hbm],
        out_specs=hbm,
        scratch_shapes=scratch,
        input_output_aliases={1: 0},
        compiler_params=grant(8),
        name="join_theirs",
    )(theirs, begun)
    return (new_weights.reshape(1, -1, width), new_master, new_first, new_second)


def solution(mesh):
    fine = Mesh(mesh.devices.reshape(Y, C, X, Z), ("y", "core", "x", "z"))
    dp, place = ("y", "core"), ("x", "z")
    placed = (
        P(dp, place, None, None),
        P(dp, place, None, None),
        P(dp, place, None, None),
        P(),
        P(),
        P(),
        P(None, dp + place, None),
        P(None, dp + place, None),
        P(None, dp + place, None),
    )

    return jax.shard_map(
        shards,
        mesh=fine,
        in_specs=placed,
        out_specs=(
            P(place, None, None),
            P(None, dp + place, None),
            P(None, dp + place, None),
            P(None, dp + place, None),
        ),
        check_vma=False,
    )
```

```python
import jax
import jax.numpy as jnp
from jax import lax
from jax.experimental import pallas as pl
from jax.experimental.pallas import tpu as pltpu
from jax.sharding import Mesh
from jax.sharding import PartitionSpec as P


decay_first = 0.9
decay_second = 0.95
learn_rate = 0.001
weight_decay = 0.1
epsilon = 1e-08
step_number = 20.0

Y, C, X, Z = 4, 2, 4, 16
PLACES = X * Z
UP = [(i, (i + 1) % Y) for i in range(Y)]
DOWN = [(i, (i - 1) % Y) for i in range(Y)]
ACROSS = [(i, (i + 2) % Y) for i in range(Y)]
SWAP = [(0, 1), (1, 0)]
APART = [(i * C + c, (i + 1 - 2 * c) % Y * C + c) for i in range(Y) for c in range(C)]
BACK = [(t, s) for s, t in APART]
VMEM = pl.BlockSpec(memory_space=pltpu.VMEM)
SMEM = pl.BlockSpec(memory_space=pltpu.SMEM)
ANY = pl.BlockSpec(memory_space=pl.ANY)


def grant(mib):
    return pltpu.CompilerParams(vmem_limit_bytes=mib << 20)


def lower_half(x):
    return lax.broadcasted_iota(jnp.int32, x.shape, x.ndim - 1) < x.shape[-1] // 2


def swapped(x):
    return pltpu.roll(x, x.shape[-1] // 2, x.ndim - 1)


def split_cols(*refs):
    ins, out = refs[:-1], refs[-1]
    lanes = out.shape[-1]
    half = ins[0].shape[-1] // 2
    for n, x in enumerate(ins):
        for pair in range(Y // 2):
            gate = x[:, :, pair * lanes : (pair + 1) * lanes]
            up = x[:, :, half + pair * lanes : half + (pair + 1) * lanes]
            low = lower_half(gate)
            out[2 * pair, n] = jnp.where(low, gate, swapped(up))
            out[2 * pair + 1, n] = jnp.where(low, swapped(gate), up)


def join_cols(own, low, high, far, *refs):
    outs, parts = refs[:-1], refs[-1]
    y = lax.axis_index("y")
    parts[y] = own[...]
    parts[(y + 3) % Y] = low[...]
    parts[(y + 1) % Y] = high[...]
    parts[(y + 2) % Y] = far[...]
    lanes = own.shape[-1]
    half = outs[0].shape[-1] // 2
    for n, out in enumerate(outs):
        for pair in range(Y // 2):
            a, b = parts[2 * pair, n], parts[2 * pair + 1, n]
            first = lower_half(a)
            out[:, :, pair * lanes : (pair + 1) * lanes] = jnp.where(first, a, swapped(b))
            out[:, :, half + pair * lanes : half + (pair + 1) * lanes] = jnp.where(
                first, swapped(a), b
            )


def prepare(counts, order, hidden, master, out):
    batches, batch_rows = order.shape
    experts, rows_shard, width = master.shape
    lanes = out.shape[-1]
    half = width // 2
    group_here = lax.axis_index("y") * C + lax.axis_index("core")
    count = counts[group_here, lax.axis_index("x") * Z + lax.axis_index("z")]
    blocks = []
    for m in range(batches):
        at = m * batch_rows
        slot = lax.broadcasted_iota(jnp.int32, (batch_rows, hidden.shape[1]), 0) + at
        live = jnp.where(slot < count, hidden[at : at + batch_rows, :].astype(jnp.float32), 0.0)
        row = lax.broadcasted_iota(jnp.int32, (batch_rows, batch_rows), 0)
        moves = (jnp.broadcast_to(order[m : m + 1, :], row.shape) == row).astype(jnp.bfloat16)
        blocks.append(
            jnp.dot(moves, live.astype(jnp.bfloat16), preferred_element_type=jnp.float32)
        )
    upper = jnp.concatenate(blocks[: batches // 2], axis=0)
    lower = jnp.concatenate(blocks[batches // 2 :], axis=0)
    weights = experts * rows_shard
    for pair in range(Y // 2):
        cut = slice(pair * lanes, (pair + 1) * lanes)
        first = lower_half(upper[:, cut])
        out[2 * pair, weights:, :] = jnp.where(
            first, upper[:, cut], swapped(lower[:, cut])
        ).astype(jnp.bfloat16)
        out[2 * pair + 1, weights:, :] = jnp.where(
            first, swapped(upper[:, cut]), lower[:, cut]
        ).astype(jnp.bfloat16)
        gate = jnp.concatenate([master[e, :, cut] for e in range(experts)], axis=0)
        up_cut = slice(half + pair * lanes, half + (pair + 1) * lanes)
        up = jnp.concatenate([master[e, :, up_cut] for e in range(experts)], axis=0)
        first = lower_half(gate)
        out[2 * pair, :weights, :] = jnp.where(first, gate, swapped(up)).astype(jnp.bfloat16)
        out[2 * pair + 1, :weights, :] = jnp.where(first, swapped(gate), up).astype(jnp.bfloat16)


def pick_old(slots, payload, out, table, picked, sem):
    experts, rows, _ = table.shape
    rows_shard = rows // Y
    parts = [payload[y, : experts * rows_shard, :].astype(jnp.float32) for y in range(Y)]
    for e in range(experts):
        table[e] = jnp.concatenate(
            [part[e * rows_shard : (e + 1) * rows_shard] for part in parts], axis=0
        ).astype(jnp.bfloat16)
    for p in range(PLACES):
        picked[p] = table[slots[p]]
    copy = pltpu.make_async_copy(picked, out, sem)
    copy.start()
    copy.wait()


def adam(old, new, total, got, own, low, high, far, out, after, state, acc, table):
    experts, _, data = acc.shape
    rows, lanes = state.shape[3:]
    y_here = lax.axis_index("y")
    state[y_here] = own[...]
    state[(y_here + 3) % Y] = low[...]
    state[(y_here + 1) % Y] = high[...]
    state[(y_here + 2) % Y] = far[...]
    acc[...] = jnp.zeros_like(acc)
    for p in range(PLACES):
        undo = jnp.exp2(got[p, :, data:] - 14.0)
        acc[old[p]] += got[p, :, :data] * jnp.concatenate([undo] * (data // lanes), axis=1)
    for e in range(experts):
        master, first, second = (
            jnp.concatenate([state[y, n, e] for y in range(Y)], axis=0) for n in range(3)
        )
        grad = jnp.concatenate(
            [acc[e, :, at : at + lanes] for at in range(0, data, lanes)], axis=0
        )
        grad = grad / total[e]
        new_first = decay_first * first + (1.0 - decay_first) * grad
        new_second = decay_second * second + (1.0 - decay_second) * grad * grad
        first_hat = new_first / (1.0 - decay_first**step_number)
        second_hat = new_second / (1.0 - decay_second**step_number)
        new_master = master - learn_rate * (
            first_hat / (jnp.sqrt(second_hat) + epsilon) + weight_decay * master
        )
        table[e] = new_master.astype(jnp.bfloat16)
        for n, value in enumerate((new_master, new_first, new_second)):
            for y in range(Y):
                after[y, n, e] = value[y * rows : (y + 1) * rows]
    for p in range(PLACES):
        out[p] = table[new[p]]


def forward_part(chunk, weights, which):
    rows_shard = weights.shape[1] // Y
    wide = PLACES * rows_shard
    total = None
    for y in range(Y):
        at = pl.multiple_of((2 * y + which) * wide, wide)
        block = weights[:, y * rows_shard : (y + 1) * rows_shard, :].astype(jnp.float32)
        term = jnp.dot(
            chunk[:, pl.ds(at, wide)],
            block.reshape(wide, -1).astype(jnp.bfloat16),
            preferred_element_type=jnp.float32,
        )
        total = term if total is None else total + term
    return total


def local_part(both, payload, source):
    packed = both.shape[0] // 2
    other = swapped(both)
    first = lower_half(both)
    gate = jnp.where(first, both, other)
    sigma = jax.nn.sigmoid(gate)
    active = gate * sigma
    slope = sigma * (1.0 + gate * (1.0 - sigma))
    hidden = payload[source, payload.shape[1] - packed :, :].astype(jnp.float32)
    around = swapped(hidden)
    begin = lower_half(hidden)
    incoming = jnp.concatenate(
        [jnp.where(begin, hidden, around), jnp.where(begin, around, hidden)], axis=0
    )
    local = jnp.where(first, incoming * other * slope, incoming * active)
    return local.T.astype(jnp.bfloat16)


def grad_part(local, chunk, y, half, wide):
    at = pl.multiple_of((2 * y + half) * wide, wide)
    return jnp.dot(local, chunk[:, pl.ds(at, wide)], preferred_element_type=jnp.float32)


def finish_grad(out_ref, begun, local, chunk, half):
    rows_shard = out_ref.shape[1] // Y
    wide = PLACES * rows_shard
    peak = None
    for y in range(Y):
        total = begun[y] + grad_part(local, chunk, y, half, wide)
        size = jnp.abs(total)
        peak = size if peak is None else jnp.maximum(peak, size)
        out_ref[:PLACES, y * rows_shard : (y + 1) * rows_shard, :] = total.T.reshape(
            PLACES, rows_shard, -1
        )
    out_ref[PLACES] = jnp.broadcast_to(jnp.max(peak, keepdims=True), out_ref.shape[1:])


def forward_mine(mine, *refs):
    chunks, out_ref = refs[:-1], refs[-1]
    weights = mine[...]
    for k, chunk in enumerate(chunks):
        out_ref[k] = forward_part(chunk, weights, lax.axis_index("core"))


def near_grad(part_ref, theirs, payload, *refs):
    chunks, (theirs_ref, mine_ref) = refs[:-2], refs[-2:]
    y_here, core = lax.axis_index("y"), lax.axis_index("core")
    weights = theirs[...]
    steps = (0, 3 + 2 * core, 1 + 2 * core)
    locals_ = [
        local_part(
            part_ref[k] + forward_part(chunk, weights, 1 - core), payload, (y_here + step) % Y
        )
        for k, (step, chunk) in enumerate(zip(steps, chunks))
    ]
    wide = theirs_ref.shape[2]
    for out_ref, half in ((theirs_ref, 1 - core), (mine_ref, core)):
        for y in range(Y):
            total = None
            for local, chunk in zip(locals_, chunks):
                term = grad_part(local, chunk, y, half, wide)
                total = term if total is None else total + term
            out_ref[y] = total


def grad_theirs(begun, mine, theirs, payload, chunk, out_ref, local_ref):
    core = lax.axis_index("core")
    both = forward_part(chunk, mine[...], core) + forward_part(chunk, theirs[...], 1 - core)
    local = local_part(both, payload, (lax.axis_index("y") + 2) % Y)
    local_ref[...] = local
    finish_grad(out_ref, begun, local, chunk, 1 - core)


def grad_mine(begun, local_ref, chunk, out_ref):
    finish_grad(out_ref, begun, local_ref[...], chunk, lax.axis_index("core"))


def combine(mine, theirs, out):
    lanes = mine.shape[-1]
    pairs = out.shape[2] // lanes - 1
    bits = jnp.ceil(jnp.log2(jnp.maximum(mine[PLACES] + theirs[PLACES], 1e-30)))
    scale = jnp.exp2(14.0 - bits)
    for t in range(pairs):
        cut = slice(2 * t, 2 * t + 2)
        out[:, :, t * lanes : (t + 1) * lanes] = (
            mine[:PLACES, cut, :] + theirs[:PLACES, cut, :]
        ) * scale[cut]
    out[:, :, pairs * lanes :] = jnp.broadcast_to(bits[:2], (PLACES, 2, bits.shape[1]))


def join(source, out, which, blocks, sems):
    lanes = source.shape[-1]
    half = out.shape[-1] // 2
    copies = []
    for y in range(Y):
        for pair in range(Y // 2):
            a = source[2 * pair, y].astype(jnp.float32)
            b = source[2 * pair + 1, y].astype(jnp.float32)
            first = lower_half(a)
            blocks[y, :, pair * lanes : (pair + 1) * lanes] = jnp.where(
                first, a, swapped(b)
            ).astype(jnp.bfloat16)
            blocks[y, :, half + pair * lanes : half + (pair + 1) * lanes] = jnp.where(
                first, swapped(a), b
            ).astype(jnp.bfloat16)
        copy = pltpu.make_async_copy(blocks.at[y], out.at[y, which], sems.at[y])
        copy.start()
        copies.append(copy)
    for copy in copies:
        copy.wait()


def join_mine(source, out, blocks, sems):
    join(source, out, lax.axis_index("core"), blocks, sems)


def join_theirs(source, begun, out, blocks, sems):
    join(source, out, 1 - lax.axis_index("core"), blocks, sems)


def shards(
    tokens, hidden_grad, routing, row_count, old_slots, new_slots, master, first_moment, second_moment
):
    y = lax.axis_index("y")
    experts, rows_shard, width = master.shape
    hid = width // 2
    part = hid // Y
    lanes = 2 * part
    f32, bf16 = jnp.float32, jnp.bfloat16
    own = tokens[0, 0]
    rows = own.shape[0]
    half_rows = rows // 2
    hbm = pl.BlockSpec(memory_space=pltpu.MemorySpace.HBM)
    payload = pl.pallas_call(
        prepare,
        out_shape=jax.ShapeDtypeStruct((Y, experts * rows_shard + half_rows, lanes), bf16),
        in_specs=[SMEM, VMEM, VMEM, VMEM],
        out_specs=VMEM,
        name="prepare",
    )(row_count, routing[0, 0], hidden_grad[0, 0], master)
    payload = lax.all_to_all(payload, "y", 0, 0, tiled=True)
    near_one = lax.ppermute(own, ("y", "core"), APART)
    near_two = lax.ppermute(own, ("y", "core"), BACK)
    picked = pl.pallas_call(
        pick_old,
        out_shape=jax.ShapeDtypeStruct((PLACES, Y * rows_shard, lanes), bf16),
        in_specs=[SMEM, VMEM],
        out_specs=pl.BlockSpec(memory_space=pltpu.MemorySpace.HBM),
        scratch_shapes=[
            pltpu.VMEM((experts, Y * rows_shard, lanes), bf16),
            pltpu.VMEM((PLACES, Y * rows_shard, lanes), bf16),
            pltpu.SemaphoreType.DMA(()),
        ],
        compiler_params=grant(4),
        name="pick_old",
    )(old_slots, payload)
    landed = lax.all_to_all(picked, ("x", "z"), 0, 0, tiled=True)
    far = lax.ppermute(near_one, ("y", "core"), APART)

    def by_rows(x):
        return (
            x.reshape(PLACES, Y, rows_shard, lanes)
            .transpose(1, 0, 2, 3)
            .reshape(Y, PLACES * rows_shard, lanes)
        )

    w_mine = landed
    w_theirs = lax.ppermute(w_mine, "core", SWAP)

    near = [own, near_one, near_two]
    forward = pl.pallas_call(
        forward_mine,
        out_shape=jax.ShapeDtypeStruct((len(near), rows, lanes), f32),
        in_specs=[VMEM] * (1 + len(near)),
        out_specs=VMEM,
        compiler_params=grant(24),
        name="forward_mine",
    )(w_mine, *near)
    begun_shape = jax.ShapeDtypeStruct((Y, lanes, PLACES * rows_shard), f32)
    begun_theirs, begun_mine = pl.pallas_call(
        near_grad,
        out_shape=(begun_shape, begun_shape),
        in_specs=[VMEM] * (3 + len(near)),
        out_specs=(VMEM, VMEM),
        compiler_params=grant(24),
        name="near_grad",
    )(forward, w_theirs, payload, *near)
    grad_shape = jax.ShapeDtypeStruct((PLACES + 1, Y * rows_shard, lanes), f32)
    sent, local = pl.pallas_call(
        grad_theirs,
        out_shape=(grad_shape, jax.ShapeDtypeStruct((lanes, rows), bf16)),
        in_specs=[VMEM] * 5,
        out_specs=(VMEM, VMEM),
        compiler_params=grant(24),
        name="grad_theirs",
    )(begun_theirs, w_mine, w_theirs, payload, far)
    received = lax.ppermute(sent, "core", SWAP)
    summed = pl.pallas_call(
        grad_mine,
        out_shape=grad_shape,
        in_specs=[VMEM] * 3,
        out_specs=VMEM,
        compiler_params=grant(24),
        name="grad_mine",
    )(begun_mine, local, far)
    pairs = Y * rows_shard // 2
    scaled = pl.pallas_call(
        combine,
        out_shape=jax.ShapeDtypeStruct((PLACES, 2, (pairs + 1) * lanes), f32),
        in_specs=[VMEM] * 2,
        out_specs=VMEM,
        compiler_params=grant(6),
        name="combine",
    )(summed, received)

    columns = pl.pallas_call(
        split_cols,
        out_shape=jax.ShapeDtypeStruct((Y, 3, experts, rows_shard, lanes), f32),
        in_specs=[VMEM] * 3,
        out_specs=VMEM,
        compiler_params=grant(4),
        name="split_cols",
    )(master, first_moment, second_moment)

    def for_chip(step, x):
        return lax.dynamic_index_in_dim(x, (y + step) % Y, keepdims=False)

    m_low = lax.ppermute(for_chip(1, columns), "y", UP)
    m_high = lax.ppermute(for_chip(3, columns), "y", DOWN)
    m_far = lax.ppermute(for_chip(2, columns), "y", ACROSS)
    m_own = for_chip(0, columns)

    got = lax.all_to_all(scaled.astype(jnp.float16), ("x", "z"), 0, 0, tiled=True)
    got = got.astype(f32)
    select = (old_slots[:, None] == jnp.arange(experts, dtype=jnp.int32)[None, :]).astype(f32)
    per_slot = jnp.sum(row_count.astype(f32), axis=0)
    total = jnp.dot(per_slot, select, precision=lax.Precision.HIGHEST)
    picked, after = pl.pallas_call(
        adam,
        out_shape=(
            jax.ShapeDtypeStruct((PLACES, Y * rows_shard, lanes), bf16),
            jax.ShapeDtypeStruct((Y, 3, experts, rows_shard, lanes), f32),
        ),
        in_specs=[SMEM] * 3 + [VMEM] * 5,
        out_specs=(VMEM, VMEM),
        scratch_shapes=[
            pltpu.VMEM((Y, 3, experts, rows_shard, lanes), f32),
            pltpu.VMEM((experts, 2, pairs * lanes), f32),
            pltpu.VMEM((experts, Y * rows_shard, lanes), bf16),
        ],
        compiler_params=grant(6),
        name="adam",
    )(old_slots, new_slots, total, got, m_own, m_low, m_high, m_far)
    landed = lax.all_to_all(picked, ("x", "z"), 0, 0, tiled=True)

    s_low = lax.ppermute(for_chip(1, after), "y", UP)
    s_high = lax.ppermute(for_chip(3, after), "y", DOWN)
    s_far = lax.ppermute(for_chip(2, after), "y", ACROSS)
    whole = jax.ShapeDtypeStruct((experts, rows_shard, width), f32)
    new_master, new_first, new_second = pl.pallas_call(
        join_cols,
        out_shape=(whole,) * 3,
        in_specs=[VMEM] * 4,
        out_specs=(VMEM,) * 3,
        scratch_shapes=[pltpu.VMEM((Y, 3, experts, rows_shard, lanes), f32)],
        compiler_params=grant(6),
        name="join_cols",
    )(for_chip(0, after), s_low, s_high, s_far)

    landed = by_rows(landed)
    copies = jnp.broadcast_to(landed[None], (Y, *landed.shape))
    mine = lax.all_to_all(copies, "y", 0, 0, tiled=True)
    theirs = lax.ppermute(mine, "core", SWAP)
    block_rows = PLACES * rows_shard
    scratch = [pltpu.VMEM((Y, block_rows, width), bf16), pltpu.SemaphoreType.DMA((Y,))]
    whole = jax.ShapeDtypeStruct((Y, C, block_rows, width), bf16)
    begun = pl.pallas_call(
        join_mine,
        out_shape=whole,
        in_specs=[VMEM],
        out_specs=hbm,
        scratch_shapes=scratch,
        compiler_params=grant(8),
        name="join_mine",
    )(mine)
    new_weights = pl.pallas_call(
        join_theirs,
        out_shape=whole,
        in_specs=[VMEM, hbm],
        out_specs=hbm,
        scratch_shapes=scratch,
        input_output_aliases={1: 0},
        compiler_params=grant(8),
        name="join_theirs",
    )(theirs, begun)
    return (new_weights.reshape(1, -1, width), new_master, new_first, new_second)


def solution(mesh):
    fine = Mesh(mesh.devices.reshape(Y, C, X, Z), ("y", "core", "x", "z"))
    dp, place = ("y", "core"), ("x", "z")
    placed = (
        P(dp, place, None, None),
        P(dp, place, None, None),
        P(dp, place, None, None),
        P(),
        P(),
        P(),
        P(None, dp + place, None),
        P(None, dp + place, None),
        P(None, dp + place, None),
    )

    return jax.shard_map(
        shards,
        mesh=fine,
        in_specs=placed,
        out_specs=(
            P(place, None, None),
            P(None, dp + place, None),
            P(None, dp + place, None),
            P(None, dp + place, None),
        ),
        check_vma=False,
    )
```

```python
import jax
import jax.numpy as jnp
from jax import lax
from jax.experimental import pallas as pl
from jax.experimental.pallas import tpu as pltpu
from jax.sharding import Mesh
from jax.sharding import PartitionSpec as P


decay_first = 0.9
decay_second = 0.95
learn_rate = 0.001
weight_decay = 0.1
epsilon = 1e-08
step_number = 20.0

Y, C, X, Z = 4, 2, 4, 16
PLACES = X * Z
UP = [(i, (i + 1) % Y) for i in range(Y)]
DOWN = [(i, (i - 1) % Y) for i in range(Y)]
ACROSS = [(i, (i + 2) % Y) for i in range(Y)]
SWAP = [(0, 1), (1, 0)]
APART = [(i * C + c, (i + 1 - 2 * c) % Y * C + c) for i in range(Y) for c in range(C)]
BACK = [(t, s) for s, t in APART]
VMEM = pl.BlockSpec(memory_space=pltpu.VMEM)
SMEM = pl.BlockSpec(memory_space=pltpu.SMEM)
ANY = pl.BlockSpec(memory_space=pl.ANY)


def grant(mib):
    return pltpu.CompilerParams(vmem_limit_bytes=mib << 20)


def lower_half(x):
    return lax.broadcasted_iota(jnp.int32, x.shape, x.ndim - 1) < x.shape[-1] // 2


def swapped(x):
    return pltpu.roll(x, x.shape[-1] // 2, x.ndim - 1)


def split_cols(*refs):
    ins, out = refs[:-1], refs[-1]
    lanes = out.shape[-1]
    half = ins[0].shape[-1] // 2
    for n, x in enumerate(ins):
        for pair in range(Y // 2):
            gate = x[:, :, pair * lanes : (pair + 1) * lanes]
            up = x[:, :, half + pair * lanes : half + (pair + 1) * lanes]
            low = lower_half(gate)
            out[2 * pair, n] = jnp.where(low, gate, swapped(up))
            out[2 * pair + 1, n] = jnp.where(low, swapped(gate), up)


def join_cols(own, low, high, far, *refs):
    outs, parts = refs[:-1], refs[-1]
    y = lax.axis_index("y")
    parts[y] = own[...]
    parts[(y + 3) % Y] = low[...]
    parts[(y + 1) % Y] = high[...]
    parts[(y + 2) % Y] = far[...]
    lanes = own.shape[-1]
    half = outs[0].shape[-1] // 2
    for n, out in enumerate(outs):
        for pair in range(Y // 2):
            a, b = parts[2 * pair, n], parts[2 * pair + 1, n]
            first = lower_half(a)
            out[:, :, pair * lanes : (pair + 1) * lanes] = jnp.where(first, a, swapped(b))
            out[:, :, half + pair * lanes : half + (pair + 1) * lanes] = jnp.where(
                first, swapped(a), b
            )


def prepare(counts, order, hidden, master, out):
    batches, batch_rows = order.shape
    experts, rows_shard, width = master.shape
    lanes = out.shape[-1]
    half = width // 2
    group_here = lax.axis_index("y") * C + lax.axis_index("core")
    count = counts[group_here, lax.axis_index("x") * Z + lax.axis_index("z")]
    blocks = []
    for m in range(batches):
        at = m * batch_rows
        slot = lax.broadcasted_iota(jnp.int32, (batch_rows, hidden.shape[1]), 0) + at
        live = jnp.where(slot < count, hidden[at : at + batch_rows, :].astype(jnp.float32), 0.0)
        row = lax.broadcasted_iota(jnp.int32, (batch_rows, batch_rows), 0)
        moves = (jnp.broadcast_to(order[m : m + 1, :], row.shape) == row).astype(jnp.bfloat16)
        blocks.append(
            jnp.dot(moves, live.astype(jnp.bfloat16), preferred_element_type=jnp.float32)
        )
    upper = jnp.concatenate(blocks[: batches // 2], axis=0)
    lower = jnp.concatenate(blocks[batches // 2 :], axis=0)
    weights = experts * rows_shard
    for pair in range(Y // 2):
        cut = slice(pair * lanes, (pair + 1) * lanes)
        first = lower_half(upper[:, cut])
        out[2 * pair, weights:, :] = jnp.where(
            first, upper[:, cut], swapped(lower[:, cut])
        ).astype(jnp.bfloat16)
        out[2 * pair + 1, weights:, :] = jnp.where(
            first, swapped(upper[:, cut]), lower[:, cut]
        ).astype(jnp.bfloat16)
        gate = jnp.concatenate([master[e, :, cut] for e in range(experts)], axis=0)
        up_cut = slice(half + pair * lanes, half + (pair + 1) * lanes)
        up = jnp.concatenate([master[e, :, up_cut] for e in range(experts)], axis=0)
        first = lower_half(gate)
        out[2 * pair, :weights, :] = jnp.where(first, gate, swapped(up)).astype(jnp.bfloat16)
        out[2 * pair + 1, :weights, :] = jnp.where(first, swapped(gate), up).astype(jnp.bfloat16)


def pick_old(slots, payload, out, table, picked, sem):
    experts, rows, _ = table.shape
    rows_shard = rows // Y
    parts = [payload[y, : experts * rows_shard, :].astype(jnp.float32) for y in range(Y)]
    for e in range(experts):
        table[e] = jnp.concatenate(
            [part[e * rows_shard : (e + 1) * rows_shard] for part in parts], axis=0
        ).astype(jnp.bfloat16)
    for p in range(PLACES):
        picked[p] = table[slots[p]]
    copy = pltpu.make_async_copy(picked, out, sem)
    copy.start()
    copy.wait()


def adam(old, new, total, got, own, low, high, far, out, after, state, acc, table):
    experts, _, data = acc.shape
    rows, lanes = state.shape[3:]
    y_here = lax.axis_index("y")
    state[y_here] = own[...]
    state[(y_here + 3) % Y] = low[...]
    state[(y_here + 1) % Y] = high[...]
    state[(y_here + 2) % Y] = far[...]
    acc[...] = jnp.zeros_like(acc)
    for p in range(PLACES):
        undo = jnp.exp2(got[p, :, data:] - 14.0)
        acc[old[p]] += got[p, :, :data] * jnp.concatenate([undo] * (data // lanes), axis=1)
    for e in range(experts):
        master, first, second = (
            jnp.concatenate([state[y, n, e] for y in range(Y)], axis=0) for n in range(3)
        )
        grad = jnp.concatenate(
            [acc[e, :, at : at + lanes] for at in range(0, data, lanes)], axis=0
        )
        grad = grad / total[e]
        new_first = decay_first * first + (1.0 - decay_first) * grad
        new_second = decay_second * second + (1.0 - decay_second) * grad * grad
        first_hat = new_first / (1.0 - decay_first**step_number)
        second_hat = new_second / (1.0 - decay_second**step_number)
        new_master = master - learn_rate * (
            first_hat / (jnp.sqrt(second_hat) + epsilon) + weight_decay * master
        )
        table[e] = new_master.astype(jnp.bfloat16)
        for n, value in enumerate((new_master, new_first, new_second)):
            for y in range(Y):
                after[y, n, e] = value[y * rows : (y + 1) * rows]
    for p in range(PLACES):
        out[p % Z * X + p // Z] = table[new[p]]


def forward_part(chunk, weights, which):
    rows_shard = weights.shape[1] // Y
    wide = PLACES * rows_shard
    total = None
    for y in range(Y):
        at = pl.multiple_of((2 * y + which) * wide, wide)
        block = weights[:, y * rows_shard : (y + 1) * rows_shard, :].astype(jnp.float32)
        term = jnp.dot(
            chunk[:, pl.ds(at, wide)],
            block.reshape(wide, -1).astype(jnp.bfloat16),
            preferred_element_type=jnp.float32,
        )
        total = term if total is None else total + term
    return total


def local_part(both, payload, source):
    packed = both.shape[0] // 2
    other = swapped(both)
    first = lower_half(both)
    gate = jnp.where(first, both, other)
    sigma = jax.nn.sigmoid(gate)
    active = gate * sigma
    slope = sigma * (1.0 + gate * (1.0 - sigma))
    hidden = payload[source, payload.shape[1] - packed :, :].astype(jnp.float32)
    around = swapped(hidden)
    begin = lower_half(hidden)
    incoming = jnp.concatenate(
        [jnp.where(begin, hidden, around), jnp.where(begin, around, hidden)], axis=0
    )
    local = jnp.where(first, incoming * other * slope, incoming * active)
    return local.T.astype(jnp.bfloat16)


def grad_part(local, chunk, y, half, wide):
    at = pl.multiple_of((2 * y + half) * wide, wide)
    return jnp.dot(local, chunk[:, pl.ds(at, wide)], preferred_element_type=jnp.float32)


def finish_grad(out_ref, begun, local, chunk, half):
    rows_shard = out_ref.shape[1] // Y
    wide = PLACES * rows_shard
    peak = None
    for y in range(Y):
        total = begun[y] + grad_part(local, chunk, y, half, wide)
        size = jnp.abs(total)
        peak = size if peak is None else jnp.maximum(peak, size)
        out_ref[:PLACES, y * rows_shard : (y + 1) * rows_shard, :] = total.T.reshape(
            PLACES, rows_shard, -1
        )
    out_ref[PLACES] = jnp.broadcast_to(jnp.max(peak, keepdims=True), out_ref.shape[1:])


def forward_mine(mine, *refs):
    chunks, out_ref = refs[:-1], refs[-1]
    weights = mine[...]
    for k, chunk in enumerate(chunks):
        out_ref[k] = forward_part(chunk, weights, lax.axis_index("core"))


def near_grad(part_ref, theirs, payload, *refs):
    chunks, (theirs_ref, mine_ref) = refs[:-2], refs[-2:]
    y_here, core = lax.axis_index("y"), lax.axis_index("core")
    weights = theirs[...]
    steps = (0, 3 + 2 * core, 1 + 2 * core)
    locals_ = [
        local_part(
            part_ref[k] + forward_part(chunk, weights, 1 - core), payload, (y_here + step) % Y
        )
        for k, (step, chunk) in enumerate(zip(steps, chunks))
    ]
    wide = theirs_ref.shape[2]
    for out_ref, half in ((theirs_ref, 1 - core), (mine_ref, core)):
        for y in range(Y):
            total = None
            for local, chunk in zip(locals_, chunks):
                term = grad_part(local, chunk, y, half, wide)
                total = term if total is None else total + term
            out_ref[y] = total


def grad_theirs(begun, mine, theirs, payload, chunk, out_ref, local_ref):
    core = lax.axis_index("core")
    both = forward_part(chunk, mine[...], core) + forward_part(chunk, theirs[...], 1 - core)
    local = local_part(both, payload, (lax.axis_index("y") + 2) % Y)
    local_ref[...] = local
    finish_grad(out_ref, begun, local, chunk, 1 - core)


def grad_mine(begun, local_ref, chunk, out_ref):
    finish_grad(out_ref, begun, local_ref[...], chunk, lax.axis_index("core"))


def combine(mine, theirs, out):
    lanes = mine.shape[-1]
    pairs = out.shape[2] // lanes - 1
    bits = jnp.ceil(jnp.log2(jnp.maximum(mine[PLACES] + theirs[PLACES], 1e-30)))
    scale = jnp.exp2(14.0 - bits)
    for t in range(pairs):
        cut = slice(2 * t, 2 * t + 2)
        out[:, :, t * lanes : (t + 1) * lanes] = (
            mine[:PLACES, cut, :] + theirs[:PLACES, cut, :]
        ) * scale[cut]
    out[:, :, pairs * lanes :] = jnp.broadcast_to(bits[:2], (PLACES, 2, bits.shape[1]))


def join(source, out, which, blocks, sems):
    rows, lanes = source.shape[3:]
    half = out.shape[-1] // 2
    copies = []
    for y in range(Y):
        for x in range(X):
            at = slice(x * rows, (x + 1) * rows)
            for pair in range(Y // 2):
                a = source[2 * pair, x, y].astype(jnp.float32)
                b = source[2 * pair + 1, x, y].astype(jnp.float32)
                first = lower_half(a)
                blocks[y, at, pair * lanes : (pair + 1) * lanes] = jnp.where(
                    first, a, swapped(b)
                ).astype(jnp.bfloat16)
                blocks[y, at, half + pair * lanes : half + (pair + 1) * lanes] = jnp.where(
                    first, swapped(a), b
                ).astype(jnp.bfloat16)
        copy = pltpu.make_async_copy(blocks.at[y], out.at[y, which], sems.at[y])
        copy.start()
        copies.append(copy)
    for copy in copies:
        copy.wait()


def join_mine(source, out, blocks, sems):
    join(source, out, lax.axis_index("core"), blocks, sems)


def join_theirs(source, begun, out, blocks, sems):
    join(source, out, 1 - lax.axis_index("core"), blocks, sems)


def shards(
    tokens, hidden_grad, routing, row_count, old_slots, new_slots, master, first_moment, second_moment
):
    y = lax.axis_index("y")
    experts, rows_shard, width = master.shape
    hid = width // 2
    part = hid // Y
    lanes = 2 * part
    f32, bf16 = jnp.float32, jnp.bfloat16
    own = tokens[0, 0]
    rows = own.shape[0]
    half_rows = rows // 2
    hbm = pl.BlockSpec(memory_space=pltpu.MemorySpace.HBM)
    payload = pl.pallas_call(
        prepare,
        out_shape=jax.ShapeDtypeStruct((Y, experts * rows_shard + half_rows, lanes), bf16),
        in_specs=[SMEM, VMEM, VMEM, VMEM],
        out_specs=VMEM,
        name="prepare",
    )(row_count, routing[0, 0], hidden_grad[0, 0], master)
    payload = lax.all_to_all(payload, "y", 0, 0, tiled=True)
    near_one = lax.ppermute(own, ("y", "core"), APART)
    near_two = lax.ppermute(own, ("y", "core"), BACK)
    picked = pl.pallas_call(
        pick_old,
        out_shape=jax.ShapeDtypeStruct((PLACES, Y * rows_shard, lanes), bf16),
        in_specs=[SMEM, VMEM],
        out_specs=pl.BlockSpec(memory_space=pltpu.MemorySpace.HBM),
        scratch_shapes=[
            pltpu.VMEM((experts, Y * rows_shard, lanes), bf16),
            pltpu.VMEM((PLACES, Y * rows_shard, lanes), bf16),
            pltpu.SemaphoreType.DMA(()),
        ],
        compiler_params=grant(4),
        name="pick_old",
    )(old_slots, payload)
    landed = lax.all_to_all(picked, ("x", "z"), 0, 0, tiled=True)
    far = lax.ppermute(near_one, ("y", "core"), APART)

    w_mine = landed
    w_theirs = lax.ppermute(w_mine, "core", SWAP)

    near = [own, near_one, near_two]
    forward = pl.pallas_call(
        forward_mine,
        out_shape=jax.ShapeDtypeStruct((len(near), rows, lanes), f32),
        in_specs=[VMEM] * (1 + len(near)),
        out_specs=VMEM,
        compiler_params=grant(24),
        name="forward_mine",
    )(w_mine, *near)
    begun_shape = jax.ShapeDtypeStruct((Y, lanes, PLACES * rows_shard), f32)
    begun_theirs, begun_mine = pl.pallas_call(
        near_grad,
        out_shape=(begun_shape, begun_shape),
        in_specs=[VMEM] * (3 + len(near)),
        out_specs=(VMEM, VMEM),
        compiler_params=grant(24),
        name="near_grad",
    )(forward, w_theirs, payload, *near)
    grad_shape = jax.ShapeDtypeStruct((PLACES + 1, Y * rows_shard, lanes), f32)
    sent, local = pl.pallas_call(
        grad_theirs,
        out_shape=(grad_shape, jax.ShapeDtypeStruct((lanes, rows), bf16)),
        in_specs=[VMEM] * 5,
        out_specs=(VMEM, VMEM),
        compiler_params=grant(24),
        name="grad_theirs",
    )(begun_theirs, w_mine, w_theirs, payload, far)
    received = lax.ppermute(sent, "core", SWAP)
    summed = pl.pallas_call(
        grad_mine,
        out_shape=grad_shape,
        in_specs=[VMEM] * 3,
        out_specs=VMEM,
        compiler_params=grant(24),
        name="grad_mine",
    )(begun_mine, local, far)
    pairs = Y * rows_shard // 2
    scaled = pl.pallas_call(
        combine,
        out_shape=jax.ShapeDtypeStruct((PLACES, 2, (pairs + 1) * lanes), f32),
        in_specs=[VMEM] * 2,
        out_specs=VMEM,
        compiler_params=grant(6),
        name="combine",
    )(summed, received)

    columns = pl.pallas_call(
        split_cols,
        out_shape=jax.ShapeDtypeStruct((Y, 3, experts, rows_shard, lanes), f32),
        in_specs=[VMEM] * 3,
        out_specs=VMEM,
        compiler_params=grant(4),
        name="split_cols",
    )(master, first_moment, second_moment)

    def for_chip(step, x):
        return lax.dynamic_index_in_dim(x, (y + step) % Y, keepdims=False)

    m_low = lax.ppermute(for_chip(1, columns), "y", UP)
    m_high = lax.ppermute(for_chip(3, columns), "y", DOWN)
    m_far = lax.ppermute(for_chip(2, columns), "y", ACROSS)
    m_own = for_chip(0, columns)

    got = lax.all_to_all(scaled.astype(jnp.float16), ("x", "z"), 0, 0, tiled=True)
    got = got.astype(f32)
    select = (old_slots[:, None] == jnp.arange(experts, dtype=jnp.int32)[None, :]).astype(f32)
    per_slot = jnp.sum(row_count.astype(f32), axis=0)
    total = jnp.dot(per_slot, select, precision=lax.Precision.HIGHEST)
    picked, after = pl.pallas_call(
        adam,
        out_shape=(
            jax.ShapeDtypeStruct((PLACES, Y * rows_shard, lanes), bf16),
            jax.ShapeDtypeStruct((Y, 3, experts, rows_shard, lanes), f32),
        ),
        in_specs=[SMEM] * 3 + [VMEM] * 5,
        out_specs=(VMEM, VMEM),
        scratch_shapes=[
            pltpu.VMEM((Y, 3, experts, rows_shard, lanes), f32),
            pltpu.VMEM((experts, 2, pairs * lanes), f32),
            pltpu.VMEM((experts, Y * rows_shard, lanes), bf16),
        ],
        compiler_params=grant(6),
        name="adam",
    )(old_slots, new_slots, total, got, m_own, m_low, m_high, m_far)
    block_rows = PLACES * rows_shard
    landed = lax.all_to_all(
        picked.reshape(Z, X * Y * rows_shard, lanes), "z", 0, 0, tiled=True
    )

    s_low = lax.ppermute(for_chip(1, after), "y", UP)
    s_high = lax.ppermute(for_chip(3, after), "y", DOWN)
    s_far = lax.ppermute(for_chip(2, after), "y", ACROSS)
    whole = jax.ShapeDtypeStruct((experts, rows_shard, width), f32)
    new_master, new_first, new_second = pl.pallas_call(
        join_cols,
        out_shape=(whole,) * 3,
        in_specs=[VMEM] * 4,
        out_specs=(VMEM,) * 3,
        scratch_shapes=[pltpu.VMEM((Y, 3, experts, rows_shard, lanes), f32)],
        compiler_params=grant(6),
        name="join_cols",
    )(for_chip(0, after), s_low, s_high, s_far)

    landed = (
        landed.reshape(Z, X, Y, rows_shard, lanes)
        .transpose(1, 2, 0, 3, 4)
        .reshape(X, Y * Z * rows_shard, lanes)
    )
    copies = jnp.broadcast_to(landed[None], (Y, *landed.shape))
    mine = lax.all_to_all(
        copies.reshape(Y * X, Y * Z * rows_shard, lanes), ("y", "x"), 0, 0, tiled=True
    ).reshape(Y, X, Y, Z * rows_shard, lanes)
    theirs = lax.ppermute(mine, "core", SWAP)
    scratch = [pltpu.VMEM((Y, block_rows, width), bf16), pltpu.SemaphoreType.DMA((Y,))]
    whole = jax.ShapeDtypeStruct((Y, C, block_rows, width), bf16)
    begun = pl.pallas_call(
        join_mine,
        out_shape=whole,
        in_specs=[VMEM],
        out_specs=hbm,
        scratch_shapes=scratch,
        compiler_params=grant(8),
        name="join_mine",
    )(mine)
    new_weights = pl.pallas_call(
        join_theirs,
        out_shape=whole,
        in_specs=[VMEM, hbm],
        out_specs=hbm,
        scratch_shapes=scratch,
        input_output_aliases={1: 0},
        compiler_params=grant(8),
        name="join_theirs",
    )(theirs, begun)
    return (new_weights.reshape(1, -1, width), new_master, new_first, new_second)


def solution(mesh):
    fine = Mesh(mesh.devices.reshape(Y, C, X, Z), ("y", "core", "x", "z"))
    dp, place = ("y", "core"), ("x", "z")
    placed = (
        P(dp, place, None, None),
        P(dp, place, None, None),
        P(dp, place, None, None),
        P(),
        P(),
        P(),
        P(None, dp + place, None),
        P(None, dp + place, None),
        P(None, dp + place, None),
    )

    return jax.shard_map(
        shards,
        mesh=fine,
        in_specs=placed,
        out_specs=(
            P(place, None, None),
            P(None, dp + place, None),
            P(None, dp + place, None),
            P(None, dp + place, None),
        ),
        check_vma=False,
    )
```

```python
import jax
import jax.numpy as jnp
from jax import lax
from jax.experimental import pallas as pl
from jax.experimental.pallas import tpu as pltpu
from jax.sharding import Mesh
from jax.sharding import PartitionSpec as P


decay_first = 0.9
decay_second = 0.95
learn_rate = 0.001
weight_decay = 0.1
epsilon = 1e-08
step_number = 20.0

Y, C, X, Z = 4, 2, 4, 16
PLACES = X * Z
UP = [(i, (i + 1) % Y) for i in range(Y)]
DOWN = [(i, (i - 1) % Y) for i in range(Y)]
ACROSS = [(i, (i + 2) % Y) for i in range(Y)]
SWAP = [(0, 1), (1, 0)]
APART = [(i * C + c, (i + 1 - 2 * c) % Y * C + c) for i in range(Y) for c in range(C)]
BACK = [(t, s) for s, t in APART]
VMEM = pl.BlockSpec(memory_space=pltpu.VMEM)
SMEM = pl.BlockSpec(memory_space=pltpu.SMEM)
ANY = pl.BlockSpec(memory_space=pl.ANY)


def grant(mib):
    return pltpu.CompilerParams(vmem_limit_bytes=mib << 20)


def lower_half(x):
    return lax.broadcasted_iota(jnp.int32, x.shape, x.ndim - 1) < x.shape[-1] // 2


def swapped(x):
    return pltpu.roll(x, x.shape[-1] // 2, x.ndim - 1)


def split_cols(*refs):
    ins, out = refs[:-1], refs[-1]
    lanes = out.shape[-1]
    half = ins[0].shape[-1] // 2
    for n, x in enumerate(ins):
        for pair in range(Y // 2):
            gate = x[:, :, pair * lanes : (pair + 1) * lanes]
            up = x[:, :, half + pair * lanes : half + (pair + 1) * lanes]
            low = lower_half(gate)
            out[2 * pair, n] = jnp.where(low, gate, swapped(up))
            out[2 * pair + 1, n] = jnp.where(low, swapped(gate), up)


def join_cols(own, low, high, far, *refs):
    outs, parts = refs[:-1], refs[-1]
    y = lax.axis_index("y")
    parts[y] = own[...]
    parts[(y + 3) % Y] = low[...]
    parts[(y + 1) % Y] = high[...]
    parts[(y + 2) % Y] = far[...]
    lanes = own.shape[-1]
    half = outs[0].shape[-1] // 2
    for n, out in enumerate(outs):
        for pair in range(Y // 2):
            a, b = parts[2 * pair, n], parts[2 * pair + 1, n]
            first = lower_half(a)
            out[:, :, pair * lanes : (pair + 1) * lanes] = jnp.where(first, a, swapped(b))
            out[:, :, half + pair * lanes : half + (pair + 1) * lanes] = jnp.where(
                first, swapped(a), b
            )


def prepare(counts, order, hidden, master, out):
    batches, batch_rows = order.shape
    experts, rows_shard, width = master.shape
    lanes = out.shape[-1]
    half = width // 2
    group_here = lax.axis_index("y") * C + lax.axis_index("core")
    count = counts[group_here, lax.axis_index("x") * Z + lax.axis_index("z")]
    blocks = []
    for m in range(batches):
        at = m * batch_rows
        slot = lax.broadcasted_iota(jnp.int32, (batch_rows, hidden.shape[1]), 0) + at
        live = jnp.where(slot < count, hidden[at : at + batch_rows, :].astype(jnp.float32), 0.0)
        row = lax.broadcasted_iota(jnp.int32, (batch_rows, batch_rows), 0)
        moves = (jnp.broadcast_to(order[m : m + 1, :], row.shape) == row).astype(jnp.bfloat16)
        blocks.append(
            jnp.dot(moves, live.astype(jnp.bfloat16), preferred_element_type=jnp.float32)
        )
    upper = jnp.concatenate(blocks[: batches // 2], axis=0)
    lower = jnp.concatenate(blocks[batches // 2 :], axis=0)
    weights = experts * rows_shard
    for pair in range(Y // 2):
        cut = slice(pair * lanes, (pair + 1) * lanes)
        first = lower_half(upper[:, cut])
        out[2 * pair, weights:, :] = jnp.where(
            first, upper[:, cut], swapped(lower[:, cut])
        ).astype(jnp.bfloat16)
        out[2 * pair + 1, weights:, :] = jnp.where(
            first, swapped(upper[:, cut]), lower[:, cut]
        ).astype(jnp.bfloat16)
        gate = jnp.concatenate([master[e, :, cut] for e in range(experts)], axis=0)
        up_cut = slice(half + pair * lanes, half + (pair + 1) * lanes)
        up = jnp.concatenate([master[e, :, up_cut] for e in range(experts)], axis=0)
        first = lower_half(gate)
        out[2 * pair, :weights, :] = jnp.where(first, gate, swapped(up)).astype(jnp.bfloat16)
        out[2 * pair + 1, :weights, :] = jnp.where(first, swapped(gate), up).astype(jnp.bfloat16)


def pick_old(slots, payload, out, table, picked, sem):
    experts, rows, _ = table.shape
    rows_shard = rows // Y
    parts = [payload[y, : experts * rows_shard, :].astype(jnp.float32) for y in range(Y)]
    for e in range(experts):
        table[e] = jnp.concatenate(
            [part[e * rows_shard : (e + 1) * rows_shard] for part in parts], axis=0
        ).astype(jnp.bfloat16)
    for p in range(PLACES):
        picked[p] = table[slots[p]]
    copy = pltpu.make_async_copy(picked, out, sem)
    copy.start()
    copy.wait()


def adam(old, new, total, got, own, low, high, far, out, after, state, acc, table):
    experts, _, data = acc.shape
    rows, lanes = state.shape[3:]
    y_here = lax.axis_index("y")
    state[y_here] = own[...]
    state[(y_here + 3) % Y] = low[...]
    state[(y_here + 1) % Y] = high[...]
    state[(y_here + 2) % Y] = far[...]
    acc[...] = jnp.zeros_like(acc)
    for p in range(PLACES):
        undo = jnp.exp2(got[p, :, data:] - 14.0)
        acc[old[p]] += got[p, :, :data] * jnp.concatenate([undo] * (data // lanes), axis=1)
    for e in range(experts):
        master, first, second = (
            jnp.concatenate([state[y, n, e] for y in range(Y)], axis=0) for n in range(3)
        )
        grad = jnp.concatenate(
            [acc[e, :, at : at + lanes] for at in range(0, data, lanes)], axis=0
        )
        grad = grad / total[e]
        new_first = decay_first * first + (1.0 - decay_first) * grad
        new_second = decay_second * second + (1.0 - decay_second) * grad * grad
        first_hat = new_first / (1.0 - decay_first**step_number)
        second_hat = new_second / (1.0 - decay_second**step_number)
        new_master = master - learn_rate * (
            first_hat / (jnp.sqrt(second_hat) + epsilon) + weight_decay * master
        )
        table[e] = new_master.astype(jnp.bfloat16)
        for n, value in enumerate((new_master, new_first, new_second)):
            for y in range(Y):
                after[y, n, e] = value[y * rows : (y + 1) * rows]
    for p in range(PLACES):
        out[p % Z * X + p // Z] = table[new[p]]


def natural(weights):
    rows_shard = weights.shape[1] // Y
    wide = weights[...].astype(jnp.float32)
    return [
        wide[:, y * rows_shard : (y + 1) * rows_shard, :]
        .reshape(PLACES * rows_shard, -1)
        .astype(jnp.bfloat16)
        for y in range(Y)
    ]


def forward_part(chunk, weights, which):
    wide = weights.shape[1]
    total = None
    for y in range(Y):
        at = pl.multiple_of((2 * y + which) * wide, wide)
        term = jnp.dot(chunk[:, pl.ds(at, wide)], weights[y], preferred_element_type=jnp.float32)
        total = term if total is None else total + term
    return total


def local_part(both, payload, source):
    packed = both.shape[0] // 2
    other = swapped(both)
    first = lower_half(both)
    gate = jnp.where(first, both, other)
    sigma = jax.nn.sigmoid(gate)
    active = gate * sigma
    slope = sigma * (1.0 + gate * (1.0 - sigma))
    hidden = payload[source, payload.shape[1] - packed :, :].astype(jnp.float32)
    around = swapped(hidden)
    begin = lower_half(hidden)
    incoming = jnp.concatenate(
        [jnp.where(begin, hidden, around), jnp.where(begin, around, hidden)], axis=0
    )
    local = jnp.where(first, incoming * other * slope, incoming * active)
    return local.T.astype(jnp.bfloat16)


def grad_part(local, chunk, y, half, wide):
    at = pl.multiple_of((2 * y + half) * wide, wide)
    return jnp.dot(local, chunk[:, pl.ds(at, wide)], preferred_element_type=jnp.float32)


def finish_grad(out_ref, begun, local, chunk, half):
    rows_shard = out_ref.shape[1] // Y
    wide = PLACES * rows_shard
    peak = None
    for y in range(Y):
        total = begun[y] + grad_part(local, chunk, y, half, wide)
        size = jnp.abs(total)
        peak = size if peak is None else jnp.maximum(peak, size)
        out_ref[:PLACES, y * rows_shard : (y + 1) * rows_shard, :] = total.T.reshape(
            PLACES, rows_shard, -1
        )
    out_ref[PLACES] = jnp.broadcast_to(jnp.max(peak, keepdims=True), out_ref.shape[1:])


def forward_mine(mine, own, one, two, out_ref, weights_ref, held, sem):
    copy = pltpu.make_async_copy(two, held, sem)
    copy.start()
    for y, block in enumerate(natural(mine)):
        weights_ref[y] = block
    core = lax.axis_index("core")
    out_ref[0] = forward_part(own, weights_ref, core)
    out_ref[1] = forward_part(one, weights_ref, core)
    copy.wait()
    out_ref[2] = forward_part(held, weights_ref, core)


def near_grad(part_ref, theirs, payload, own, one, two, theirs_ref, mine_ref, weights_ref, held, sem):
    copy = pltpu.make_async_copy(two, held, sem)
    copy.start()
    for y, block in enumerate(natural(theirs)):
        weights_ref[y] = block
    y_here, core = lax.axis_index("y"), lax.axis_index("core")
    chunks = (own, one, held)
    steps = (0, 3 + 2 * core, 1 + 2 * core)
    locals_ = []
    for k, (step, chunk) in enumerate(zip(steps, chunks)):
        if k == 2:
            copy.wait()
        both = part_ref[k] + forward_part(chunk, weights_ref, 1 - core)
        locals_.append(local_part(both, payload, (y_here + step) % Y))
    wide = theirs_ref.shape[2]
    for out_ref, half in ((theirs_ref, 1 - core), (mine_ref, core)):
        for y in range(Y):
            total = None
            for local, chunk in zip(locals_, chunks):
                term = grad_part(local, chunk, y, half, wide)
                total = term if total is None else total + term
            out_ref[y] = total


def grad_theirs(begun, mine, theirs, payload, chunk, out_ref, local_ref):
    core = lax.axis_index("core")
    both = forward_part(chunk, mine, core) + forward_part(chunk, theirs, 1 - core)
    local = local_part(both, payload, (lax.axis_index("y") + 2) % Y)
    local_ref[...] = local
    finish_grad(out_ref, begun, local, chunk, 1 - core)


def grad_mine(begun, local_ref, chunk, out_ref):
    finish_grad(out_ref, begun, local_ref[...], chunk, lax.axis_index("core"))


def combine(mine, theirs, out):
    lanes = mine.shape[-1]
    pairs = out.shape[2] // lanes - 1
    bits = jnp.ceil(jnp.log2(jnp.maximum(mine[PLACES] + theirs[PLACES], 1e-30)))
    scale = jnp.exp2(14.0 - bits)
    for t in range(pairs):
        cut = slice(2 * t, 2 * t + 2)
        out[:, :, t * lanes : (t + 1) * lanes] = (
            mine[:PLACES, cut, :] + theirs[:PLACES, cut, :]
        ) * scale[cut]
    out[:, :, pairs * lanes :] = jnp.broadcast_to(bits[:2], (PLACES, 2, bits.shape[1]))


def join(source, out, which, blocks, sems):
    rows, lanes = source.shape[3:]
    half = out.shape[-1] // 2
    copies = []
    for y in range(Y):
        for x in range(X):
            at = slice(x * rows, (x + 1) * rows)
            for pair in range(Y // 2):
                a = source[2 * pair, x, y].astype(jnp.float32)
                b = source[2 * pair + 1, x, y].astype(jnp.float32)
                first = lower_half(a)
                blocks[y, at, pair * lanes : (pair + 1) * lanes] = jnp.where(
                    first, a, swapped(b)
                ).astype(jnp.bfloat16)
                blocks[y, at, half + pair * lanes : half + (pair + 1) * lanes] = jnp.where(
                    first, swapped(a), b
                ).astype(jnp.bfloat16)
        copy = pltpu.make_async_copy(blocks.at[y], out.at[y, which], sems.at[y])
        copy.start()
        copies.append(copy)
    for copy in copies:
        copy.wait()


def join_mine(source, out, blocks, sems):
    join(source, out, lax.axis_index("core"), blocks, sems)


def join_theirs(source, begun, out, blocks, sems):
    join(source, out, 1 - lax.axis_index("core"), blocks, sems)


def shards(
    tokens, hidden_grad, routing, row_count, old_slots, new_slots, master, first_moment, second_moment
):
    y = lax.axis_index("y")
    experts, rows_shard, width = master.shape
    hid = width // 2
    part = hid // Y
    lanes = 2 * part
    f32, bf16 = jnp.float32, jnp.bfloat16
    own = tokens[0, 0]
    rows = own.shape[0]
    half_rows = rows // 2
    hbm = pl.BlockSpec(memory_space=pltpu.MemorySpace.HBM)
    payload = pl.pallas_call(
        prepare,
        out_shape=jax.ShapeDtypeStruct((Y, experts * rows_shard + half_rows, lanes), bf16),
        in_specs=[SMEM, VMEM, VMEM, VMEM],
        out_specs=VMEM,
        name="prepare",
    )(row_count, routing[0, 0], hidden_grad[0, 0], master)
    payload = lax.all_to_all(payload, "y", 0, 0, tiled=True)
    near_one = lax.ppermute(own, ("y", "core"), APART)
    near_two = lax.ppermute(own, ("y", "core"), BACK)
    picked = pl.pallas_call(
        pick_old,
        out_shape=jax.ShapeDtypeStruct((PLACES, Y * rows_shard, lanes), bf16),
        in_specs=[SMEM, VMEM],
        out_specs=pl.BlockSpec(memory_space=pltpu.MemorySpace.HBM),
        scratch_shapes=[
            pltpu.VMEM((experts, Y * rows_shard, lanes), bf16),
            pltpu.VMEM((PLACES, Y * rows_shard, lanes), bf16),
            pltpu.SemaphoreType.DMA(()),
        ],
        compiler_params=grant(4),
        name="pick_old",
    )(old_slots, payload)
    landed = lax.all_to_all(picked, ("x", "z"), 0, 0, tiled=True)
    far = lax.ppermute(near_one, ("y", "core"), APART)

    w_mine = landed
    w_theirs = lax.ppermute(w_mine, "core", SWAP)

    wide = PLACES * rows_shard
    weights_shape = jax.ShapeDtypeStruct((Y, wide, lanes), bf16)
    held = [pltpu.VMEM(own.shape, bf16), pltpu.SemaphoreType.DMA(())]
    forward, w_mine = pl.pallas_call(
        forward_mine,
        out_shape=(jax.ShapeDtypeStruct((3, rows, lanes), f32), weights_shape),
        in_specs=[VMEM] * 3 + [ANY],
        out_specs=(VMEM, VMEM),
        scratch_shapes=held,
        compiler_params=grant(24),
        name="forward_mine",
    )(w_mine, own, near_one, near_two)
    begun_shape = jax.ShapeDtypeStruct((Y, lanes, wide), f32)
    begun_theirs, begun_mine, w_theirs = pl.pallas_call(
        near_grad,
        out_shape=(begun_shape, begun_shape, weights_shape),
        in_specs=[VMEM] * 5 + [ANY],
        out_specs=(VMEM, VMEM, VMEM),
        scratch_shapes=held,
        compiler_params=grant(24),
        name="near_grad",
    )(forward, w_theirs, payload, own, near_one, near_two)
    grad_shape = jax.ShapeDtypeStruct((PLACES + 1, Y * rows_shard, lanes), f32)
    sent, local = pl.pallas_call(
        grad_theirs,
        out_shape=(grad_shape, jax.ShapeDtypeStruct((lanes, rows), bf16)),
        in_specs=[VMEM] * 5,
        out_specs=(VMEM, VMEM),
        compiler_params=grant(24),
        name="grad_theirs",
    )(begun_theirs, w_mine, w_theirs, payload, far)
    received = lax.ppermute(sent, "core", SWAP)
    summed = pl.pallas_call(
        grad_mine,
        out_shape=grad_shape,
        in_specs=[VMEM] * 3,
        out_specs=VMEM,
        compiler_params=grant(24),
        name="grad_mine",
    )(begun_mine, local, far)
    pairs = Y * rows_shard // 2
    scaled = pl.pallas_call(
        combine,
        out_shape=jax.ShapeDtypeStruct((PLACES, 2, (pairs + 1) * lanes), f32),
        in_specs=[VMEM] * 2,
        out_specs=VMEM,
        compiler_params=grant(6),
        name="combine",
    )(summed, received)

    columns = pl.pallas_call(
        split_cols,
        out_shape=jax.ShapeDtypeStruct((Y, 3, experts, rows_shard, lanes), f32),
        in_specs=[VMEM] * 3,
        out_specs=VMEM,
        compiler_params=grant(4),
        name="split_cols",
    )(master, first_moment, second_moment)

    def for_chip(step, x):
        return lax.dynamic_index_in_dim(x, (y + step) % Y, keepdims=False)

    m_low = lax.ppermute(for_chip(1, columns), "y", UP)
    m_high = lax.ppermute(for_chip(3, columns), "y", DOWN)
    m_far = lax.ppermute(for_chip(2, columns), "y", ACROSS)
    m_own = for_chip(0, columns)

    got = lax.all_to_all(scaled.astype(jnp.float16), ("x", "z"), 0, 0, tiled=True)
    got = got.astype(f32)
    select = (old_slots[:, None] == jnp.arange(experts, dtype=jnp.int32)[None, :]).astype(f32)
    per_slot = jnp.sum(row_count.astype(f32), axis=0)
    total = jnp.dot(per_slot, select, precision=lax.Precision.HIGHEST)
    picked, after = pl.pallas_call(
        adam,
        out_shape=(
            jax.ShapeDtypeStruct((PLACES, Y * rows_shard, lanes), bf16),
            jax.ShapeDtypeStruct((Y, 3, experts, rows_shard, lanes), f32),
        ),
        in_specs=[SMEM] * 3 + [VMEM] * 5,
        out_specs=(VMEM, VMEM),
        scratch_shapes=[
            pltpu.VMEM((Y, 3, experts, rows_shard, lanes), f32),
            pltpu.VMEM((experts, 2, pairs * lanes), f32),
            pltpu.VMEM((experts, Y * rows_shard, lanes), bf16),
        ],
        compiler_params=grant(6),
        name="adam",
    )(old_slots, new_slots, total, got, m_own, m_low, m_high, m_far)
    block_rows = PLACES * rows_shard
    landed = lax.all_to_all(
        picked.reshape(Z, X * Y * rows_shard, lanes), "z", 0, 0, tiled=True
    )

    s_low = lax.ppermute(for_chip(1, after), "y", UP)
    s_high = lax.ppermute(for_chip(3, after), "y", DOWN)
    s_far = lax.ppermute(for_chip(2, after), "y", ACROSS)
    whole = jax.ShapeDtypeStruct((experts, rows_shard, width), f32)
    new_master, new_first, new_second = pl.pallas_call(
        join_cols,
        out_shape=(whole,) * 3,
        in_specs=[VMEM] * 4,
        out_specs=(VMEM,) * 3,
        scratch_shapes=[pltpu.VMEM((Y, 3, experts, rows_shard, lanes), f32)],
        compiler_params=grant(6),
        name="join_cols",
    )(for_chip(0, after), s_low, s_high, s_far)

    landed = (
        landed.reshape(Z, X, Y, rows_shard, lanes)
        .transpose(1, 2, 0, 3, 4)
        .reshape(X, Y * Z * rows_shard, lanes)
    )
    copies = jnp.broadcast_to(landed[None], (Y, *landed.shape))
    mine = lax.all_to_all(
        copies.reshape(Y * X, Y * Z * rows_shard, lanes), ("y", "x"), 0, 0, tiled=True
    ).reshape(Y, X, Y, Z * rows_shard, lanes)
    theirs = lax.ppermute(mine, "core", SWAP)
    scratch = [pltpu.VMEM((Y, block_rows, width), bf16), pltpu.SemaphoreType.DMA((Y,))]
    whole = jax.ShapeDtypeStruct((Y, C, block_rows, width), bf16)
    begun = pl.pallas_call(
        join_mine,
        out_shape=whole,
        in_specs=[VMEM],
        out_specs=hbm,
        scratch_shapes=scratch,
        compiler_params=grant(8),
        name="join_mine",
    )(mine)
    new_weights = pl.pallas_call(
        join_theirs,
        out_shape=whole,
        in_specs=[VMEM, hbm],
        out_specs=hbm,
        scratch_shapes=scratch,
        input_output_aliases={1: 0},
        compiler_params=grant(8),
        name="join_theirs",
    )(theirs, begun)
    return (new_weights.reshape(1, -1, width), new_master, new_first, new_second)


def solution(mesh):
    fine = Mesh(mesh.devices.reshape(Y, C, X, Z), ("y", "core", "x", "z"))
    dp, place = ("y", "core"), ("x", "z")
    placed = (
        P(dp, place, None, None),
        P(dp, place, None, None),
        P(dp, place, None, None),
        P(),
        P(),
        P(),
        P(None, dp + place, None),
        P(None, dp + place, None),
        P(None, dp + place, None),
    )

    return jax.shard_map(
        shards,
        mesh=fine,
        in_specs=placed,
        out_specs=(
            P(place, None, None),
            P(None, dp + place, None),
            P(None, dp + place, None),
            P(None, dp + place, None),
        ),
        check_vma=False,
    )
```

```python
import jax
import jax.numpy as jnp
from jax import lax
from jax.experimental import pallas as pl
from jax.experimental.pallas import tpu as pltpu
from jax.sharding import Mesh
from jax.sharding import PartitionSpec as P


decay_first = 0.9
decay_second = 0.95
learn_rate = 0.001
weight_decay = 0.1
epsilon = 1e-08
step_number = 20.0

Y, C, X, Z = 4, 2, 4, 16
PLACES = X * Z
UP = [(i, (i + 1) % Y) for i in range(Y)]
DOWN = [(i, (i - 1) % Y) for i in range(Y)]
ACROSS = [(i, (i + 2) % Y) for i in range(Y)]
SWAP = [(0, 1), (1, 0)]
APART = [(i * C + c, (i + 1 - 2 * c) % Y * C + c) for i in range(Y) for c in range(C)]
BACK = [(t, s) for s, t in APART]
VMEM = pl.BlockSpec(memory_space=pltpu.VMEM)
SMEM = pl.BlockSpec(memory_space=pltpu.SMEM)
ANY = pl.BlockSpec(memory_space=pl.ANY)


def grant(mib):
    return pltpu.CompilerParams(vmem_limit_bytes=mib << 20)


def lower_half(x):
    return lax.broadcasted_iota(jnp.int32, x.shape, x.ndim - 1) < x.shape[-1] // 2


def swapped(x):
    return pltpu.roll(x, x.shape[-1] // 2, x.ndim - 1)


def split_cols(*refs):
    ins, out = refs[:-1], refs[-1]
    lanes = out.shape[-1]
    half = ins[0].shape[-1] // 2
    for n, x in enumerate(ins):
        for pair in range(Y // 2):
            gate = x[:, :, pair * lanes : (pair + 1) * lanes]
            up = x[:, :, half + pair * lanes : half + (pair + 1) * lanes]
            low = lower_half(gate)
            out[2 * pair, n] = jnp.where(low, gate, swapped(up))
            out[2 * pair + 1, n] = jnp.where(low, swapped(gate), up)


def join_cols(own, low, high, far, *refs):
    outs, parts = refs[:-1], refs[-1]
    y = lax.axis_index("y")
    parts[y] = own[...]
    parts[(y + 3) % Y] = low[...]
    parts[(y + 1) % Y] = high[...]
    parts[(y + 2) % Y] = far[...]
    lanes = own.shape[-1]
    half = outs[0].shape[-1] // 2
    for n, out in enumerate(outs):
        for pair in range(Y // 2):
            a, b = parts[2 * pair, n], parts[2 * pair + 1, n]
            first = lower_half(a)
            out[:, :, pair * lanes : (pair + 1) * lanes] = jnp.where(first, a, swapped(b))
            out[:, :, half + pair * lanes : half + (pair + 1) * lanes] = jnp.where(
                first, swapped(a), b
            )


def prepare(counts, order, hidden, master, out):
    batches, batch_rows = order.shape
    experts, rows_shard, width = master.shape
    lanes = out.shape[-1]
    half = width // 2
    group_here = lax.axis_index("y") * C + lax.axis_index("core")
    count = counts[group_here, lax.axis_index("x") * Z + lax.axis_index("z")]
    blocks = []
    for m in range(batches):
        at = m * batch_rows
        slot = lax.broadcasted_iota(jnp.int32, (batch_rows, hidden.shape[1]), 0) + at
        live = jnp.where(slot < count, hidden[at : at + batch_rows, :].astype(jnp.float32), 0.0)
        row = lax.broadcasted_iota(jnp.int32, (batch_rows, batch_rows), 0)
        moves = (jnp.broadcast_to(order[m : m + 1, :], row.shape) == row).astype(jnp.bfloat16)
        blocks.append(
            jnp.dot(moves, live.astype(jnp.bfloat16), preferred_element_type=jnp.float32)
        )
    upper = jnp.concatenate(blocks[: batches // 2], axis=0)
    lower = jnp.concatenate(blocks[batches // 2 :], axis=0)
    weights = experts * rows_shard
    for pair in range(Y // 2):
        cut = slice(pair * lanes, (pair + 1) * lanes)
        first = lower_half(upper[:, cut])
        out[2 * pair, weights:, :] = jnp.where(
            first, upper[:, cut], swapped(lower[:, cut])
        ).astype(jnp.bfloat16)
        out[2 * pair + 1, weights:, :] = jnp.where(
            first, swapped(upper[:, cut]), lower[:, cut]
        ).astype(jnp.bfloat16)
        gate = jnp.concatenate([master[e, :, cut] for e in range(experts)], axis=0)
        up_cut = slice(half + pair * lanes, half + (pair + 1) * lanes)
        up = jnp.concatenate([master[e, :, up_cut] for e in range(experts)], axis=0)
        first = lower_half(gate)
        out[2 * pair, :weights, :] = jnp.where(first, gate, swapped(up)).astype(jnp.bfloat16)
        out[2 * pair + 1, :weights, :] = jnp.where(first, swapped(gate), up).astype(jnp.bfloat16)


def pick_old(slots, payload, out, table, picked, sem):
    experts, rows, _ = table.shape
    rows_shard = rows // Y
    parts = [payload[y, : experts * rows_shard, :].astype(jnp.float32) for y in range(Y)]
    for e in range(experts):
        table[e] = jnp.concatenate(
            [part[e * rows_shard : (e + 1) * rows_shard] for part in parts], axis=0
        ).astype(jnp.bfloat16)
    for p in range(PLACES):
        picked[p] = table[slots[p]]
    copy = pltpu.make_async_copy(picked, out, sem)
    copy.start()
    copy.wait()


def adam(old, new, total, got, own, low, high, far, out, after, state, acc, table):
    experts, _, data = acc.shape
    rows, lanes = state.shape[3:]
    y_here = lax.axis_index("y")
    state[y_here] = own[...]
    state[(y_here + 3) % Y] = low[...]
    state[(y_here + 1) % Y] = high[...]
    state[(y_here + 2) % Y] = far[...]
    acc[...] = jnp.zeros_like(acc)
    for p in range(PLACES):
        undo = jnp.exp2(got[p, :, data:] - 14.0)
        acc[old[p]] += got[p, :, :data] * jnp.concatenate([undo] * (data // lanes), axis=1)
    for e in range(experts):
        master, first, second = (
            jnp.concatenate([state[y, n, e] for y in range(Y)], axis=0) for n in range(3)
        )
        grad = jnp.concatenate(
            [acc[e, :, at : at + lanes] for at in range(0, data, lanes)], axis=0
        )
        grad = grad / total[e]
        new_first = decay_first * first + (1.0 - decay_first) * grad
        new_second = decay_second * second + (1.0 - decay_second) * grad * grad
        first_hat = new_first / (1.0 - decay_first**step_number)
        second_hat = new_second / (1.0 - decay_second**step_number)
        new_master = master - learn_rate * (
            first_hat / (jnp.sqrt(second_hat) + epsilon) + weight_decay * master
        )
        table[e] = new_master.astype(jnp.bfloat16)
        for n, value in enumerate((new_master, new_first, new_second)):
            for y in range(Y):
                after[y, n, e] = value[y * rows : (y + 1) * rows]
    for p in range(PLACES):
        out[p % Z * X + p // Z] = table[new[p]]


def natural(weights):
    rows_shard = weights.shape[1] // Y
    wide = weights[...].astype(jnp.float32)
    return [
        wide[:, y * rows_shard : (y + 1) * rows_shard, :]
        .reshape(PLACES * rows_shard, -1)
        .astype(jnp.bfloat16)
        for y in range(Y)
    ]


def forward_part(chunk, weights, which):
    wide = weights.shape[1]
    total = None
    for y in range(Y):
        at = pl.multiple_of((2 * y + which) * wide, wide)
        term = jnp.dot(chunk[:, pl.ds(at, wide)], weights[y], preferred_element_type=jnp.float32)
        total = term if total is None else total + term
    return total


def local_part(both, payload, source):
    packed = both.shape[0] // 2
    other = swapped(both)
    first = lower_half(both)
    gate = jnp.where(first, both, other)
    sigma = jax.nn.sigmoid(gate)
    active = gate * sigma
    slope = sigma * (1.0 + gate * (1.0 - sigma))
    hidden = payload[source, payload.shape[1] - packed :, :].astype(jnp.float32)
    around = swapped(hidden)
    begin = lower_half(hidden)
    incoming = jnp.concatenate(
        [jnp.where(begin, hidden, around), jnp.where(begin, around, hidden)], axis=0
    )
    local = jnp.where(first, incoming * other * slope, incoming * active)
    return local.T.astype(jnp.bfloat16)


def grad_part(local, chunk, y, half, wide):
    at = pl.multiple_of((2 * y + half) * wide, wide)
    return jnp.dot(local, chunk[:, pl.ds(at, wide)], preferred_element_type=jnp.float32)


def finish_grad(out_ref, begun, local, chunk, half):
    rows_shard = out_ref.shape[1] // Y
    wide = PLACES * rows_shard
    peak = None
    for y in range(Y):
        total = begun[y] + grad_part(local, chunk, y, half, wide)
        size = jnp.abs(total)
        peak = size if peak is None else jnp.maximum(peak, size)
        out_ref[:PLACES, y * rows_shard : (y + 1) * rows_shard, :] = total.T.reshape(
            PLACES, rows_shard, -1
        )
    out_ref[PLACES] = jnp.broadcast_to(jnp.max(peak, keepdims=True), out_ref.shape[1:])


def forward_mine(mine, own, one, two, out_ref, weights_ref):
    for y, block in enumerate(natural(mine)):
        weights_ref[y] = block
    core = lax.axis_index("core")
    out_ref[0] = forward_part(own, weights_ref, core)
    out_ref[1] = forward_part(one, weights_ref, core)
    out_ref[2] = forward_part(two, weights_ref, core)


def near_grad(part_ref, theirs, payload, own, one, two, theirs_ref, mine_ref, weights_ref):
    for y, block in enumerate(natural(theirs)):
        weights_ref[y] = block
    y_here, core = lax.axis_index("y"), lax.axis_index("core")
    chunks = (own, one, two)
    steps = (0, 3 + 2 * core, 1 + 2 * core)
    locals_ = []
    for k, (step, chunk) in enumerate(zip(steps, chunks)):
        both = part_ref[k] + forward_part(chunk, weights_ref, 1 - core)
        locals_.append(local_part(both, payload, (y_here + step) % Y))
    wide = theirs_ref.shape[2]
    for out_ref, half in ((theirs_ref, 1 - core), (mine_ref, core)):
        for y in range(Y):
            total = None
            for local, chunk in zip(locals_, chunks):
                term = grad_part(local, chunk, y, half, wide)
                total = term if total is None else total + term
            out_ref[y] = total


def grad_theirs(begun, mine, theirs, payload, chunk, out_ref, local_ref):
    core = lax.axis_index("core")
    both = forward_part(chunk, mine, core) + forward_part(chunk, theirs, 1 - core)
    local = local_part(both, payload, (lax.axis_index("y") + 2) % Y)
    local_ref[...] = local
    finish_grad(out_ref, begun, local, chunk, 1 - core)


def grad_mine(begun, local_ref, chunk, out_ref):
    finish_grad(out_ref, begun, local_ref[...], chunk, lax.axis_index("core"))


def combine(mine, theirs, out):
    lanes = mine.shape[-1]
    pairs = out.shape[2] // lanes - 1
    bits = jnp.ceil(jnp.log2(jnp.maximum(mine[PLACES] + theirs[PLACES], 1e-30)))
    scale = jnp.exp2(14.0 - bits)
    for t in range(pairs):
        cut = slice(2 * t, 2 * t + 2)
        out[:, :, t * lanes : (t + 1) * lanes] = (
            mine[:PLACES, cut, :] + theirs[:PLACES, cut, :]
        ) * scale[cut]
    out[:, :, pairs * lanes :] = jnp.broadcast_to(bits[:2], (PLACES, 2, bits.shape[1]))


def join(source, out, which, blocks, sems):
    rows, lanes = source.shape[3:]
    half = out.shape[-1] // 2
    copies = []
    for y in range(Y):
        for x in range(X):
            at = slice(x * rows, (x + 1) * rows)
            for pair in range(Y // 2):
                a = source[2 * pair, x, y].astype(jnp.float32)
                b = source[2 * pair + 1, x, y].astype(jnp.float32)
                first = lower_half(a)
                blocks[y, at, pair * lanes : (pair + 1) * lanes] = jnp.where(
                    first, a, swapped(b)
                ).astype(jnp.bfloat16)
                blocks[y, at, half + pair * lanes : half + (pair + 1) * lanes] = jnp.where(
                    first, swapped(a), b
                ).astype(jnp.bfloat16)
        copy = pltpu.make_async_copy(blocks.at[y], out.at[y, which], sems.at[y])
        copy.start()
        copies.append(copy)
    for copy in copies:
        copy.wait()


def join_mine(source, out, blocks, sems):
    join(source, out, lax.axis_index("core"), blocks, sems)


def join_theirs(source, begun, out, blocks, sems):
    join(source, out, 1 - lax.axis_index("core"), blocks, sems)


def shards(
    tokens, hidden_grad, routing, row_count, old_slots, new_slots, master, first_moment, second_moment
):
    y = lax.axis_index("y")
    experts, rows_shard, width = master.shape
    hid = width // 2
    part = hid // Y
    lanes = 2 * part
    f32, bf16 = jnp.float32, jnp.bfloat16
    own = tokens[0, 0]
    rows = own.shape[0]
    half_rows = rows // 2
    hbm = pl.BlockSpec(memory_space=pltpu.MemorySpace.HBM)
    payload = pl.pallas_call(
        prepare,
        out_shape=jax.ShapeDtypeStruct((Y, experts * rows_shard + half_rows, lanes), bf16),
        in_specs=[SMEM, VMEM, VMEM, VMEM],
        out_specs=VMEM,
        name="prepare",
    )(row_count, routing[0, 0], hidden_grad[0, 0], master)
    payload = lax.all_to_all(payload, "y", 0, 0, tiled=True)
    near_one = lax.ppermute(own, ("y", "core"), APART)
    near_two = lax.ppermute(own, ("y", "core"), BACK)
    picked = pl.pallas_call(
        pick_old,
        out_shape=jax.ShapeDtypeStruct((PLACES, Y * rows_shard, lanes), bf16),
        in_specs=[SMEM, VMEM],
        out_specs=pl.BlockSpec(memory_space=pltpu.MemorySpace.HBM),
        scratch_shapes=[
            pltpu.VMEM((experts, Y * rows_shard, lanes), bf16),
            pltpu.VMEM((PLACES, Y * rows_shard, lanes), bf16),
            pltpu.SemaphoreType.DMA(()),
        ],
        compiler_params=grant(4),
        name="pick_old",
    )(old_slots, payload)
    landed = lax.all_to_all(picked, ("x", "z"), 0, 0, tiled=True)
    far = lax.ppermute(near_one, ("y", "core"), APART)

    w_mine = landed
    w_theirs = lax.ppermute(w_mine, "core", SWAP)

    wide = PLACES * rows_shard
    weights_shape = jax.ShapeDtypeStruct((Y, wide, lanes), bf16)
    forward, w_mine = pl.pallas_call(
        forward_mine,
        out_shape=(jax.ShapeDtypeStruct((3, rows, lanes), f32), weights_shape),
        in_specs=[VMEM] * 4,
        out_specs=(VMEM, VMEM),
        compiler_params=grant(24),
        name="forward_mine",
    )(w_mine, own, near_one, near_two)
    begun_shape = jax.ShapeDtypeStruct((Y, lanes, wide), f32)
    begun_theirs, begun_mine, w_theirs = pl.pallas_call(
        near_grad,
        out_shape=(begun_shape, begun_shape, weights_shape),
        in_specs=[VMEM] * 6,
        out_specs=(VMEM, VMEM, VMEM),
        compiler_params=grant(24),
        name="near_grad",
    )(forward, w_theirs, payload, own, near_one, near_two)
    grad_shape = jax.ShapeDtypeStruct((PLACES + 1, Y * rows_shard, lanes), f32)
    sent, local = pl.pallas_call(
        grad_theirs,
        out_shape=(grad_shape, jax.ShapeDtypeStruct((lanes, rows), bf16)),
        in_specs=[VMEM] * 5,
        out_specs=(VMEM, VMEM),
        compiler_params=grant(24),
        name="grad_theirs",
    )(begun_theirs, w_mine, w_theirs, payload, far)
    received = lax.ppermute(sent, "core", SWAP)
    summed = pl.pallas_call(
        grad_mine,
        out_shape=grad_shape,
        in_specs=[VMEM] * 3,
        out_specs=VMEM,
        compiler_params=grant(24),
        name="grad_mine",
    )(begun_mine, local, far)
    pairs = Y * rows_shard // 2
    scaled = pl.pallas_call(
        combine,
        out_shape=jax.ShapeDtypeStruct((PLACES, 2, (pairs + 1) * lanes), f32),
        in_specs=[VMEM] * 2,
        out_specs=VMEM,
        compiler_params=grant(6),
        name="combine",
    )(summed, received)

    columns = pl.pallas_call(
        split_cols,
        out_shape=jax.ShapeDtypeStruct((Y, 3, experts, rows_shard, lanes), f32),
        in_specs=[VMEM] * 3,
        out_specs=VMEM,
        compiler_params=grant(4),
        name="split_cols",
    )(master, first_moment, second_moment)

    def for_chip(step, x):
        return lax.dynamic_index_in_dim(x, (y + step) % Y, keepdims=False)

    m_low = lax.ppermute(for_chip(1, columns), "y", UP)
    m_high = lax.ppermute(for_chip(3, columns), "y", DOWN)
    m_far = lax.ppermute(for_chip(2, columns), "y", ACROSS)
    m_own = for_chip(0, columns)

    got = lax.all_to_all(scaled.astype(jnp.float16), ("x", "z"), 0, 0, tiled=True)
    got = got.astype(f32)
    select = (old_slots[:, None] == jnp.arange(experts, dtype=jnp.int32)[None, :]).astype(f32)
    per_slot = jnp.sum(row_count.astype(f32), axis=0)
    total = jnp.dot(per_slot, select, precision=lax.Precision.HIGHEST)
    picked, after = pl.pallas_call(
        adam,
        out_shape=(
            jax.ShapeDtypeStruct((PLACES, Y * rows_shard, lanes), bf16),
            jax.ShapeDtypeStruct((Y, 3, experts, rows_shard, lanes), f32),
        ),
        in_specs=[SMEM] * 3 + [VMEM] * 5,
        out_specs=(VMEM, VMEM),
        scratch_shapes=[
            pltpu.VMEM((Y, 3, experts, rows_shard, lanes), f32),
            pltpu.VMEM((experts, 2, pairs * lanes), f32),
            pltpu.VMEM((experts, Y * rows_shard, lanes), bf16),
        ],
        compiler_params=grant(6),
        name="adam",
    )(old_slots, new_slots, total, got, m_own, m_low, m_high, m_far)
    block_rows = PLACES * rows_shard
    landed = lax.all_to_all(
        picked.reshape(Z, X * Y * rows_shard, lanes), "z", 0, 0, tiled=True
    )

    s_low = lax.ppermute(for_chip(1, after), "y", UP)
    s_high = lax.ppermute(for_chip(3, after), "y", DOWN)
    s_far = lax.ppermute(for_chip(2, after), "y", ACROSS)
    whole = jax.ShapeDtypeStruct((experts, rows_shard, width), f32)
    new_master, new_first, new_second = pl.pallas_call(
        join_cols,
        out_shape=(whole,) * 3,
        in_specs=[VMEM] * 4,
        out_specs=(VMEM,) * 3,
        scratch_shapes=[pltpu.VMEM((Y, 3, experts, rows_shard, lanes), f32)],
        compiler_params=grant(6),
        name="join_cols",
    )(for_chip(0, after), s_low, s_high, s_far)

    landed = (
        landed.reshape(Z, X, Y, rows_shard, lanes)
        .transpose(1, 2, 0, 3, 4)
        .reshape(X, Y * Z * rows_shard, lanes)
    )
    copies = jnp.broadcast_to(landed[None], (Y, *landed.shape))
    mine = lax.all_to_all(
        copies.reshape(Y * X, Y * Z * rows_shard, lanes), ("y", "x"), 0, 0, tiled=True
    ).reshape(Y, X, Y, Z * rows_shard, lanes)
    theirs = lax.ppermute(mine, "core", SWAP)
    scratch = [pltpu.VMEM((Y, block_rows, width), bf16), pltpu.SemaphoreType.DMA((Y,))]
    whole = jax.ShapeDtypeStruct((Y, C, block_rows, width), bf16)
    begun = pl.pallas_call(
        join_mine,
        out_shape=whole,
        in_specs=[VMEM],
        out_specs=hbm,
        scratch_shapes=scratch,
        compiler_params=grant(8),
        name="join_mine",
    )(mine)
    new_weights = pl.pallas_call(
        join_theirs,
        out_shape=whole,
        in_specs=[VMEM, hbm],
        out_specs=hbm,
        scratch_shapes=scratch,
        input_output_aliases={1: 0},
        compiler_params=grant(8),
        name="join_theirs",
    )(theirs, begun)
    return (new_weights.reshape(1, -1, width), new_master, new_first, new_second)


def solution(mesh):
    fine = Mesh(mesh.devices.reshape(Y, C, X, Z), ("y", "core", "x", "z"))
    dp, place = ("y", "core"), ("x", "z")
    placed = (
        P(dp, place, None, None),
        P(dp, place, None, None),
        P(dp, place, None, None),
        P(),
        P(),
        P(),
        P(None, dp + place, None),
        P(None, dp + place, None),
        P(None, dp + place, None),
    )

    return jax.shard_map(
        shards,
        mesh=fine,
        in_specs=placed,
        out_specs=(
            P(place, None, None),
            P(None, dp + place, None),
            P(None, dp + place, None),
            P(None, dp + place, None),
        ),
        check_vma=False,
    )
```

```python
import jax
import jax.numpy as jnp
from jax import lax
from jax.experimental import pallas as pl
from jax.experimental.pallas import tpu as pltpu
from jax.sharding import Mesh
from jax.sharding import PartitionSpec as P


decay_first = 0.9
decay_second = 0.95
learn_rate = 0.001
weight_decay = 0.1
epsilon = 1e-08
step_number = 20.0

Y, C, X, Z = 4, 2, 4, 16
PLACES = X * Z
UP = [(i, (i + 1) % Y) for i in range(Y)]
DOWN = [(i, (i - 1) % Y) for i in range(Y)]
ACROSS = [(i, (i + 2) % Y) for i in range(Y)]
SWAP = [(0, 1), (1, 0)]
APART = [(i * C + c, (i + 1 - 2 * c) % Y * C + c) for i in range(Y) for c in range(C)]
BACK = [(t, s) for s, t in APART]
VMEM = pl.BlockSpec(memory_space=pltpu.VMEM)
SMEM = pl.BlockSpec(memory_space=pltpu.SMEM)
ANY = pl.BlockSpec(memory_space=pl.ANY)


def grant(mib):
    return pltpu.CompilerParams(vmem_limit_bytes=mib << 20)


def lower_half(x):
    return lax.broadcasted_iota(jnp.int32, x.shape, x.ndim - 1) < x.shape[-1] // 2


def swapped(x):
    return pltpu.roll(x, x.shape[-1] // 2, x.ndim - 1)


def split_cols(*refs):
    ins, out = refs[:-1], refs[-1]
    lanes = out.shape[-1]
    half = ins[0].shape[-1] // 2
    for n, x in enumerate(ins):
        for pair in range(Y // 2):
            gate = x[:, :, pair * lanes : (pair + 1) * lanes]
            up = x[:, :, half + pair * lanes : half + (pair + 1) * lanes]
            low = lower_half(gate)
            out[2 * pair, n] = jnp.where(low, gate, swapped(up))
            out[2 * pair + 1, n] = jnp.where(low, swapped(gate), up)


def join_cols(own, low, high, far, *refs):
    outs, parts = refs[:-1], refs[-1]
    y = lax.axis_index("y")
    parts[y] = own[...]
    parts[(y + 3) % Y] = low[...]
    parts[(y + 1) % Y] = high[...]
    parts[(y + 2) % Y] = far[...]
    lanes = own.shape[-1]
    half = outs[0].shape[-1] // 2
    for n, out in enumerate(outs):
        for pair in range(Y // 2):
            a, b = parts[2 * pair, n], parts[2 * pair + 1, n]
            first = lower_half(a)
            out[:, :, pair * lanes : (pair + 1) * lanes] = jnp.where(first, a, swapped(b))
            out[:, :, half + pair * lanes : half + (pair + 1) * lanes] = jnp.where(
                first, swapped(a), b
            )


def prepare(counts, order, hidden, master, out):
    batches, batch_rows = order.shape
    experts, rows_shard, width = master.shape
    lanes = out.shape[-1]
    half = width // 2
    group_here = lax.axis_index("y") * C + lax.axis_index("core")
    count = counts[group_here, lax.axis_index("x") * Z + lax.axis_index("z")]
    blocks = []
    for m in range(batches):
        at = m * batch_rows
        slot = lax.broadcasted_iota(jnp.int32, (batch_rows, hidden.shape[1]), 0) + at
        live = jnp.where(slot < count, hidden[at : at + batch_rows, :].astype(jnp.float32), 0.0)
        row = lax.broadcasted_iota(jnp.int32, (batch_rows, batch_rows), 0)
        moves = (jnp.broadcast_to(order[m : m + 1, :], row.shape) == row).astype(jnp.bfloat16)
        blocks.append(
            jnp.dot(moves, live.astype(jnp.bfloat16), preferred_element_type=jnp.float32)
        )
    upper = jnp.concatenate(blocks[: batches // 2], axis=0)
    lower = jnp.concatenate(blocks[batches // 2 :], axis=0)
    weights = experts * rows_shard
    for pair in range(Y // 2):
        cut = slice(pair * lanes, (pair + 1) * lanes)
        first = lower_half(upper[:, cut])
        out[2 * pair, weights:, :] = jnp.where(
            first, upper[:, cut], swapped(lower[:, cut])
        ).astype(jnp.bfloat16)
        out[2 * pair + 1, weights:, :] = jnp.where(
            first, swapped(upper[:, cut]), lower[:, cut]
        ).astype(jnp.bfloat16)
        gate = jnp.concatenate([master[e, :, cut] for e in range(experts)], axis=0)
        up_cut = slice(half + pair * lanes, half + (pair + 1) * lanes)
        up = jnp.concatenate([master[e, :, up_cut] for e in range(experts)], axis=0)
        first = lower_half(gate)
        out[2 * pair, :weights, :] = jnp.where(first, gate, swapped(up)).astype(jnp.bfloat16)
        out[2 * pair + 1, :weights, :] = jnp.where(first, swapped(gate), up).astype(jnp.bfloat16)


def pick_old(slots, payload, out, table, picked, sem):
    experts, rows, _ = table.shape
    rows_shard = rows // Y
    parts = [payload[y, : experts * rows_shard, :].astype(jnp.float32) for y in range(Y)]
    for e in range(experts):
        table[e] = jnp.concatenate(
            [part[e * rows_shard : (e + 1) * rows_shard] for part in parts], axis=0
        ).astype(jnp.bfloat16)
    for p in range(PLACES):
        picked[p] = table[slots[p]]
    copy = pltpu.make_async_copy(picked, out, sem)
    copy.start()
    copy.wait()


def adam(old, new, total, got, own, low, high, far, out, after, state, acc, table):
    experts, _, data = acc.shape
    rows, lanes = state.shape[3:]
    y_here = lax.axis_index("y")
    state[y_here] = own[...]
    state[(y_here + 3) % Y] = low[...]
    state[(y_here + 1) % Y] = high[...]
    state[(y_here + 2) % Y] = far[...]
    acc[...] = jnp.zeros_like(acc)
    for p in range(PLACES):
        undo = jnp.exp2(got[p, :, data:] - 14.0)
        acc[old[p]] += got[p, :, :data] * jnp.concatenate([undo] * (data // lanes), axis=1)
    for e in range(experts):
        master, first, second = (
            jnp.concatenate([state[y, n, e] for y in range(Y)], axis=0) for n in range(3)
        )
        grad = jnp.concatenate(
            [acc[e, :, at : at + lanes] for at in range(0, data, lanes)], axis=0
        )
        grad = grad / total[e]
        new_first = decay_first * first + (1.0 - decay_first) * grad
        new_second = decay_second * second + (1.0 - decay_second) * grad * grad
        first_hat = new_first / (1.0 - decay_first**step_number)
        second_hat = new_second / (1.0 - decay_second**step_number)
        new_master = master - learn_rate * (
            first_hat / (jnp.sqrt(second_hat) + epsilon) + weight_decay * master
        )
        table[e] = new_master.astype(jnp.bfloat16)
        for n, value in enumerate((new_master, new_first, new_second)):
            for y in range(Y):
                after[y, n, e] = value[y * rows : (y + 1) * rows]
    for p in range(PLACES):
        out[p % Z * X + p // Z] = table[new[p]]


def natural(weights):
    rows_shard = weights.shape[1] // Y
    wide = weights[...].astype(jnp.float32)
    return [
        wide[:, y * rows_shard : (y + 1) * rows_shard, :]
        .reshape(PLACES * rows_shard, -1)
        .astype(jnp.bfloat16)
        for y in range(Y)
    ]


def forward_part(chunk, weights, which):
    wide = weights.shape[1]
    total = None
    for y in range(Y):
        at = pl.multiple_of((2 * y + which) * wide, wide)
        term = jnp.dot(chunk[:, pl.ds(at, wide)], weights[y], preferred_element_type=jnp.float32)
        total = term if total is None else total + term
    return total


def local_part(both, payload, source):
    packed = both.shape[0] // 2
    other = swapped(both)
    first = lower_half(both)
    gate = jnp.where(first, both, other)
    sigma = jax.nn.sigmoid(gate)
    active = gate * sigma
    slope = sigma * (1.0 + gate * (1.0 - sigma))
    hidden = payload[source, payload.shape[1] - packed :, :].astype(jnp.float32)
    around = swapped(hidden)
    begin = lower_half(hidden)
    incoming = jnp.concatenate(
        [jnp.where(begin, hidden, around), jnp.where(begin, around, hidden)], axis=0
    )
    local = jnp.where(first, incoming * other * slope, incoming * active)
    return local.T.astype(jnp.bfloat16)


def grad_part(local, chunk, y, half, wide):
    at = pl.multiple_of((2 * y + half) * wide, wide)
    return jnp.dot(local, chunk[:, pl.ds(at, wide)], preferred_element_type=jnp.float32)


def finish_grad(out_ref, begun, local, chunk, half):
    rows_shard = out_ref.shape[1] // Y
    wide = PLACES * rows_shard
    peak = None
    for y in range(Y):
        total = begun[y] + grad_part(local, chunk, y, half, wide)
        size = jnp.abs(total)
        peak = size if peak is None else jnp.maximum(peak, size)
        out_ref[:PLACES, y * rows_shard : (y + 1) * rows_shard, :] = total.T.reshape(
            PLACES, rows_shard, -1
        )
    out_ref[PLACES] = jnp.broadcast_to(jnp.max(peak, keepdims=True), out_ref.shape[1:])


def forward_mine(mine, own, one, two, out_ref, weights_ref):
    for y, block in enumerate(natural(mine)):
        weights_ref[y] = block
    core = lax.axis_index("core")
    out_ref[0] = forward_part(own, weights_ref, core)
    out_ref[1] = forward_part(one, weights_ref, core)
    out_ref[2] = forward_part(two, weights_ref, core)


def near_grad(part_ref, theirs, payload, own, one, two, theirs_ref, mine_ref, weights_ref):
    for y, block in enumerate(natural(theirs)):
        weights_ref[y] = block
    y_here, core = lax.axis_index("y"), lax.axis_index("core")
    chunks = (own, one, two)
    steps = (0, 3 + 2 * core, 1 + 2 * core)
    locals_ = []
    for k, (step, chunk) in enumerate(zip(steps, chunks)):
        both = part_ref[k] + forward_part(chunk, weights_ref, 1 - core)
        locals_.append(local_part(both, payload, (y_here + step) % Y))
    wide = theirs_ref.shape[2]
    for out_ref, half in ((theirs_ref, 1 - core), (mine_ref, core)):
        for y in range(Y):
            total = None
            for local, chunk in zip(locals_, chunks):
                term = grad_part(local, chunk, y, half, wide)
                total = term if total is None else total + term
            out_ref[y] = total


def grad_theirs(begun, mine, theirs, payload, chunk, out_ref, local_ref):
    core = lax.axis_index("core")
    both = forward_part(chunk, mine, core) + forward_part(chunk, theirs, 1 - core)
    local = local_part(both, payload, (lax.axis_index("y") + 2) % Y)
    local_ref[...] = local
    finish_grad(out_ref, begun, local, chunk, 1 - core)


def grad_mine(begun, local_ref, chunk, out_ref):
    finish_grad(out_ref, begun, local_ref[...], chunk, lax.axis_index("core"))


def combine(mine, theirs, out):
    lanes = mine.shape[-1]
    pairs = out.shape[2] // lanes - 1
    bits = jnp.ceil(jnp.log2(jnp.maximum(mine[PLACES] + theirs[PLACES], 1e-30)))
    scale = jnp.exp2(14.0 - bits)
    for t in range(pairs):
        cut = slice(2 * t, 2 * t + 2)
        out[:, :, t * lanes : (t + 1) * lanes] = (
            mine[:PLACES, cut, :] + theirs[:PLACES, cut, :]
        ) * scale[cut]
    out[:, :, pairs * lanes :] = jnp.broadcast_to(bits[:2], (PLACES, 2, bits.shape[1]))


def join(source, out, which, blocks, sems):
    rows, lanes = source.shape[3:]
    half = out.shape[-1] // 2
    copies = []
    for y in range(Y):
        for x in range(X):
            at = slice(x * rows, (x + 1) * rows)
            for pair in range(Y // 2):
                a = source[2 * pair, x, y]
                b = source[2 * pair + 1, x, y]
                first = lower_half(a)
                blocks[y, at, pair * lanes : (pair + 1) * lanes] = jnp.where(
                    first, a, swapped(b)
                )
                blocks[y, at, half + pair * lanes : half + (pair + 1) * lanes] = jnp.where(
                    first, swapped(a), b
                )
        copy = pltpu.make_async_copy(blocks.at[y], out.at[y, which], sems.at[y])
        copy.start()
        copies.append(copy)
    for copy in copies:
        copy.wait()


def join_mine(source, out, blocks, sems):
    join(source, out, lax.axis_index("core"), blocks, sems)


def join_theirs(source, begun, out, blocks, sems):
    join(source, out, 1 - lax.axis_index("core"), blocks, sems)


def shards(
    tokens, hidden_grad, routing, row_count, old_slots, new_slots, master, first_moment, second_moment
):
    y = lax.axis_index("y")
    experts, rows_shard, width = master.shape
    hid = width // 2
    part = hid // Y
    lanes = 2 * part
    f32, bf16 = jnp.float32, jnp.bfloat16
    own = tokens[0, 0]
    rows = own.shape[0]
    half_rows = rows // 2
    hbm = pl.BlockSpec(memory_space=pltpu.MemorySpace.HBM)
    payload = pl.pallas_call(
        prepare,
        out_shape=jax.ShapeDtypeStruct((Y, experts * rows_shard + half_rows, lanes), bf16),
        in_specs=[SMEM, VMEM, VMEM, VMEM],
        out_specs=VMEM,
        name="prepare",
    )(row_count, routing[0, 0], hidden_grad[0, 0], master)
    payload = lax.all_to_all(payload, "y", 0, 0, tiled=True)
    near_one = lax.ppermute(own, ("y", "core"), APART)
    near_two = lax.ppermute(own, ("y", "core"), BACK)
    picked = pl.pallas_call(
        pick_old,
        out_shape=jax.ShapeDtypeStruct((PLACES, Y * rows_shard, lanes), bf16),
        in_specs=[SMEM, VMEM],
        out_specs=pl.BlockSpec(memory_space=pltpu.MemorySpace.HBM),
        scratch_shapes=[
            pltpu.VMEM((experts, Y * rows_shard, lanes), bf16),
            pltpu.VMEM((PLACES, Y * rows_shard, lanes), bf16),
            pltpu.SemaphoreType.DMA(()),
        ],
        compiler_params=grant(4),
        name="pick_old",
    )(old_slots, payload)
    landed = lax.all_to_all(picked, ("x", "z"), 0, 0, tiled=True)
    far = lax.ppermute(near_one, ("y", "core"), APART)

    w_mine = landed
    w_theirs = lax.ppermute(w_mine, "core", SWAP)

    wide = PLACES * rows_shard
    weights_shape = jax.ShapeDtypeStruct((Y, wide, lanes), bf16)
    forward, w_mine = pl.pallas_call(
        forward_mine,
        out_shape=(jax.ShapeDtypeStruct((3, rows, lanes), f32), weights_shape),
        in_specs=[VMEM] * 4,
        out_specs=(VMEM, VMEM),
        compiler_params=grant(24),
        name="forward_mine",
    )(w_mine, own, near_one, near_two)
    begun_shape = jax.ShapeDtypeStruct((Y, lanes, wide), f32)
    begun_theirs, begun_mine, w_theirs = pl.pallas_call(
        near_grad,
        out_shape=(begun_shape, begun_shape, weights_shape),
        in_specs=[VMEM] * 6,
        out_specs=(VMEM, VMEM, VMEM),
        compiler_params=grant(24),
        name="near_grad",
    )(forward, w_theirs, payload, own, near_one, near_two)
    grad_shape = jax.ShapeDtypeStruct((PLACES + 1, Y * rows_shard, lanes), f32)
    sent, local = pl.pallas_call(
        grad_theirs,
        out_shape=(grad_shape, jax.ShapeDtypeStruct((lanes, rows), bf16)),
        in_specs=[VMEM] * 5,
        out_specs=(VMEM, VMEM),
        compiler_params=grant(24),
        name="grad_theirs",
    )(begun_theirs, w_mine, w_theirs, payload, far)
    received = lax.ppermute(sent, "core", SWAP)
    summed = pl.pallas_call(
        grad_mine,
        out_shape=grad_shape,
        in_specs=[VMEM] * 3,
        out_specs=VMEM,
        compiler_params=grant(24),
        name="grad_mine",
    )(begun_mine, local, far)
    pairs = Y * rows_shard // 2
    scaled = pl.pallas_call(
        combine,
        out_shape=jax.ShapeDtypeStruct((PLACES, 2, (pairs + 1) * lanes), f32),
        in_specs=[VMEM] * 2,
        out_specs=VMEM,
        compiler_params=grant(6),
        name="combine",
    )(summed, received)

    columns = pl.pallas_call(
        split_cols,
        out_shape=jax.ShapeDtypeStruct((Y, 3, experts, rows_shard, lanes), f32),
        in_specs=[VMEM] * 3,
        out_specs=VMEM,
        compiler_params=grant(4),
        name="split_cols",
    )(master, first_moment, second_moment)

    def for_chip(step, x):
        return lax.dynamic_index_in_dim(x, (y + step) % Y, keepdims=False)

    m_low = lax.ppermute(for_chip(1, columns), "y", UP)
    m_high = lax.ppermute(for_chip(3, columns), "y", DOWN)
    m_far = lax.ppermute(for_chip(2, columns), "y", ACROSS)
    m_own = for_chip(0, columns)

    got = lax.all_to_all(scaled.astype(jnp.float16), ("x", "z"), 0, 0, tiled=True)
    got = got.astype(f32)
    select = (old_slots[:, None] == jnp.arange(experts, dtype=jnp.int32)[None, :]).astype(f32)
    per_slot = jnp.sum(row_count.astype(f32), axis=0)
    total = jnp.dot(per_slot, select, precision=lax.Precision.HIGHEST)
    picked, after = pl.pallas_call(
        adam,
        out_shape=(
            jax.ShapeDtypeStruct((PLACES, Y * rows_shard, lanes), bf16),
            jax.ShapeDtypeStruct((Y, 3, experts, rows_shard, lanes), f32),
        ),
        in_specs=[SMEM] * 3 + [VMEM] * 5,
        out_specs=(VMEM, VMEM),
        scratch_shapes=[
            pltpu.VMEM((Y, 3, experts, rows_shard, lanes), f32),
            pltpu.VMEM((experts, 2, pairs * lanes), f32),
            pltpu.VMEM((experts, Y * rows_shard, lanes), bf16),
        ],
        compiler_params=grant(6),
        name="adam",
    )(old_slots, new_slots, total, got, m_own, m_low, m_high, m_far)
    block_rows = PLACES * rows_shard
    landed = lax.all_to_all(
        picked.reshape(Z, X * Y * rows_shard, lanes), "z", 0, 0, tiled=True
    )

    s_low = lax.ppermute(for_chip(1, after), "y", UP)
    s_high = lax.ppermute(for_chip(3, after), "y", DOWN)
    s_far = lax.ppermute(for_chip(2, after), "y", ACROSS)
    whole = jax.ShapeDtypeStruct((experts, rows_shard, width), f32)
    new_master, new_first, new_second = pl.pallas_call(
        join_cols,
        out_shape=(whole,) * 3,
        in_specs=[VMEM] * 4,
        out_specs=(VMEM,) * 3,
        scratch_shapes=[pltpu.VMEM((Y, 3, experts, rows_shard, lanes), f32)],
        compiler_params=grant(6),
        name="join_cols",
    )(for_chip(0, after), s_low, s_high, s_far)

    landed = (
        landed.reshape(Z, X, Y, rows_shard, lanes)
        .transpose(1, 2, 0, 3, 4)
        .reshape(X, Y * Z * rows_shard, lanes)
    )
    copies = jnp.broadcast_to(landed[None], (Y, *landed.shape))
    mine = lax.all_to_all(
        copies.reshape(Y * X, Y * Z * rows_shard, lanes), ("y", "x"), 0, 0, tiled=True
    ).reshape(Y, X, Y, Z * rows_shard, lanes)
    theirs = lax.ppermute(mine, "core", SWAP)
    scratch = [pltpu.VMEM((Y, block_rows, width), bf16), pltpu.SemaphoreType.DMA((Y,))]
    whole = jax.ShapeDtypeStruct((Y, C, block_rows, width), bf16)
    begun = pl.pallas_call(
        join_mine,
        out_shape=whole,
        in_specs=[VMEM],
        out_specs=hbm,
        scratch_shapes=scratch,
        compiler_params=grant(8),
        name="join_mine",
    )(mine)
    new_weights = pl.pallas_call(
        join_theirs,
        out_shape=whole,
        in_specs=[VMEM, hbm],
        out_specs=hbm,
        scratch_shapes=scratch,
        input_output_aliases={1: 0},
        compiler_params=grant(8),
        name="join_theirs",
    )(theirs, begun)
    return (new_weights.reshape(1, -1, width), new_master, new_first, new_second)


def solution(mesh):
    fine = Mesh(mesh.devices.reshape(Y, C, X, Z), ("y", "core", "x", "z"))
    dp, place = ("y", "core"), ("x", "z")
    placed = (
        P(dp, place, None, None),
        P(dp, place, None, None),
        P(dp, place, None, None),
        P(),
        P(),
        P(),
        P(None, dp + place, None),
        P(None, dp + place, None),
        P(None, dp + place, None),
    )

    return jax.shard_map(
        shards,
        mesh=fine,
        in_specs=placed,
        out_specs=(
            P(place, None, None),
            P(None, dp + place, None),
            P(None, dp + place, None),
            P(None, dp + place, None),
        ),
        check_vma=False,
    )
```

```python
import jax
import jax.numpy as jnp
from jax import lax
from jax.experimental import pallas as pl
from jax.experimental.pallas import tpu as pltpu
from jax.sharding import Mesh
from jax.sharding import PartitionSpec as P


decay_first = 0.9
decay_second = 0.95
learn_rate = 0.001
weight_decay = 0.1
epsilon = 1e-08
step_number = 20.0

Y, C, X, Z = 4, 2, 4, 16
PLACES = X * Z
UP = [(i, (i + 1) % Y) for i in range(Y)]
DOWN = [(i, (i - 1) % Y) for i in range(Y)]
ACROSS = [(i, (i + 2) % Y) for i in range(Y)]
SWAP = [(0, 1), (1, 0)]
APART = [(i * C + c, (i + 1 - 2 * c) % Y * C + c) for i in range(Y) for c in range(C)]
BACK = [(t, s) for s, t in APART]
VMEM = pl.BlockSpec(memory_space=pltpu.VMEM)
SMEM = pl.BlockSpec(memory_space=pltpu.SMEM)
ANY = pl.BlockSpec(memory_space=pl.ANY)


def grant(mib):
    return pltpu.CompilerParams(vmem_limit_bytes=mib << 20)


def lower_half(x):
    return lax.broadcasted_iota(jnp.int32, x.shape, x.ndim - 1) < x.shape[-1] // 2


def swapped(x):
    return pltpu.roll(x, x.shape[-1] // 2, x.ndim - 1)


def split_cols(*refs):
    ins, out = refs[:-1], refs[-1]
    lanes = out.shape[-1]
    half = ins[0].shape[-1] // 2
    for n, x in enumerate(ins):
        for pair in range(Y // 2):
            gate = x[:, :, pair * lanes : (pair + 1) * lanes]
            up = x[:, :, half + pair * lanes : half + (pair + 1) * lanes]
            low = lower_half(gate)
            out[2 * pair, n] = jnp.where(low, gate, swapped(up))
            out[2 * pair + 1, n] = jnp.where(low, swapped(gate), up)


def join_cols(own, low, high, far, *refs):
    outs, parts = refs[:-1], refs[-1]
    y = lax.axis_index("y")
    parts[y] = own[...]
    parts[(y + 3) % Y] = low[...]
    parts[(y + 1) % Y] = high[...]
    parts[(y + 2) % Y] = far[...]
    lanes = own.shape[-1]
    half = outs[0].shape[-1] // 2
    for n, out in enumerate(outs):
        for pair in range(Y // 2):
            a, b = parts[2 * pair, n], parts[2 * pair + 1, n]
            first = lower_half(a)
            out[:, :, pair * lanes : (pair + 1) * lanes] = jnp.where(first, a, swapped(b))
            out[:, :, half + pair * lanes : half + (pair + 1) * lanes] = jnp.where(
                first, swapped(a), b
            )


def prepare(counts, order, hidden, master, out):
    batches, batch_rows = order.shape
    experts, rows_shard, width = master.shape
    lanes = out.shape[-1]
    half = width // 2
    group_here = lax.axis_index("y") * C + lax.axis_index("core")
    count = counts[group_here, lax.axis_index("x") * Z + lax.axis_index("z")]
    blocks = []
    for m in range(batches):
        at = m * batch_rows
        slot = lax.broadcasted_iota(jnp.int32, (batch_rows, hidden.shape[1]), 0) + at
        live = jnp.where(slot < count, hidden[at : at + batch_rows, :].astype(jnp.float32), 0.0)
        row = lax.broadcasted_iota(jnp.int32, (batch_rows, batch_rows), 0)
        moves = (jnp.broadcast_to(order[m : m + 1, :], row.shape) == row).astype(jnp.bfloat16)
        blocks.append(
            jnp.dot(moves, live.astype(jnp.bfloat16), preferred_element_type=jnp.float32)
        )
    upper = jnp.concatenate(blocks[: batches // 2], axis=0)
    lower = jnp.concatenate(blocks[batches // 2 :], axis=0)
    weights = experts * rows_shard
    for pair in range(Y // 2):
        cut = slice(pair * lanes, (pair + 1) * lanes)
        first = lower_half(upper[:, cut])
        out[2 * pair, weights:, :] = jnp.where(
            first, upper[:, cut], swapped(lower[:, cut])
        ).astype(jnp.bfloat16)
        out[2 * pair + 1, weights:, :] = jnp.where(
            first, swapped(upper[:, cut]), lower[:, cut]
        ).astype(jnp.bfloat16)
        gate = jnp.concatenate([master[e, :, cut] for e in range(experts)], axis=0)
        up_cut = slice(half + pair * lanes, half + (pair + 1) * lanes)
        up = jnp.concatenate([master[e, :, up_cut] for e in range(experts)], axis=0)
        first = lower_half(gate)
        out[2 * pair, :weights, :] = jnp.where(first, gate, swapped(up)).astype(jnp.bfloat16)
        out[2 * pair + 1, :weights, :] = jnp.where(first, swapped(gate), up).astype(jnp.bfloat16)


def pick_old(slots, payload, out, table, picked, sem):
    experts, rows, _ = table.shape
    rows_shard = rows // Y
    parts = [payload[y, : experts * rows_shard, :].astype(jnp.float32) for y in range(Y)]
    for e in range(experts):
        table[e] = jnp.concatenate(
            [part[e * rows_shard : (e + 1) * rows_shard] for part in parts], axis=0
        ).astype(jnp.bfloat16)
    step = PLACES // 4
    copies = []
    for k in range(4):
        for p in range(k * step, (k + 1) * step):
            picked[p] = table[slots[p]]
        part = pl.ds(k * step, step)
        copies.append(pltpu.make_async_copy(picked.at[part], out.at[part], sem.at[k]))
        copies[-1].start()
    for copy in copies:
        copy.wait()


def adam(old, new, total, got, own, low, high, far, out, after, state, acc, table):
    experts, _, data = acc.shape
    rows, lanes = state.shape[3:]
    y_here = lax.axis_index("y")
    state[y_here] = own[...]
    state[(y_here + 3) % Y] = low[...]
    state[(y_here + 1) % Y] = high[...]
    state[(y_here + 2) % Y] = far[...]
    acc[...] = jnp.zeros_like(acc)
    for p in range(PLACES):
        undo = jnp.exp2(got[p, :, data:] - 14.0)
        acc[old[p]] += got[p, :, :data] * jnp.concatenate([undo] * (data // lanes), axis=1)
    for e in range(experts):
        master, first, second = (
            jnp.concatenate([state[y, n, e] for y in range(Y)], axis=0) for n in range(3)
        )
        grad = jnp.concatenate(
            [acc[e, :, at : at + lanes] for at in range(0, data, lanes)], axis=0
        )
        grad = grad / total[e]
        new_first = decay_first * first + (1.0 - decay_first) * grad
        new_second = decay_second * second + (1.0 - decay_second) * grad * grad
        first_hat = new_first / (1.0 - decay_first**step_number)
        second_hat = new_second / (1.0 - decay_second**step_number)
        new_master = master - learn_rate * (
            first_hat / (jnp.sqrt(second_hat) + epsilon) + weight_decay * master
        )
        table[e] = new_master.astype(jnp.bfloat16)
        for n, value in enumerate((new_master, new_first, new_second)):
            for y in range(Y):
                after[y, n, e] = value[y * rows : (y + 1) * rows]
    for p in range(PLACES):
        out[p % Z * X + p // Z] = table[new[p]]


def natural(weights):
    rows_shard = weights.shape[1] // Y
    wide = weights[...].astype(jnp.float32)
    return [
        wide[:, y * rows_shard : (y + 1) * rows_shard, :]
        .reshape(PLACES * rows_shard, -1)
        .astype(jnp.bfloat16)
        for y in range(Y)
    ]


def forward_part(chunk, weights, which):
    wide = weights.shape[1]
    total = None
    for y in range(Y):
        at = pl.multiple_of((2 * y + which) * wide, wide)
        term = jnp.dot(chunk[:, pl.ds(at, wide)], weights[y], preferred_element_type=jnp.float32)
        total = term if total is None else total + term
    return total


def local_part(both, payload, source):
    packed = both.shape[0] // 2
    other = swapped(both)
    first = lower_half(both)
    gate = jnp.where(first, both, other)
    sigma = jax.nn.sigmoid(gate)
    active = gate * sigma
    slope = sigma * (1.0 + gate * (1.0 - sigma))
    hidden = payload[source, payload.shape[1] - packed :, :].astype(jnp.float32)
    around = swapped(hidden)
    begin = lower_half(hidden)
    incoming = jnp.concatenate(
        [jnp.where(begin, hidden, around), jnp.where(begin, around, hidden)], axis=0
    )
    local = jnp.where(first, incoming * other * slope, incoming * active)
    return local.T.astype(jnp.bfloat16)


def grad_part(local, chunk, y, half, wide):
    at = pl.multiple_of((2 * y + half) * wide, wide)
    return jnp.dot(local, chunk[:, pl.ds(at, wide)], preferred_element_type=jnp.float32)


def finish_grad(out_ref, begun, local, chunk, half):
    rows_shard = out_ref.shape[1] // Y
    wide = PLACES * rows_shard
    peak = None
    for y in range(Y):
        total = begun[y] + grad_part(local, chunk, y, half, wide)
        size = jnp.abs(total)
        peak = size if peak is None else jnp.maximum(peak, size)
        out_ref[:PLACES, y * rows_shard : (y + 1) * rows_shard, :] = total.T.reshape(
            PLACES, rows_shard, -1
        )
    out_ref[PLACES] = jnp.broadcast_to(jnp.max(peak, keepdims=True), out_ref.shape[1:])


def forward_mine(mine, own, one, two, out_ref, weights_ref):
    for y, block in enumerate(natural(mine)):
        weights_ref[y] = block
    core = lax.axis_index("core")
    out_ref[0] = forward_part(own, weights_ref, core)
    out_ref[1] = forward_part(one, weights_ref, core)
    out_ref[2] = forward_part(two, weights_ref, core)


def near_grad(part_ref, theirs, payload, own, one, two, theirs_ref, mine_ref, weights_ref):
    for y, block in enumerate(natural(theirs)):
        weights_ref[y] = block
    y_here, core = lax.axis_index("y"), lax.axis_index("core")
    chunks = (own, one, two)
    steps = (0, 3 + 2 * core, 1 + 2 * core)
    locals_ = []
    for k, (step, chunk) in enumerate(zip(steps, chunks)):
        both = part_ref[k] + forward_part(chunk, weights_ref, 1 - core)
        locals_.append(local_part(both, payload, (y_here + step) % Y))
    wide = theirs_ref.shape[2]
    for out_ref, half in ((theirs_ref, 1 - core), (mine_ref, core)):
        for y in range(Y):
            total = None
            for local, chunk in zip(locals_, chunks):
                term = grad_part(local, chunk, y, half, wide)
                total = term if total is None else total + term
            out_ref[y] = total


def grad_theirs(begun, mine, theirs, payload, chunk, out_ref, local_ref):
    core = lax.axis_index("core")
    both = forward_part(chunk, mine, core) + forward_part(chunk, theirs, 1 - core)
    local = local_part(both, payload, (lax.axis_index("y") + 2) % Y)
    local_ref[...] = local
    finish_grad(out_ref, begun, local, chunk, 1 - core)


def grad_mine(begun, local_ref, chunk, out_ref):
    finish_grad(out_ref, begun, local_ref[...], chunk, lax.axis_index("core"))


def combine(mine, theirs, out):
    lanes = mine.shape[-1]
    pairs = out.shape[2] // lanes - 1
    bits = jnp.ceil(jnp.log2(jnp.maximum(mine[PLACES] + theirs[PLACES], 1e-30)))
    scale = jnp.exp2(14.0 - bits)
    for t in range(pairs):
        cut = slice(2 * t, 2 * t + 2)
        out[:, :, t * lanes : (t + 1) * lanes] = (
            mine[:PLACES, cut, :] + theirs[:PLACES, cut, :]
        ) * scale[cut]
    out[:, :, pairs * lanes :] = jnp.broadcast_to(bits[:2], (PLACES, 2, bits.shape[1]))


def join(source, out, which, blocks, sems):
    rows, lanes = source.shape[3:]
    half = out.shape[-1] // 2
    copies = []
    for y in range(Y):
        for x in range(X):
            at = slice(x * rows, (x + 1) * rows)
            for pair in range(Y // 2):
                a = source[2 * pair, x, y].astype(jnp.float32)
                b = source[2 * pair + 1, x, y].astype(jnp.float32)
                first = lower_half(a)
                blocks[y, at, pair * lanes : (pair + 1) * lanes] = jnp.where(
                    first, a, swapped(b)
                ).astype(jnp.bfloat16)
                blocks[y, at, half + pair * lanes : half + (pair + 1) * lanes] = jnp.where(
                    first, swapped(a), b
                ).astype(jnp.bfloat16)
        copy = pltpu.make_async_copy(blocks.at[y], out.at[y, which], sems.at[y])
        copy.start()
        copies.append(copy)
    for copy in copies:
        copy.wait()


def join_mine(source, out, blocks, sems):
    join(source, out, lax.axis_index("core"), blocks, sems)


def join_theirs(source, begun, out, blocks, sems):
    join(source, out, 1 - lax.axis_index("core"), blocks, sems)


def shards(
    tokens, hidden_grad, routing, row_count, old_slots, new_slots, master, first_moment, second_moment
):
    y = lax.axis_index("y")
    experts, rows_shard, width = master.shape
    hid = width // 2
    part = hid // Y
    lanes = 2 * part
    f32, bf16 = jnp.float32, jnp.bfloat16
    own = tokens[0, 0]
    rows = own.shape[0]
    half_rows = rows // 2
    hbm = pl.BlockSpec(memory_space=pltpu.MemorySpace.HBM)
    payload = pl.pallas_call(
        prepare,
        out_shape=jax.ShapeDtypeStruct((Y, experts * rows_shard + half_rows, lanes), bf16),
        in_specs=[SMEM, VMEM, VMEM, VMEM],
        out_specs=VMEM,
        name="prepare",
    )(row_count, routing[0, 0], hidden_grad[0, 0], master)
    payload = lax.all_to_all(payload, "y", 0, 0, tiled=True)
    near_one = lax.ppermute(own, ("y", "core"), APART)
    near_two = lax.ppermute(own, ("y", "core"), BACK)
    picked = pl.pallas_call(
        pick_old,
        out_shape=jax.ShapeDtypeStruct((PLACES, Y * rows_shard, lanes), bf16),
        in_specs=[SMEM, VMEM],
        out_specs=pl.BlockSpec(memory_space=pltpu.MemorySpace.HBM),
        scratch_shapes=[
            pltpu.VMEM((experts, Y * rows_shard, lanes), bf16),
            pltpu.VMEM((PLACES, Y * rows_shard, lanes), bf16),
            pltpu.SemaphoreType.DMA((4,)),
        ],
        compiler_params=grant(4),
        name="pick_old",
    )(old_slots, payload)
    landed = lax.all_to_all(picked, ("x", "z"), 0, 0, tiled=True)
    far = lax.ppermute(near_one, ("y", "core"), APART)

    w_mine = landed
    w_theirs = lax.ppermute(w_mine, "core", SWAP)

    wide = PLACES * rows_shard
    weights_shape = jax.ShapeDtypeStruct((Y, wide, lanes), bf16)
    forward, w_mine = pl.pallas_call(
        forward_mine,
        out_shape=(jax.ShapeDtypeStruct((3, rows, lanes), f32), weights_shape),
        in_specs=[VMEM] * 4,
        out_specs=(VMEM, VMEM),
        compiler_params=grant(24),
        name="forward_mine",
    )(w_mine, own, near_one, near_two)
    begun_shape = jax.ShapeDtypeStruct((Y, lanes, wide), f32)
    begun_theirs, begun_mine, w_theirs = pl.pallas_call(
        near_grad,
        out_shape=(begun_shape, begun_shape, weights_shape),
        in_specs=[VMEM] * 6,
        out_specs=(VMEM, VMEM, VMEM),
        compiler_params=grant(24),
        name="near_grad",
    )(forward, w_theirs, payload, own, near_one, near_two)
    grad_shape = jax.ShapeDtypeStruct((PLACES + 1, Y * rows_shard, lanes), f32)
    sent, local = pl.pallas_call(
        grad_theirs,
        out_shape=(grad_shape, jax.ShapeDtypeStruct((lanes, rows), bf16)),
        in_specs=[VMEM] * 5,
        out_specs=(VMEM, VMEM),
        compiler_params=grant(24),
        name="grad_theirs",
    )(begun_theirs, w_mine, w_theirs, payload, far)
    received = lax.ppermute(sent, "core", SWAP)
    summed = pl.pallas_call(
        grad_mine,
        out_shape=grad_shape,
        in_specs=[VMEM] * 3,
        out_specs=VMEM,
        compiler_params=grant(24),
        name="grad_mine",
    )(begun_mine, local, far)
    pairs = Y * rows_shard // 2
    scaled = pl.pallas_call(
        combine,
        out_shape=jax.ShapeDtypeStruct((PLACES, 2, (pairs + 1) * lanes), f32),
        in_specs=[VMEM] * 2,
        out_specs=VMEM,
        compiler_params=grant(6),
        name="combine",
    )(summed, received)

    columns = pl.pallas_call(
        split_cols,
        out_shape=jax.ShapeDtypeStruct((Y, 3, experts, rows_shard, lanes), f32),
        in_specs=[VMEM] * 3,
        out_specs=VMEM,
        compiler_params=grant(4),
        name="split_cols",
    )(master, first_moment, second_moment)

    def for_chip(step, x):
        return lax.dynamic_index_in_dim(x, (y + step) % Y, keepdims=False)

    m_low = lax.ppermute(for_chip(1, columns), "y", UP)
    m_high = lax.ppermute(for_chip(3, columns), "y", DOWN)
    m_far = lax.ppermute(for_chip(2, columns), "y", ACROSS)
    m_own = for_chip(0, columns)

    got = lax.all_to_all(scaled.astype(jnp.float16), ("x", "z"), 0, 0, tiled=True)
    got = got.astype(f32)
    select = (old_slots[:, None] == jnp.arange(experts, dtype=jnp.int32)[None, :]).astype(f32)
    per_slot = jnp.sum(row_count.astype(f32), axis=0)
    total = jnp.dot(per_slot, select, precision=lax.Precision.HIGHEST)
    picked, after = pl.pallas_call(
        adam,
        out_shape=(
            jax.ShapeDtypeStruct((PLACES, Y * rows_shard, lanes), bf16),
            jax.ShapeDtypeStruct((Y, 3, experts, rows_shard, lanes), f32),
        ),
        in_specs=[SMEM] * 3 + [VMEM] * 5,
        out_specs=(VMEM, VMEM),
        scratch_shapes=[
            pltpu.VMEM((Y, 3, experts, rows_shard, lanes), f32),
            pltpu.VMEM((experts, 2, pairs * lanes), f32),
            pltpu.VMEM((experts, Y * rows_shard, lanes), bf16),
        ],
        compiler_params=grant(6),
        name="adam",
    )(old_slots, new_slots, total, got, m_own, m_low, m_high, m_far)
    block_rows = PLACES * rows_shard
    landed = lax.all_to_all(
        picked.reshape(Z, X * Y * rows_shard, lanes), "z", 0, 0, tiled=True
    )

    s_low = lax.ppermute(for_chip(1, after), "y", UP)
    s_high = lax.ppermute(for_chip(3, after), "y", DOWN)
    s_far = lax.ppermute(for_chip(2, after), "y", ACROSS)
    whole = jax.ShapeDtypeStruct((experts, rows_shard, width), f32)
    new_master, new_first, new_second = pl.pallas_call(
        join_cols,
        out_shape=(whole,) * 3,
        in_specs=[VMEM] * 4,
        out_specs=(VMEM,) * 3,
        scratch_shapes=[pltpu.VMEM((Y, 3, experts, rows_shard, lanes), f32)],
        compiler_params=grant(6),
        name="join_cols",
    )(for_chip(0, after), s_low, s_high, s_far)

    landed = (
        landed.reshape(Z, X, Y, rows_shard, lanes)
        .transpose(1, 2, 0, 3, 4)
        .reshape(X, Y * Z * rows_shard, lanes)
    )
    copies = jnp.broadcast_to(landed[None], (Y, *landed.shape))
    mine = lax.all_to_all(
        copies.reshape(Y * X, Y * Z * rows_shard, lanes), ("y", "x"), 0, 0, tiled=True
    ).reshape(Y, X, Y, Z * rows_shard, lanes)
    theirs = lax.ppermute(mine, "core", SWAP)
    scratch = [pltpu.VMEM((Y, block_rows, width), bf16), pltpu.SemaphoreType.DMA((Y,))]
    whole = jax.ShapeDtypeStruct((Y, C, block_rows, width), bf16)
    begun = pl.pallas_call(
        join_mine,
        out_shape=whole,
        in_specs=[VMEM],
        out_specs=hbm,
        scratch_shapes=scratch,
        compiler_params=grant(8),
        name="join_mine",
    )(mine)
    new_weights = pl.pallas_call(
        join_theirs,
        out_shape=whole,
        in_specs=[VMEM, hbm],
        out_specs=hbm,
        scratch_shapes=scratch,
        input_output_aliases={1: 0},
        compiler_params=grant(8),
        name="join_theirs",
    )(theirs, begun)
    return (new_weights.reshape(1, -1, width), new_master, new_first, new_second)


def solution(mesh):
    fine = Mesh(mesh.devices.reshape(Y, C, X, Z), ("y", "core", "x", "z"))
    dp, place = ("y", "core"), ("x", "z")
    placed = (
        P(dp, place, None, None),
        P(dp, place, None, None),
        P(dp, place, None, None),
        P(),
        P(),
        P(),
        P(None, dp + place, None),
        P(None, dp + place, None),
        P(None, dp + place, None),
    )

    return jax.shard_map(
        shards,
        mesh=fine,
        in_specs=placed,
        out_specs=(
            P(place, None, None),
            P(None, dp + place, None),
            P(None, dp + place, None),
            P(None, dp + place, None),
        ),
        check_vma=False,
    )
```
